128 devices in a mesh: col: 4 (over y), row: 32 (over z, x, core).
Axes of the slice: x: 4, y: 4, z: 4, core: 2. Of those that a mesh axis runs over, the one named last changes fastest.
Arguments:
- locked: float32 [1024, 524288], P('col', 'row'), may hold values from -6 to 6
- vectors: float32 [64, 524288], P(None, 'row'), may hold values from -125 to 125
- mass: float32 [524288], P('row'), may hold values from 0.18 to 3.5
Outputs:
- appended: float32 [64, 524288], P(None, 'row')
- factor: float32 [64, 64], replicated
The draws below stay inside these ranges and needn't reach their ends.
All inputs are finite; a program needn't handle non-finite values.
Results may differ from the reference program's by a relative error of at most 0.0003.
Values sent between devices are 32-bit elements; how exact they have to be, the bound alone decides.
A program may use at most 128 MiB of HBM per device.

```python
import jax
import jax.numpy as jnp
from jax import lax

LOCKED = 1024
NEW = 64
NROWS = 524288


def locked_rows(key, count):
    base = jax.random.fold_in(key, 11)

    def one_row(index):
        sub = jax.random.fold_in(base, index)
        return jnp.clip(jax.random.normal(sub, (NROWS,), jnp.float32), -6.0, 6.0)
    return jax.vmap(one_row)(jnp.arange(count))


def draw_locked(key, part):
    return locked_rows(key, LOCKED)


def draw_vectors(key, part):
    shared = locked_rows(key, NEW)
    noise = jnp.clip(jax.random.normal(jax.random.fold_in(key, 12), (NEW, NROWS), jnp.float32), -6.0, 6.0)
    even = 0.6 * shared[0::2] + 0.8 * noise[0::2]
    odd = even + 0.007 * noise[1::2]
    base = jnp.stack([even, odd], axis=1).reshape(NEW, NROWS)
    colscale = 10.0 ** jax.random.uniform(jax.random.fold_in(key, 13), (NEW, 1), jnp.float32)
    return base * colscale


def draw_mass(key, part):
    position = jnp.arange(NROWS).astype(jnp.float32) / (NROWS - 1)
    rough = jnp.exp(jax.random.uniform(jax.random.fold_in(key, 15), (NROWS,), jnp.float32, -0.35, 0.35))
    rough = rough / 1.0204942
    trend = 0.5 + position
    return trend * rough


def setup_inputs(seed: int = 0) -> dict:
    key_of = jax.random.split(jax.random.key(seed), 4)
    locked = draw_locked(jax.random.fold_in(key_of[3], 71), 0)
    vectors = draw_vectors(jax.random.fold_in(key_of[3], 71), 0)
    mass = draw_mass(jax.random.fold_in(key_of[3], 71), 0)
    return dict(locked=locked, vectors=vectors, mass=mass)


def inner(left, right, mass):
    return jnp.dot(left * mass, right.T, precision=lax.Precision.HIGHEST) / NROWS

def factorize(gram):
    size = gram.shape[0]
    places = jnp.arange(size, dtype=jnp.int32)

    def step(index, state):
        work, lower = state
        column = lax.dynamic_slice_in_dim(work, index, 1, 1)[:, 0]
        pivot = jnp.sqrt(lax.dynamic_slice_in_dim(column, index, 1, 0)[0])
        column = jnp.where(places >= index, column / pivot, jnp.zeros_like(column))
        pick = (places == index).astype(work.dtype)
        lower = lower + column[:, None] * pick[None, :]
        work = work - column[:, None] * column[None, :]
        return (work, lower)
    work, lower = lax.fori_loop(0, size, step, (gram, jnp.zeros_like(gram)))
    return lower

def invert_lower(lower):
    size = lower.shape[0]
    places = jnp.arange(size, dtype=jnp.int32)

    def step(index, inverse):
        line = lax.dynamic_slice_in_dim(lower, index, 1, 0)[0]
        pick = (places == index).astype(lower.dtype)
        pivot = jnp.sum(line * pick)
        solved = (pick - jnp.dot(line, inverse, precision=lax.Precision.HIGHEST)) / pivot
        return inverse + pick[:, None] * solved[None, :]
    return lax.fori_loop(0, size, step, jnp.zeros_like(lower))

def project(block, locked, mass):
    coef = inner(locked, block, mass)
    return block - jnp.dot(coef.T, locked, precision=lax.Precision.HIGHEST)

def orthonormal(block, mass):
    gram = inner(block, block, mass)
    lower = factorize(gram)
    inverse = invert_lower(lower)
    return (jnp.dot(inverse, block, precision=lax.Precision.HIGHEST), lower.T)

def reference(locked, vectors, mass):
    once = project(vectors, locked, mass)
    projected = project(once, locked, mass)
    middle, upper_one = orthonormal(projected, mass)
    appended, upper_two = orthonormal(middle, mass)
    factor = jnp.dot(upper_two, upper_one, precision=lax.Precision.HIGHEST)
    return (appended, factor)
```

```python
import functools

import jax
import jax.numpy as jnp
from jax import lax
from jax.experimental import pallas as pl
from jax.experimental.pallas import tpu as pltpu
from jax.sharding import PartitionSpec as P

MESH = pl.DeviceIdType.MESH
F32 = jnp.float32
BF16 = jnp.bfloat16
HIGHEST = lax.Precision.HIGHEST
WIDTH = 512
GROUP = 8
SLOTS = 4


def split3(x):
    high = x.astype(BF16)
    rest = x - high.astype(F32)
    middle = rest.astype(BF16)
    low = (rest - middle.astype(F32)).astype(BF16)
    return high, middle, low


def dot_nt(a, b):
    return lax.dot_general(a, b, (((1,), (1,)), ((), ())), preferred_element_type=F32)


def dot_nn(a, b):
    return lax.dot_general(a, b, (((1,), (0,)), ((), ())), preferred_element_type=F32)


def exchange_sum(src, scratch, out, row, col, col_size, z_size, over_col):
    (part, part_s, part_r, red, zbuf, z_s, z_r, ybuf, y_s, y_r, full_s, full_r) = scratch
    place = lax.rem(row, GROUP)
    base = row - place
    z = lax.div(row, GROUP)
    rows = src.shape[0] // GROUP

    copies = []
    for d in range(1, GROUP):
        peer = lax.rem(place + d, GROUP)
        copy = pltpu.make_async_remote_copy(
            src_ref=src.at[pl.ds(pl.multiple_of(peer * rows, rows), rows), :],
            dst_ref=part.at[d - 1],
            send_sem=part_s.at[d - 1],
            recv_sem=part_r.at[d - 1],
            device_id={"row": base + peer},
            device_id_type=MESH,
        )
        copy.start()
        copies.append(copy)
    total = src[pl.ds(pl.multiple_of(place * rows, rows), rows), :]
    for d in range(1, GROUP):
        copies[d - 1].wait_recv()
        total = total + part[d - 1]
    stages = [(zbuf, z_s, z_r, z, z_size, "row")]
    if over_col:
        stages.append((ybuf, y_s, y_r, col, col_size, "col"))
    for stage, (buf, sems, semr, mine, size, axis) in enumerate(stages):
        red[stage] = total
        later = []
        for d in range(1, size):
            peer = lax.rem(mine + d, size)
            target = peer * GROUP + place if axis == "row" else peer
            copy = pltpu.make_async_remote_copy(
                src_ref=red.at[stage],
                dst_ref=buf.at[mine],
                send_sem=sems.at[d - 1],
                recv_sem=semr.at[mine],
                device_id={axis: target},
                device_id_type=MESH,
            )
            copy.start()
            later.append(copy)
        buf[mine] = total
        for d in range(1, size):
            peer = lax.rem(mine + d, size)
            pltpu.make_async_remote_copy(
                src_ref=red.at[stage],
                dst_ref=buf.at[peer],
                send_sem=sems.at[d - 1],
                recv_sem=semr.at[peer],
                device_id={axis: mine * GROUP + place if axis == "row" else mine},
                device_id_type=MESH,
            ).wait_recv()
        total = buf[0]
        for i in range(1, size):
            total = total + buf[i]
        copies += later
    mine_rows = pl.ds(pl.multiple_of(place * rows, rows), rows)
    out[mine_rows, :] = total
    for d in range(1, GROUP):
        peer = lax.rem(place + d, GROUP)
        copy = pltpu.make_async_remote_copy(
            src_ref=out.at[mine_rows, :],
            dst_ref=out.at[mine_rows, :],
            send_sem=full_s.at[d - 1],
            recv_sem=full_r.at[place],
            device_id={"row": base + peer},
            device_id_type=MESH,
        )
        copy.start()
        copies.append(copy)
    for d in range(1, GROUP):
        peer = lax.rem(place + d, GROUP)
        rows_of = pl.ds(pl.multiple_of(peer * rows, rows), rows)
        pltpu.make_async_remote_copy(
            src_ref=out.at[rows_of, :],
            dst_ref=out.at[rows_of, :],
            send_sem=full_s.at[d - 1],
            recv_sem=full_r.at[peer],
            device_id={"row": row},
            device_id_type=MESH,
        ).wait_recv()
    for copy in copies:
        copy.wait_send()


def factorize(gram, work):
    size = gram.shape[0]
    lane = lax.broadcasted_iota(jnp.int32, (size, 2 * size), 1)
    sub = lax.broadcasted_iota(jnp.int32, (size, 2 * size), 0)
    work[...] = jnp.where(lane < size, gram, jnp.where(lane - size == sub, 1.0, 0.0))

    def step(j, carry):
        line = work[pl.ds(j, 1), :]
        body = work[...]
        lane1 = lax.broadcasted_iota(jnp.int32, (1, 2 * size), 1)
        pivot = jnp.sum(jnp.where(lane1 == j, line, 0.0), axis=1, keepdims=True)
        column = jnp.sum(jnp.where(lane == j, body, 0.0), axis=1, keepdims=True)
        root = jnp.sqrt(pivot)
        line = line / root
        times = jnp.where(sub > j, column / root, 0.0)
        work[...] = jnp.where(sub == j, line, body - times * line)
        return carry

    lax.fori_loop(0, size, step, 0)
    body = work[...]
    upper = jnp.where(lane >= sub, body, 0.0)[:, :size]
    return upper, body[:, size:]


def fused(
    n_col, n_row, scale,
    l_hbm, v_hbm, m_ref, p_hbm, t_ref, f_ref,
    lbuf, lsem, vc, vsem, l1, l2, l3, acc, bt, b2, wsp, src2, ggram,
    zf, po, stage, d2a, fla, fra, d2b, flb, frb,
    rs_sa, rs_ra, rs_sb, rs_rb, ag_sa, ag_ra, ag_sb, ag_rb, psem,
    gsrc, gout, work, *ar,
):
    per = len(ar) // 4
    ars = [ar[i * per : (i + 1) * per] for i in range(4)]
    col, row = lax.axis_index("col"), lax.axis_index("row")
    right, left = lax.rem(col + 1, n_col), lax.rem(col + n_col - 1, n_col)
    across = lax.rem(col + 2, n_col)
    z_size = n_row // GROUP
    place = lax.rem(row, GROUP)
    base = row - place
    z = lax.div(row, GROUP)
    chunks = vc.shape[0]
    per_slice = chunks // n_col
    half = per_slice // 2
    new = vc.shape[1]

    def load_l(ch, slot):
        return pltpu.make_async_copy(
            l_hbm.at[:, pl.ds(pl.multiple_of(ch * WIDTH, WIDTH), WIDTH)], lbuf.at[slot], lsem.at[slot]
        )

    def load_v(ch):
        return pltpu.make_async_copy(
            v_hbm.at[:, pl.ds(pl.multiple_of(ch * WIDTH, WIDTH), WIDTH)], vc.at[ch], vsem.at[ch]
        )

    for ch in range(SLOTS):
        load_v(ch).start()
        load_l(ch, ch).start()

    barrier = pltpu.get_barrier_semaphore()
    for d in range(1, GROUP):
        pl.semaphore_signal(barrier, inc=1, device_id={"row": base + lax.rem(place + d, GROUP)}, device_id_type=MESH)
    for d in range(1, z_size):
        pl.semaphore_signal(
            barrier, inc=1, device_id={"row": lax.rem(z + d, z_size) * GROUP + place}, device_id_type=MESH
        )
    for d in range(1, n_col):
        pl.semaphore_signal(barrier, inc=1, device_id={"col": lax.rem(col + d, n_col)}, device_id_type=MESH)

    def add_products(x, ch):
        a1, a2, a3 = split3(x)
        a = jnp.concatenate([a1, a2, a3], axis=0)
        acc[...] += dot_nt(a, l1[ch])
        acc[0 : 2 * new] += dot_nt(a[0 : 2 * new], l2[ch])
        acc[0:new] += dot_nt(a1, l3[ch])

    def collect():
        return (acc[0:new] + (acc[new : 2 * new] + acc[2 * new :])) * scale

    acc[...] = jnp.zeros_like(acc)

    def first_step(ch, carry):
        slot = lax.rem(ch, SLOTS)
        load_l(ch, slot).wait()
        load_v(ch).wait()
        high, middle, low = split3(lbuf[slot])
        l1[ch] = high
        l2[ch] = middle
        l3[ch] = low

        @pl.when(ch + SLOTS < chunks)
        def _():
            load_l(ch + SLOTS, slot).start()
            load_v(ch + SLOTS).start()

        add_products(vc[ch] * m_ref[pl.ds(ch, 1), :], ch)
        return carry

    lax.fori_loop(0, chunks, first_step, 0)
    src2[...] = collect()
    pl.semaphore_wait(barrier, (GROUP - 1) + (z_size - 1) + (n_col - 1))
    exchange_sum(src2, ars[0], bt, row, col, n_col, z_size, False)

    def set_weights(b):
        w1, w2, w3 = split3(b)
        wsp[0:new] = w1
        wsp[new : 2 * new] = w2
        wsp[2 * new :] = w3

    def term(ch):
        r = dot_nn(wsp[...], l1[ch])
        s = dot_nn(wsp[0 : 2 * new], l2[ch])
        t = dot_nn(wsp[0:new], l3[ch])
        return r[0:new] + ((r[new : 2 * new] + s[0:new]) + (r[2 * new :] + (s[new:] + t)))

    def send(src, dst, sems, semr, index, where):
        return pltpu.make_async_remote_copy(
            src_ref=src, dst_ref=dst, send_sem=sems.at[index], recv_sem=semr.at[index],
            device_id={"col": where}, device_id_type=MESH,
        )

    def far(k, where, d2, ss, sr):
        return send(stage.at[k], d2.at[k], ss, sr, k, where)

    def to_right(k, fl, ss, sr):
        return send(stage.at[per_slice + k], fl.at[k], ss, sr, per_slice + k, right)

    def to_left(k, fr, ss, sr):
        return send(stage.at[2 * per_slice + k], fr.at[k], ss, sr, 2 * per_slice + k, left)

    def reduce_scatter(d2, fl, fr, ss, sr, finish):
        def far_step(j, carry):
            stage[j] = term(across * per_slice + j)
            far(j, right, d2, ss, sr).start()
            stage[half + j] = term(across * per_slice + half + j)
            far(half + j, left, d2, ss, sr).start()
            return carry

        lax.fori_loop(0, half, far_step, 0)

        def pure_step(j, carry):
            stage[per_slice + half + j] = term(right * per_slice + half + j)
            to_right(half + j, fl, ss, sr).start()
            stage[2 * per_slice + j] = term(left * per_slice + j)
            to_left(j, fr, ss, sr).start()
            return carry

        lax.fori_loop(0, half, pure_step, 0)

        def added_step(j, carry):
            own = term(right * per_slice + j)
            far(j, right, d2, ss, sr).wait_recv()
            stage[per_slice + j] = own + d2[j]
            to_right(j, fl, ss, sr).start()
            own = term(left * per_slice + half + j)
            far(half + j, left, d2, ss, sr).wait_recv()
            stage[2 * per_slice + half + j] = own + d2[half + j]
            to_left(half + j, fr, ss, sr).start()
            return carry

        lax.fori_loop(0, half, added_step, 0)

        def own_step(j, carry):
            for k in (j, half + j):
                own = term(col * per_slice + k)
                to_left(k, fr, ss, sr).wait_recv()
                to_right(k, fl, ss, sr).wait_recv()
                finish(k, own + (fl[k] + fr[k]))
            return carry

        lax.fori_loop(0, half, own_step, 0)

        def sent_step(k, carry):
            far(k, right, d2, ss, sr).wait_send()
            to_right(k, fl, ss, sr).wait_send()
            to_left(k, fr, ss, sr).wait_send()
            return carry

        lax.fori_loop(0, per_slice, sent_step, 0)

    def give_right(src, dst, k, sl, ss, sr):
        return send(src, dst.at[sl * per_slice + k], ss, sr, k, right)

    def give_left(src, dst, k, sl, ss, sr):
        return send(src, dst.at[sl * per_slice + k], ss, sr, per_slice + k, left)

    def hand_on(dst, k, sl, where, ss, sr):
        at = dst.at[sl * per_slice + k]
        return send(at, at, ss, sr, 2 * per_slice + k, where)

    def give(src, dst, k, ss, sr):
        give_right(src, dst, k, col, ss, sr).start()
        give_left(src, dst, k, col, ss, sr).start()

    def relay(dst, ss, sr, use):
        def relay_step(j, carry):
            at = dst.at[left * per_slice + j]
            give_right(at, dst, j, left, ss, sr).wait_recv()
            hand_on(dst, j, left, right, ss, sr).start()
            use(left * per_slice + j)
            at = dst.at[right * per_slice + half + j]
            give_left(at, dst, half + j, right, ss, sr).wait_recv()
            hand_on(dst, half + j, right, left, ss, sr).start()
            use(right * per_slice + half + j)
            return carry

        lax.fori_loop(0, half, relay_step, 0)

    def gather_rest(dst, ss, sr, use):
        def near_step(j, carry):
            at = dst.at[left * per_slice + half + j]
            give_right(at, dst, half + j, left, ss, sr).wait_recv()
            use(left * per_slice + half + j)
            at = dst.at[right * per_slice + j]
            give_left(at, dst, j, right, ss, sr).wait_recv()
            use(right * per_slice + j)
            return carry

        lax.fori_loop(0, half, near_step, 0)

        def far_step(j, carry):
            for k in (j, half + j):
                hand_on(dst, k, across, right, ss, sr).wait_recv()
                use(across * per_slice + k)
            return carry

        lax.fori_loop(0, half, far_step, 0)

        def sent_step(k, carry):
            at = dst.at[col * per_slice + k]
            give_right(at, dst, k, col, ss, sr).wait_send()
            give_left(at, dst, k, col, ss, sr).wait_send()
            hand_on(dst, k, col, right, ss, sr).wait_send()
            return carry

        lax.fori_loop(0, per_slice, sent_step, 0)

    set_weights(bt[...])
    acc[...] = jnp.zeros_like(acc)

    def use_once(ch):
        add_products((vc[ch] - zf[ch]) * m_ref[pl.ds(ch, 1), :], ch)

    def finish_first(k, value):
        ch = col * per_slice + k
        zf[ch] = value
        give(zf.at[ch], zf, k, ag_sa, ag_ra)
        use_once(ch)

    reduce_scatter(d2a, fla, fra, rs_sa, rs_ra, finish_first)
    relay(zf, ag_sa, ag_ra, use_once)
    gather_rest(zf, ag_sa, ag_ra, use_once)
    src2[...] = collect()
    exchange_sum(src2, ars[1], b2, row, col, n_col, z_size, False)

    set_weights(bt[...] + b2[...])
    ggram[...] = jnp.zeros_like(ggram)

    def add_gram(p, ch):
        a = jnp.concatenate(split3(p * m_ref[pl.ds(ch, 1), :]), axis=0)
        b = jnp.concatenate(split3(p), axis=0)
        ggram[...] += dot_nt(a, b)

    def collect_gram():
        g = ggram[...]
        rows3 = g[0:new] + (g[new : 2 * new] + g[2 * new :])
        gram = rows3[:, 0:new] + (rows3[:, new : 2 * new] + rows3[:, 2 * new :])
        return jnp.concatenate([gram * scale, jnp.zeros_like(gram)], axis=1)

    def keep(k):
        return pltpu.make_async_copy(po.at[k], p_hbm.at[col * per_slice + k], psem.at[k])

    def finish_second(k, value):
        ch = col * per_slice + k
        p = vc[ch] - value
        po[k] = p
        give(po.at[k], p_hbm, k, ag_sb, ag_rb)
        keep(k).start()
        add_gram(p, ch)

    reduce_scatter(d2b, flb, frb, rs_sb, rs_rb, finish_second)
    gsrc[0] = collect_gram()
    exchange_sum(gsrc.at[0], ars[2], gout.at[0], row, col, n_col, z_size, True)
    relay(p_hbm, ag_sb, ag_rb, lambda ch: None)
    upper_one, inverse_one = factorize(gout[0], work)

    ggram[...] = jnp.zeros_like(ggram)

    def second_gram(k, carry):
        middle = jnp.dot(inverse_one, po[k], precision=HIGHEST, preferred_element_type=F32)
        add_gram(middle, col * per_slice + k)
        return carry

    lax.fori_loop(0, per_slice, second_gram, 0)
    gsrc[1] = collect_gram()
    exchange_sum(gsrc.at[1], ars[3], gout.at[1], row, col, n_col, z_size, True)
    upper_two, inverse_two = factorize(gout[1], work)
    f_ref[...] = jnp.dot(upper_two, upper_one, precision=HIGHEST, preferred_element_type=F32)
    t_ref[...] = jnp.dot(inverse_two, inverse_one, precision=HIGHEST, preferred_element_type=F32)

    def kept_step(k, carry):
        keep(k).wait()
        return carry

    lax.fori_loop(0, per_slice, kept_step, 0)
    gather_rest(p_hbm, ag_sb, ag_rb, lambda ch: None)


def apply_kernel(t_ref, p_ref, o_ref):
    for i in range(p_ref.shape[0]):
        o_ref[:, i * WIDTH : (i + 1) * WIDTH] = jnp.dot(
            t_ref[...], p_ref[i], precision=HIGHEST, preferred_element_type=F32
        )


def local(n_col, n_row, locked, vectors, mass):
    mine, cols = locked.shape
    new = vectors.shape[0]
    chunks = cols // WIDTH
    per_slice = chunks // n_col
    z_size = n_row // GROUP
    rows = new // GROUP
    dma = pltpu.SemaphoreType.DMA

    def exchange_scratch(width):
        return [
            pltpu.VMEM((GROUP - 1, rows, width), F32), dma((GROUP - 1,)), dma((GROUP - 1,)),
            pltpu.VMEM((2, rows, width), F32),
            pltpu.VMEM((z_size, rows, width), F32), dma((z_size,)), dma((z_size,)),
            pltpu.VMEM((n_col, rows, width), F32), dma((n_col,)), dma((n_col,)),
            dma((GROUP,)), dma((GROUP,)),
        ]

    chunk = lambda n: pltpu.VMEM((n, new, WIDTH), F32)
    scratch = [
        pltpu.VMEM((SLOTS, mine, WIDTH), F32), dma((SLOTS,)), chunk(chunks), dma((chunks,)),
        pltpu.VMEM((chunks, mine, WIDTH), BF16), pltpu.VMEM((chunks, mine, WIDTH), BF16),
        pltpu.VMEM((chunks, mine, WIDTH), BF16),
        pltpu.VMEM((3 * new, mine), F32), pltpu.VMEM((new, mine), F32), pltpu.VMEM((new, mine), F32),
        pltpu.VMEM((3 * new, mine), BF16), pltpu.VMEM((new, mine), F32), pltpu.VMEM((3 * new, 3 * new), F32),
        chunk(chunks), chunk(per_slice), chunk(3 * per_slice),
        chunk(per_slice), chunk(per_slice), chunk(per_slice),
        chunk(per_slice), chunk(per_slice), chunk(per_slice),
    ]
    scratch += [dma((3 * per_slice,))] * 8 + [dma((per_slice,))]
    scratch += [pltpu.VMEM((2, new, 2 * new), F32), pltpu.VMEM((2, new, 2 * new), F32), pltpu.VMEM((new, 2 * new), F32)]
    scratch += exchange_scratch(mine) * 2 + exchange_scratch(2 * new) * 2
    vmem = pl.BlockSpec(memory_space=pltpu.VMEM)
    hbm = pl.BlockSpec(memory_space=pl.ANY)
    projected, transform, factor = pl.pallas_call(
        functools.partial(fused, n_col, n_row, 1.0 / (cols * n_row)),
        out_shape=(
            jax.ShapeDtypeStruct((chunks, new, WIDTH), F32),
            jax.ShapeDtypeStruct((new, new), F32),
            jax.ShapeDtypeStruct((new, new), F32),
        ),
        in_specs=[hbm, hbm, vmem],
        out_specs=(hbm, vmem, vmem),
        scratch_shapes=scratch,
        compiler_params=pltpu.CompilerParams(
            collective_id=0, has_side_effects=True, vmem_limit_bytes=60 << 20
        ),
        name="project_and_factor",
    )(locked, vectors, mass.reshape(chunks, WIDTH))
    block = 4
    appended = pl.pallas_call(
        apply_kernel,
        grid=(chunks // block,),
        out_shape=jax.ShapeDtypeStruct((new, cols), F32),
        in_specs=[
            pl.BlockSpec((new, new), lambda i: (0, 0)),
            pl.BlockSpec((block, new, WIDTH), lambda i: (i, 0, 0)),
        ],
        out_specs=pl.BlockSpec((new, block * WIDTH), lambda i: (0, i)),
        name="apply_factors",
    )(transform, projected)
    return (appended, factor)


def solution(mesh):
    return jax.shard_map(
        functools.partial(local, mesh.shape["col"], mesh.shape["row"]),
        mesh=mesh,
        in_specs=(P("col", "row"), P(None, "row"), P("row")),
        out_specs=(P(None, "row"), P()),
        check_vma=False,
    )
```

```python
import functools

import jax
import jax.numpy as jnp
from jax import lax
from jax.experimental import pallas as pl
from jax.experimental.pallas import tpu as pltpu
from jax.sharding import PartitionSpec as P

MESH = pl.DeviceIdType.MESH
F32 = jnp.float32
BF16 = jnp.bfloat16
HIGHEST = lax.Precision.HIGHEST
WIDTH = 512
GROUP = 8
PAIR = 2 * WIDTH
SLOTS = 3


def split3(x):
    high = x.astype(BF16)
    rest = x - high.astype(F32)
    middle = rest.astype(BF16)
    low = (rest - middle.astype(F32)).astype(BF16)
    return high, middle, low


def dot_nt(a, b):
    return lax.dot_general(a, b, (((1,), (1,)), ((), ())), preferred_element_type=F32)


def dot_nn(a, b):
    return lax.dot_general(a, b, (((1,), (0,)), ((), ())), preferred_element_type=F32)


def exchange_sum(src, scratch, out, row, z_size):
    (part, part_s, part_r, red, zbuf, z_s, z_r, full_s, full_r) = scratch
    place = lax.rem(row, GROUP)
    base = row - place
    z = lax.div(row, GROUP)
    rows = src.shape[0] // GROUP
    mine_rows = pl.ds(pl.multiple_of(place * rows, rows), rows)

    copies = []
    for d in range(1, GROUP):
        peer = lax.rem(place + d, GROUP)
        copy = pltpu.make_async_remote_copy(
            src_ref=src.at[pl.ds(pl.multiple_of(peer * rows, rows), rows), :],
            dst_ref=part.at[d - 1],
            send_sem=part_s.at[d - 1],
            recv_sem=part_r.at[d - 1],
            device_id={"row": base + peer},
            device_id_type=MESH,
        )
        copy.start()
        copies.append(copy)
    total = src[mine_rows, :]
    for d in range(1, GROUP):
        copies[d - 1].wait_recv()
        total = total + part[d - 1]
    red[...] = total
    peers = [lax.rem(z + d, z_size) * GROUP + place for d in range(1, z_size)]
    total = peer_sum(red, zbuf, z_s, z_r, z, [(lax.rem(z + d, z_size), {"row": p}) for d, p in enumerate(peers, 1)])
    out[mine_rows, :] = total
    for d in range(1, GROUP):
        peer = lax.rem(place + d, GROUP)
        copy = pltpu.make_async_remote_copy(
            src_ref=out.at[mine_rows, :],
            dst_ref=out.at[mine_rows, :],
            send_sem=full_s.at[d - 1],
            recv_sem=full_r.at[place],
            device_id={"row": base + peer},
            device_id_type=MESH,
        )
        copy.start()
        copies.append(copy)
    for d in range(1, GROUP):
        peer = lax.rem(place + d, GROUP)
        rows_of = pl.ds(pl.multiple_of(peer * rows, rows), rows)
        pltpu.make_async_remote_copy(
            src_ref=out.at[rows_of, :],
            dst_ref=out.at[rows_of, :],
            send_sem=full_s.at[d - 1],
            recv_sem=full_r.at[peer],
            device_id={"row": row},
            device_id_type=MESH,
        ).wait_recv()
    for copy in copies:
        copy.wait_send()


def peer_copies(src, buf, sems, semr, mine, peers):
    return [
        (
            pltpu.make_async_remote_copy(
                src_ref=src, dst_ref=buf.at[mine], send_sem=sems.at[i], recv_sem=semr.at[mine],
                device_id=device, device_id_type=MESH,
            ),
            pltpu.make_async_remote_copy(
                src_ref=src, dst_ref=buf.at[peer], send_sem=sems.at[i], recv_sem=semr.at[peer],
                device_id=device, device_id_type=MESH,
            ),
        )
        for i, (peer, device) in enumerate(peers)
    ]


def peer_sum(src, buf, sems, semr, mine, peers, between=None):
    copies = peer_copies(src, buf, sems, semr, mine, peers)
    for out, _ in copies:
        out.start()
    buf[mine] = src[...]
    if between is not None:
        between()
    for _, arrival in copies:
        arrival.wait_recv()
    total = buf[0]
    for i in range(1, len(peers) + 1):
        total = total + buf[i]
    for out, _ in copies:
        out.wait_send()
    return total


def gram_sum(gram, scratch, row, col, n_col, z_size, between):
    half = gram.shape[0] // 2
    place = lax.rem(row, GROUP)
    base = row - place
    z = lax.div(row, GROUP)
    x, core = lax.div(place, 2), lax.rem(place, 2)
    x_size = GROUP // 2
    stages = [
        (n_col, col, lambda p: {"col": p}),
        (2, core, lambda p: {"row": base + 2 * x + p}),
        (x_size, x, lambda p: {"row": base + 2 * p + core}),
        (z_size, z, lambda p: {"row": p * GROUP + place}),
    ]
    total = jnp.concatenate([gram[:half], gram[half:]], axis=1)
    for i, (size, mine, device) in enumerate(stages):
        src, buf, sems, semr = scratch[4 * i : 4 * i + 4]
        src[...] = total
        peers = [lax.rem(mine + d, size) for d in range(1, size)]
        total = peer_sum(src, buf, sems, semr, mine, [(p, device(p)) for p in peers], between if i == 0 else None)
    new = gram.shape[0]
    return jnp.concatenate([total[:, :new], total[:, new:]], axis=0)


def factorize(gram):
    size = gram.shape[0]
    lane = lax.broadcasted_iota(jnp.int32, (size, 2 * size), 1)
    sub = lax.broadcasted_iota(jnp.int32, (size, 2 * size), 0)
    sub8 = lax.broadcasted_iota(jnp.int32, (8, 2 * size), 0)
    wide = jnp.concatenate([gram, jnp.zeros_like(gram)], axis=1)
    wide = jnp.where(lane < size, wide, jnp.where(lane - size == sub, 1.0, 0.0))
    blocks = [wide[8 * i : 8 * i + 8] for i in range(size // 8)]
    for j in range(size):
        b, r = divmod(j, 8)
        line = blocks[b][r : r + 1, :]
        line = jnp.broadcast_to(line * (1.0 / line[:, j : j + 1]), (8, 2 * size))
        for i in range(b, size // 8):
            if i == b and r == 7:
                continue
            column = blocks[i][:, j : j + 1]
            if i == b:
                column = jnp.where(sub8 > r, column, 0.0)
            blocks[i] = blocks[i] - column * line
    body = jnp.concatenate(blocks, axis=0)
    pivots = jnp.sum(jnp.where(lane == sub, body, 0.0), axis=1, keepdims=True)
    body = body / jnp.sqrt(pivots)
    upper = jnp.where(lane >= sub, body, 0.0)[:, :size]
    return upper, body[:, size:]


def terms_of(matrix):
    a, b, c = split3(matrix)
    zero = jnp.zeros_like(a)
    return jnp.concatenate(
        [
            jnp.concatenate([a, a, a], axis=1),
            jnp.concatenate([b, b, zero], axis=1),
            jnp.concatenate([c, zero, zero], axis=1),
        ],
        axis=0,
    )


def apply_terms(terms, x):
    new = x.shape[0]
    r = dot_nn(terms, jnp.concatenate(split3(x), axis=0))
    return r[:new] + (r[new : 2 * new] + r[2 * new :])


def fused(
    n_col, n_row, scale,
    l_hbm, v_hbm, m_ref, p_hbm, t_ref, f_ref,
    lbuf, lsem, vc, vsem, l1, l2, l3, acc, bt, b2, wsp, src2, ggram,
    zf, po, stage, d2a, fla, fra, d2b, flb, frb,
    rs_sa, rs_ra, rs_sb, rs_rb, ag_sa, ag_ra, ag_sb, ag_rb, psem,
    *rest,
):
    ars = [rest[0:9], rest[9:18], rest[18:34], rest[34:50]]
    col, row = lax.axis_index("col"), lax.axis_index("row")
    right, left = lax.rem(col + 1, n_col), lax.rem(col + n_col - 1, n_col)
    across = lax.rem(col + 2, n_col)
    z_size = n_row // GROUP
    place = lax.rem(row, GROUP)
    base = row - place
    z = lax.div(row, GROUP)
    chunks = vc.shape[0]
    per_slice = chunks // n_col
    half = per_slice // 2
    new = vc.shape[1]

    def load_l(ch, slot):
        return pltpu.make_async_copy(
            l_hbm.at[:, pl.ds(pl.multiple_of(ch * PAIR, PAIR), PAIR)], lbuf.at[slot], lsem.at[slot]
        )

    def load_v(ch):
        return pltpu.make_async_copy(
            v_hbm.at[:, pl.ds(pl.multiple_of(ch * WIDTH, WIDTH), WIDTH)], vc.at[ch], vsem.at[ch]
        )

    for ch in range(SLOTS):
        load_v(2 * ch).start()
        load_v(2 * ch + 1).start()
        load_l(ch, ch).start()

    barrier = pltpu.get_barrier_semaphore()
    for d in range(1, GROUP):
        pl.semaphore_signal(barrier, inc=1, device_id={"row": base + lax.rem(place + d, GROUP)}, device_id_type=MESH)
    for d in range(1, z_size):
        pl.semaphore_signal(
            barrier, inc=1, device_id={"row": lax.rem(z + d, z_size) * GROUP + place}, device_id_type=MESH
        )
    for d in range(1, n_col):
        pl.semaphore_signal(barrier, inc=1, device_id={"col": lax.rem(col + d, n_col)}, device_id_type=MESH)

    def add_products(x, ch):
        a1, a2, a3 = split3(x)
        a = jnp.concatenate([a1, a2, a3], axis=0)
        acc[...] += dot_nt(a, l1[ch])
        acc[0 : 2 * new] += dot_nt(a[0 : 2 * new], l2[ch])
        acc[0:new] += dot_nt(a1, l3[ch])

    def collect():
        return (acc[0:new] + (acc[new : 2 * new] + acc[2 * new :])) * scale

    acc[...] = jnp.zeros_like(acc)

    def first_step(pair, carry):
        slot = lax.rem(pair, SLOTS)
        load_l(pair, slot).wait()
        for i in range(2):
            ch = 2 * pair + i
            load_v(ch).wait()
            high, middle, low = split3(lbuf[slot, :, i * WIDTH : (i + 1) * WIDTH])
            l1[ch] = high
            l2[ch] = middle
            l3[ch] = low
            add_products(vc[ch] * m_ref[:, pl.ds(pl.multiple_of(ch * WIDTH, WIDTH), WIDTH)], ch)

        @pl.when(pair + SLOTS < chunks // 2)
        def _():
            load_l(pair + SLOTS, slot).start()
            load_v(2 * (pair + SLOTS)).start()
            load_v(2 * (pair + SLOTS) + 1).start()

        return carry

    lax.fori_loop(0, chunks // 2, first_step, 0)
    src2[...] = collect()
    pl.semaphore_wait(barrier, (GROUP - 1) + (z_size - 1) + (n_col - 1))
    exchange_sum(src2, ars[0], bt, row, z_size)

    def set_weights(b):
        w1, w2, w3 = split3(b)
        wsp[0:new] = w1
        wsp[new : 2 * new] = w2
        wsp[2 * new :] = w3

    def term(ch):
        r = dot_nn(wsp[...], l1[ch])
        s = dot_nn(wsp[0 : 2 * new], l2[ch])
        t = dot_nn(wsp[0:new], l3[ch])
        return r[0:new] + ((r[new : 2 * new] + s[0:new]) + (r[2 * new :] + (s[new:] + t)))

    def send(src, dst, sems, semr, index, where):
        return pltpu.make_async_remote_copy(
            src_ref=src, dst_ref=dst, send_sem=sems.at[index], recv_sem=semr.at[index],
            device_id={"col": where}, device_id_type=MESH,
        )

    def far(k, where, d2, ss, sr):
        return send(stage.at[k], d2.at[k], ss, sr, k, where)

    def to_right(k, fl, ss, sr):
        return send(stage.at[per_slice + k], fl.at[k], ss, sr, per_slice + k, right)

    def to_left(k, fr, ss, sr):
        return send(stage.at[2 * per_slice + k], fr.at[k], ss, sr, 2 * per_slice + k, left)

    def reduce_scatter(d2, fl, fr, ss, sr, finish):
        def far_step(j, carry):
            stage[j] = term(across * per_slice + j)
            far(j, right, d2, ss, sr).start()
            stage[half + j] = term(across * per_slice + half + j)
            far(half + j, left, d2, ss, sr).start()
            return carry

        lax.fori_loop(0, half, far_step, 0)

        def pure_step(j, carry):
            stage[per_slice + half + j] = term(right * per_slice + half + j)
            to_right(half + j, fl, ss, sr).start()
            stage[2 * per_slice + j] = term(left * per_slice + j)
            to_left(j, fr, ss, sr).start()
            return carry

        lax.fori_loop(0, half, pure_step, 0)

        def added_step(j, carry):
            own = term(right * per_slice + j)
            far(j, right, d2, ss, sr).wait_recv()
            stage[per_slice + j] = own + d2[j]
            to_right(j, fl, ss, sr).start()
            own = term(left * per_slice + half + j)
            far(half + j, left, d2, ss, sr).wait_recv()
            stage[2 * per_slice + half + j] = own + d2[half + j]
            to_left(half + j, fr, ss, sr).start()
            return carry

        lax.fori_loop(0, half, added_step, 0)

        def own_step(j, carry):
            for k in (j, half + j):
                own = term(col * per_slice + k)
                to_left(k, fr, ss, sr).wait_recv()
                to_right(k, fl, ss, sr).wait_recv()
                finish(k, own + (fl[k] + fr[k]))
            return carry

        lax.fori_loop(0, half, own_step, 0)

        def sent_step(k, carry):
            far(k, right, d2, ss, sr).wait_send()
            to_right(k, fl, ss, sr).wait_send()
            to_left(k, fr, ss, sr).wait_send()
            return carry

        lax.fori_loop(0, per_slice, sent_step, 0)

    def give_right(src, dst, k, sl, ss, sr):
        return send(src, dst.at[sl * per_slice + k], ss, sr, k, right)

    def give_left(src, dst, k, sl, ss, sr):
        return send(src, dst.at[sl * per_slice + k], ss, sr, per_slice + k, left)

    def hand_on(dst, k, sl, where, ss, sr):
        at = dst.at[sl * per_slice + k]
        return send(at, at, ss, sr, 2 * per_slice + k, where)

    def give(src, dst, k, ss, sr):
        give_right(src, dst, k, col, ss, sr).start()
        give_left(src, dst, k, col, ss, sr).start()

    def relay(dst, ss, sr, use):
        def relay_step(j, carry):
            at = dst.at[left * per_slice + j]
            give_right(at, dst, j, left, ss, sr).wait_recv()
            hand_on(dst, j, left, right, ss, sr).start()
            use(left * per_slice + j)
            at = dst.at[right * per_slice + half + j]
            give_left(at, dst, half + j, right, ss, sr).wait_recv()
            hand_on(dst, half + j, right, left, ss, sr).start()
            use(right * per_slice + half + j)
            return carry

        lax.fori_loop(0, half, relay_step, 0)

    def gather_rest(dst, ss, sr, use):
        def near_step(j, carry):
            at = dst.at[left * per_slice + half + j]
            give_right(at, dst, half + j, left, ss, sr).wait_recv()
            use(left * per_slice + half + j)
            at = dst.at[right * per_slice + j]
            give_left(at, dst, j, right, ss, sr).wait_recv()
            use(right * per_slice + j)
            return carry

        lax.fori_loop(0, half, near_step, 0)

        def far_step(j, carry):
            for k in (j, half + j):
                hand_on(dst, k, across, right, ss, sr).wait_recv()
                use(across * per_slice + k)
            return carry

        lax.fori_loop(0, half, far_step, 0)

        def sent_step(k, carry):
            at = dst.at[col * per_slice + k]
            give_right(at, dst, k, col, ss, sr).wait_send()
            give_left(at, dst, k, col, ss, sr).wait_send()
            hand_on(dst, k, col, right, ss, sr).wait_send()
            return carry

        lax.fori_loop(0, per_slice, sent_step, 0)

    set_weights(bt[...])
    acc[...] = jnp.zeros_like(acc)

    def use_once(ch):
        add_products((vc[ch] - zf[ch]) * m_ref[:, pl.ds(pl.multiple_of(ch * WIDTH, WIDTH), WIDTH)], ch)

    def finish_first(k, value):
        ch = col * per_slice + k
        zf[ch] = value
        give(zf.at[ch], zf, k, ag_sa, ag_ra)
        use_once(ch)

    reduce_scatter(d2a, fla, fra, rs_sa, rs_ra, finish_first)
    relay(zf, ag_sa, ag_ra, use_once)
    gather_rest(zf, ag_sa, ag_ra, use_once)
    src2[...] = collect()
    exchange_sum(src2, ars[1], b2, row, z_size)

    set_weights(bt[...] + b2[...])
    ggram[...] = jnp.zeros_like(ggram)

    def add_gram(p, ch):
        a = jnp.concatenate(split3(p * m_ref[:, pl.ds(pl.multiple_of(ch * WIDTH, WIDTH), WIDTH)]), axis=0)
        b = jnp.concatenate(split3(p), axis=0)
        ggram[...] += dot_nt(a, b)

    def collect_gram():
        g = ggram[...]
        rows3 = g[0:new] + (g[new : 2 * new] + g[2 * new :])
        gram = rows3[:, 0:new] + (rows3[:, new : 2 * new] + rows3[:, 2 * new :])
        return gram * scale

    def keep(k):
        return pltpu.make_async_copy(po.at[k], p_hbm.at[col * per_slice + k], psem.at[k])

    def finish_second(k, value):
        ch = col * per_slice + k
        p = vc[ch] - value
        po[k] = p
        keep(k).start()
        add_gram(p, ch)

    reduce_scatter(d2b, flb, frb, rs_sb, rs_rb, finish_second)

    def give_all():
        def give_step(j, carry):
            for k, other in ((j, half + j), (half + j, j)):
                give_right(po.at[k], p_hbm, k, col, ag_sb, ag_rb).start()
                give_left(po.at[other], p_hbm, other, col, ag_sb, ag_rb).start()
            return carry

        lax.fori_loop(0, half, give_step, 0)

    upper_one, inverse_one = factorize(gram_sum(collect_gram(), ars[2], row, col, n_col, z_size, give_all))

    ggram[...] = jnp.zeros_like(ggram)
    weights = terms_of(inverse_one)

    def second_gram(k, carry):
        add_gram(apply_terms(weights, po[k]), col * per_slice + k)
        return carry

    lax.fori_loop(0, per_slice, second_gram, 0)
    hand_all = lambda: relay(p_hbm, ag_sb, ag_rb, lambda ch: None)
    upper_two, inverse_two = factorize(gram_sum(collect_gram(), ars[3], row, col, n_col, z_size, hand_all))
    f_ref[...] = jnp.dot(upper_two, upper_one, precision=HIGHEST, preferred_element_type=F32)
    t_ref[...] = jnp.dot(inverse_two, inverse_one, precision=HIGHEST, preferred_element_type=F32)

    def kept_step(k, carry):
        keep(k).wait()
        return carry

    lax.fori_loop(0, per_slice, kept_step, 0)
    gather_rest(p_hbm, ag_sb, ag_rb, lambda ch: None)


def apply_kernel(t_ref, p_ref, o_ref):
    weights = terms_of(t_ref[...])
    for i in range(p_ref.shape[0]):
        o_ref[:, i * WIDTH : (i + 1) * WIDTH] = apply_terms(weights, p_ref[i])


def local(n_col, n_row, locked, vectors, mass):
    mine, cols = locked.shape
    new = vectors.shape[0]
    chunks = cols // WIDTH
    per_slice = chunks // n_col
    z_size = n_row // GROUP
    rows = new // GROUP
    dma = pltpu.SemaphoreType.DMA

    def exchange_scratch():
        return [
            pltpu.VMEM((GROUP - 1, rows, mine), F32), dma((GROUP - 1,)), dma((GROUP - 1,)),
            pltpu.VMEM((rows, mine), F32),
            pltpu.VMEM((z_size, rows, mine), F32), dma((z_size,)), dma((z_size,)),
            dma((GROUP,)), dma((GROUP,)),
        ]

    def gram_scratch():
        packed = (new // 2, 2 * new)
        return [
            ref
            for size in (n_col, 2, GROUP // 2, z_size)
            for ref in (pltpu.VMEM(packed, F32), pltpu.VMEM((size,) + packed, F32), dma((size,)), dma((size,)))
        ]

    chunk = lambda n: pltpu.VMEM((n, new, WIDTH), F32)
    scratch = [
        pltpu.VMEM((SLOTS, mine, PAIR), F32), dma((SLOTS,)), chunk(chunks), dma((chunks,)),
        pltpu.VMEM((chunks, mine, WIDTH), BF16), pltpu.VMEM((chunks, mine, WIDTH), BF16),
        pltpu.VMEM((chunks, mine, WIDTH), BF16),
        pltpu.VMEM((3 * new, mine), F32), pltpu.VMEM((new, mine), F32), pltpu.VMEM((new, mine), F32),
        pltpu.VMEM((3 * new, mine), BF16), pltpu.VMEM((new, mine), F32), pltpu.VMEM((3 * new, 3 * new), F32),
        chunk(chunks), chunk(per_slice), chunk(3 * per_slice),
        chunk(per_slice), chunk(per_slice), chunk(per_slice),
        chunk(per_slice), chunk(per_slice), chunk(per_slice),
    ]
    scratch += [dma((3 * per_slice,))] * 8 + [dma((per_slice,))]
    scratch += exchange_scratch() * 2 + gram_scratch() * 2
    vmem = pl.BlockSpec(memory_space=pltpu.VMEM)
    hbm = pl.BlockSpec(memory_space=pl.ANY)
    projected, transform, factor = pl.pallas_call(
        functools.partial(fused, n_col, n_row, 1.0 / (cols * n_row)),
        out_shape=(
            jax.ShapeDtypeStruct((chunks, new, WIDTH), F32),
            jax.ShapeDtypeStruct((new, new), F32),
            jax.ShapeDtypeStruct((new, new), F32),
        ),
        in_specs=[hbm, hbm, vmem],
        out_specs=(hbm, vmem, vmem),
        scratch_shapes=scratch,
        compiler_params=pltpu.CompilerParams(
            collective_id=0, has_side_effects=True, vmem_limit_bytes=60 << 20
        ),
        name="project_and_factor",
    )(locked, vectors, mass.reshape(1, cols))
    block = 8
    appended = pl.pallas_call(
        apply_kernel,
        grid=(chunks // block,),
        out_shape=jax.ShapeDtypeStruct((new, cols), F32),
        in_specs=[
            pl.BlockSpec((new, new), lambda i: (0, 0)),
            pl.BlockSpec((block, new, WIDTH), lambda i: (i, 0, 0)),
        ],
        out_specs=pl.BlockSpec((new, block * WIDTH), lambda i: (0, i)),
        name="apply_factors",
    )(transform, projected)
    return (appended, factor)


def solution(mesh):
    return jax.shard_map(
        functools.partial(local, mesh.shape["col"], mesh.shape["row"]),
        mesh=mesh,
        in_specs=(P("col", "row"), P(None, "row"), P("row")),
        out_specs=(P(None, "row"), P()),
        check_vma=False,
    )
```

```python
import functools

import jax
import jax.numpy as jnp
from jax import lax
from jax.experimental import pallas as pl
from jax.experimental.pallas import tpu as pltpu
from jax.sharding import PartitionSpec as P

MESH = pl.DeviceIdType.MESH
F32 = jnp.float32
BF16 = jnp.bfloat16
HIGHEST = lax.Precision.HIGHEST
WIDTH = 1024
GROUP = 8
SLOTS = 6


def split2(x):
    high = x.astype(BF16)
    return high, (x - high.astype(F32)).astype(BF16)


def split3(x):
    high = x.astype(BF16)
    rest = x - high.astype(F32)
    middle = rest.astype(BF16)
    low = (rest - middle.astype(F32)).astype(BF16)
    return high, middle, low


def dot_nt(a, b):
    return lax.dot_general(a, b, (((1,), (1,)), ((), ())), preferred_element_type=F32)


def dot_nn(a, b):
    return lax.dot_general(a, b, (((1,), (0,)), ((), ())), preferred_element_type=F32)


def exchange_sum(scratch, row, z_size, hooks=()):
    (src, out, part, part_s, part_r, red, zbuf, z_s, z_r, full_s, full_r) = scratch
    place = lax.rem(row, GROUP)
    base = row - place
    z = lax.div(row, GROUP)
    hooks = list(hooks) + [None] * (3 - len(hooks))

    copies = []
    for d in range(1, GROUP):
        peer = lax.rem(place + d, GROUP)
        copy = pltpu.make_async_remote_copy(
            src_ref=src.at[peer], dst_ref=part.at[d - 1], send_sem=part_s.at[d - 1], recv_sem=part_r.at[d - 1],
            device_id={"row": base + peer}, device_id_type=MESH,
        )
        copy.start()
        copies.append(copy)
    if hooks[0] is not None:
        hooks[0]()
    total = src[place]
    for d in range(1, GROUP):
        copies[d - 1].wait_recv()
        total = total + part[d - 1]
    red[...] = total
    peers = [lax.rem(z + d, z_size) for d in range(1, z_size)]
    devices = [(p, {"row": p * GROUP + place}) for p in peers]
    out[place] = peer_sum(red, zbuf, z_s, z_r, z, devices, hooks[1])
    for d in range(1, GROUP):
        peer = lax.rem(place + d, GROUP)
        copy = pltpu.make_async_remote_copy(
            src_ref=out.at[place], dst_ref=out.at[place], send_sem=full_s.at[d - 1], recv_sem=full_r.at[place],
            device_id={"row": base + peer}, device_id_type=MESH,
        )
        copy.start()
        copies.append(copy)
    if hooks[2] is not None:
        hooks[2]()
    for d in range(1, GROUP):
        peer = lax.rem(place + d, GROUP)
        pltpu.make_async_remote_copy(
            src_ref=out.at[peer], dst_ref=out.at[peer], send_sem=full_s.at[d - 1], recv_sem=full_r.at[peer],
            device_id={"row": row}, device_id_type=MESH,
        ).wait_recv()
    for copy in copies:
        copy.wait_send()


def peer_copies(src, buf, sems, semr, mine, peers):
    return [
        (
            pltpu.make_async_remote_copy(
                src_ref=src, dst_ref=buf.at[mine], send_sem=sems.at[i], recv_sem=semr.at[mine],
                device_id=device, device_id_type=MESH,
            ),
            pltpu.make_async_remote_copy(
                src_ref=src, dst_ref=buf.at[peer], send_sem=sems.at[i], recv_sem=semr.at[peer],
                device_id=device, device_id_type=MESH,
            ),
        )
        for i, (peer, device) in enumerate(peers)
    ]


def peer_sum(src, buf, sems, semr, mine, peers, between=None):
    copies = peer_copies(src, buf, sems, semr, mine, peers)
    for out, _ in copies:
        out.start()
    buf[mine] = src[...]
    if between is not None:
        between()
    for _, arrival in copies:
        arrival.wait_recv()
    total = buf[0]
    for i in range(1, len(peers) + 1):
        total = total + buf[i]
    for out, _ in copies:
        out.wait_send()
    return total


def gram_sum(gram, scratch, row, col, n_col, z_size, between):
    half = gram.shape[0] // 2
    place = lax.rem(row, GROUP)
    base = row - place
    z = lax.div(row, GROUP)
    x, core = lax.div(place, 2), lax.rem(place, 2)
    x_size = GROUP // 2
    stages = [
        (n_col, col, lambda p: {"col": p}),
        (2, core, lambda p: {"row": base + 2 * x + p}),
        (x_size, x, lambda p: {"row": base + 2 * p + core}),
        (z_size, z, lambda p: {"row": p * GROUP + place}),
    ]
    total = jnp.concatenate([gram[:half], gram[half:]], axis=1)
    for i, (size, mine, device) in enumerate(stages):
        src, buf, sems, semr = scratch[4 * i : 4 * i + 4]
        src[...] = total
        peers = [lax.rem(mine + d, size) for d in range(1, size)]
        total = peer_sum(src, buf, sems, semr, mine, [(p, device(p)) for p in peers], between if i == 0 else None)
    new = gram.shape[0]
    return jnp.concatenate([total[:, :new], total[:, new:]], axis=0)


def factorize(gram):
    size = gram.shape[0]
    lane = lax.broadcasted_iota(jnp.int32, (size, 2 * size), 1)
    sub = lax.broadcasted_iota(jnp.int32, (size, 2 * size), 0)
    sub8 = lax.broadcasted_iota(jnp.int32, (8, 2 * size), 0)
    wide = jnp.concatenate([gram, jnp.zeros_like(gram)], axis=1)
    wide = jnp.where(lane < size, wide, jnp.where(lane - size == sub, 1.0, 0.0))
    blocks = [wide[8 * i : 8 * i + 8] for i in range(size // 8)]
    for j in range(size):
        b, r = divmod(j, 8)
        line = blocks[b][r : r + 1, :]
        line = jnp.broadcast_to(line * (1.0 / line[:, j : j + 1]), (8, 2 * size))
        for i in range(b, size // 8):
            if i == b and r == 7:
                continue
            column = blocks[i][:, j : j + 1]
            if i == b:
                column = jnp.where(sub8 > r, column, 0.0)
            blocks[i] = blocks[i] - column * line
    body = jnp.concatenate(blocks, axis=0)
    pivots = jnp.sum(jnp.where(lane == sub, body, 0.0), axis=1, keepdims=True)
    body = body / jnp.sqrt(pivots)
    upper = jnp.where(lane >= sub, body, 0.0)[:, :size]
    return upper, body[:, size:]


def terms_of(matrix):
    a, b, c = split3(matrix)
    zero = jnp.zeros_like(a)
    return jnp.concatenate(
        [
            jnp.concatenate([a, a, a], axis=1),
            jnp.concatenate([b, b, zero], axis=1),
            jnp.concatenate([c, zero, zero], axis=1),
        ],
        axis=0,
    )


def apply_terms(terms, x):
    new = x.shape[0]
    r = dot_nn(terms, jnp.concatenate(split3(x), axis=0))
    return r[:new] + (r[new : 2 * new] + r[2 * new :])


def fused(
    n_col, n_row, scale,
    l_hbm, v_hbm, m_ref, p_hbm, t_ref, f_ref,
    lbuf, lsem, vc, vsem, l1, l2, acc, acc2, wsp, ggram, zf, po, psem,
    *rest,
):
    sums = [rest[11 * i : 11 * i + 11] for i in range(3)]
    grams = [rest[33 + 16 * i : 49 + 16 * i] for i in range(2)]
    scatters = [rest[65 + 6 * i : 71 + 6 * i] for i in range(4)]
    gathers = [rest[89 + 2 * i : 91 + 2 * i] for i in range(4)]
    col, row = lax.axis_index("col"), lax.axis_index("row")
    right, left = lax.rem(col + 1, n_col), lax.rem(col + n_col - 1, n_col)
    across = lax.rem(col + 2, n_col)
    z_size = n_row // GROUP
    place = lax.rem(row, GROUP)
    base = row - place
    z = lax.div(row, GROUP)
    chunks, part = vc.shape[1], vc.shape[2]
    per_slice = chunks // n_col
    half = per_slice // 2
    new = 2 * part

    def columns(ch):
        return pl.ds(pl.multiple_of(ch * WIDTH, WIDTH), WIDTH)

    def load_l(ch, slot):
        return pltpu.make_async_copy(l_hbm.at[:, columns(ch)], lbuf.at[slot], lsem.at[slot])

    def load_v(h, ch):
        return pltpu.make_async_copy(
            v_hbm.at[h * part : (h + 1) * part, columns(ch)], vc.at[h, ch], vsem.at[h, ch]
        )

    for ch in range(SLOTS):
        load_v(0, ch).start()
        load_v(1, ch).start()
        load_l(ch, ch).start()

    barrier = pltpu.get_barrier_semaphore()
    for d in range(1, GROUP):
        pl.semaphore_signal(barrier, inc=1, device_id={"row": base + lax.rem(place + d, GROUP)}, device_id_type=MESH)
    for d in range(1, z_size):
        pl.semaphore_signal(
            barrier, inc=1, device_id={"row": lax.rem(z + d, z_size) * GROUP + place}, device_id_type=MESH
        )
    for d in range(1, n_col):
        pl.semaphore_signal(barrier, inc=1, device_id={"col": lax.rem(col + d, n_col)}, device_id_type=MESH)

    def collect(total):
        n = total.shape[0] // 3
        return (total[0:n] + (total[n : 2 * n] + total[2 * n :])) * scale

    acc[...] = jnp.zeros_like(acc)
    acc2[...] = jnp.zeros_like(acc2)

    def first_step(ch, carry):
        slot = lax.rem(ch, SLOTS)
        load_l(ch, slot).wait()
        high, low = split2(lbuf[slot])
        l1[ch] = high
        l2[ch] = low
        load_v(0, ch).wait()
        load_v(1, ch).wait()
        x = jnp.concatenate([vc[0, ch], vc[1, ch]], axis=0) * m_ref[:, columns(ch)]
        a = jnp.concatenate(split3(x), axis=0)
        acc[...] += dot_nt(a, high)
        acc[0 : 2 * new] += dot_nt(a[0 : 2 * new], low)

        @pl.when(ch + SLOTS < chunks)
        def _():
            load_l(ch + SLOTS, slot).start()
            load_v(0, ch + SLOTS).start()
            load_v(1, ch + SLOTS).start()

        return carry

    lax.fori_loop(0, chunks, first_step, 0)
    first = collect(acc[...])
    src = sums[0][0]
    for i in range(GROUP):
        src[i] = first[i * new // GROUP : (i + 1) * new // GROUP]
    pl.semaphore_wait(barrier, (GROUP - 1) + (z_size - 1) + (n_col - 1))
    exchange_sum(sums[0], row, z_size)
    b1 = [jnp.concatenate([sums[0][1][GROUP // 2 * h + i] for i in range(GROUP // 2)], axis=0) for h in range(2)]

    def set_weights(h, b):
        for i, w in enumerate(split3(b)):
            wsp[h, i * part : (i + 1) * part] = w

    def term(h, ch):
        r = dot_nn(wsp[h], l1[ch])
        s = dot_nn(wsp[h, 0 : 2 * part], l2[ch])
        return r[0:part] + ((r[part : 2 * part] + s[0:part]) + (r[2 * part :] + s[part:]))

    def send(src, dst, sems, semr, index, where):
        return pltpu.make_async_remote_copy(
            src_ref=src, dst_ref=dst, send_sem=sems.at[index], recv_sem=semr.at[index],
            device_id={"col": where}, device_id_type=MESH,
        )

    def far(c, k, where):
        d2, fl, fr, stage, ss, sr = scatters[c]
        return send(stage.at[k], d2.at[k], ss, sr, k, where)

    def to_right(c, k):
        d2, fl, fr, stage, ss, sr = scatters[c]
        return send(stage.at[per_slice + k], fl.at[k], ss, sr, per_slice + k, right)

    def to_left(c, k):
        d2, fl, fr, stage, ss, sr = scatters[c]
        return send(stage.at[2 * per_slice + k], fr.at[k], ss, sr, 2 * per_slice + k, left)

    def loop(count, body):
        def step(j, carry):
            body(j)
            return carry

        lax.fori_loop(0, count, step, 0)

    def scatter_start(c):
        h, stage = c % 2, scatters[c][3]

        def far_step(j):
            stage[j] = term(h, across * per_slice + j)
            far(c, j, right).start()
            stage[half + j] = term(h, across * per_slice + half + j)
            far(c, half + j, left).start()

        def pure_step(j):
            stage[per_slice + half + j] = term(h, right * per_slice + half + j)
            to_right(c, half + j).start()
            stage[2 * per_slice + j] = term(h, left * per_slice + j)
            to_left(c, j).start()

        loop(half, far_step)
        loop(half, pure_step)

    def scatter_added(c):
        h, d2, stage = c % 2, scatters[c][0], scatters[c][3]

        def added_step(j):
            own = term(h, right * per_slice + j)
            far(c, j, right).wait_recv()
            stage[per_slice + j] = own + d2[j]
            to_right(c, j).start()
            own = term(h, left * per_slice + half + j)
            far(c, half + j, left).wait_recv()
            stage[2 * per_slice + half + j] = own + d2[half + j]
            to_left(c, half + j).start()

        loop(half, added_step)

    def scatter_own(c, finish):
        h, fl, fr = c % 2, scatters[c][1], scatters[c][2]

        def own_step(j):
            for k in (j, half + j):
                own = term(h, col * per_slice + k)
                to_left(c, k).wait_recv()
                to_right(c, k).wait_recv()
                finish(k, own + (fl[k] + fr[k]))

        loop(half, own_step)

    def targets(g):
        return (zf if g < 2 else p_hbm).at[g % 2]

    def give_right(g, src, k, sl):
        return send(src, targets(g).at[sl * per_slice + k], *gathers[g], k, right)

    def give_left(g, src, k, sl):
        return send(src, targets(g).at[sl * per_slice + k], *gathers[g], per_slice + k, left)

    def hand_on(g, k, sl, where):
        at = targets(g).at[sl * per_slice + k]
        return send(at, at, *gathers[g], 2 * per_slice + k, where)

    def relay(g, j, use):
        give_right(g, targets(g).at[left * per_slice + j], j, left).wait_recv()
        hand_on(g, j, left, right).start()
        give_left(g, targets(g).at[right * per_slice + half + j], half + j, right).wait_recv()
        hand_on(g, half + j, right, left).start()
        use(left * per_slice + j)
        use(right * per_slice + half + j)

    def gather_rest(g, use):
        def near_step(j):
            give_right(g, targets(g).at[left * per_slice + half + j], half + j, left).wait_recv()
            use(left * per_slice + half + j)
            give_left(g, targets(g).at[right * per_slice + j], j, right).wait_recv()
            use(right * per_slice + j)

        def far_step(j):
            for k in (j, half + j):
                hand_on(g, k, across, right).wait_recv()
                use(across * per_slice + k)

        loop(half, near_step)
        loop(half, far_step)

    def use_once(h):
        def use(ch):
            x = (vc[h, ch] - zf[h, ch]) * m_ref[:, columns(ch)]
            a = jnp.concatenate(split3(x), axis=0)
            acc2[h] += dot_nt(a, l1[ch])
            acc2[h, 0 : 2 * part] += dot_nt(a[0 : 2 * part], l2[ch])

        return use

    def finish_first(h):
        def finish(k, value):
            ch = col * per_slice + k
            zf[h, ch] = value
            give_right(h, zf.at[h, ch], k, col).start()
            give_left(h, zf.at[h, ch], k, col).start()
            use_once(h)(ch)

        return finish

    def second_sum(h, hooks):
        second = collect(acc2[h])
        src, out = sums[1 + h][0], sums[1 + h][1]
        wide = second.shape[1] // 2
        for i in range(GROUP):
            r, c = divmod(i, 2)
            src[i] = second[8 * r : 8 * r + 8, c * wide : (c + 1) * wide]
        exchange_sum(sums[1 + h], row, z_size, hooks)
        lines = [jnp.concatenate([out[2 * r], out[2 * r + 1]], axis=1) for r in range(GROUP // 2)]
        set_weights(h, b1[h] + jnp.concatenate(lines, axis=0))

    set_weights(0, b1[0])
    set_weights(1, b1[1])
    scatter_start(0)
    scatter_added(0)
    scatter_start(1)
    scatter_own(0, finish_first(0))
    scatter_added(1)
    loop(half, lambda j: relay(0, j, use_once(0)))
    scatter_own(1, finish_first(1))
    gather_rest(0, use_once(0))
    second_sum(0, [lambda j=j: relay(1, j, use_once(1)) for j in range(half)])
    scatter_start(2)
    gather_rest(1, use_once(1))
    second_sum(1, [None, lambda: scatter_added(2)])
    scatter_start(3)

    ggram[...] = jnp.zeros_like(ggram)

    def add_gram(p, ch):
        a = jnp.concatenate(split3(p * m_ref[:, columns(ch)]), axis=0)
        b = jnp.concatenate(split3(p), axis=0)
        ggram[...] += dot_nt(a, b)

    def collect_gram():
        g = ggram[...]
        rows3 = g[0:new] + (g[new : 2 * new] + g[2 * new :])
        gram = rows3[:, 0:new] + (rows3[:, new : 2 * new] + rows3[:, 2 * new :])
        return gram * scale

    def keep(h, k):
        return pltpu.make_async_copy(po.at[h, k], p_hbm.at[h, col * per_slice + k], psem.at[h, k])

    def both(k):
        return jnp.concatenate([po[0, k], po[1, k]], axis=0)

    def finish_second(h):
        def finish(k, value):
            ch = col * per_slice + k
            po[h, k] = vc[h, ch] - value
            keep(h, k).start()
            if h == 1:
                add_gram(both(k), ch)

        return finish

    scatter_own(2, finish_second(0))
    scatter_added(3)
    scatter_own(3, finish_second(1))

    def give_all():
        for h in range(2):

            def give_step(j):
                for k, other in ((j, half + j), (half + j, j)):
                    give_right(2 + h, po.at[h, k], k, col).start()
                    give_left(2 + h, po.at[h, other], other, col).start()

            loop(half, give_step)

    upper_one, inverse_one = factorize(gram_sum(collect_gram(), grams[0], row, col, n_col, z_size, give_all))

    ggram[...] = jnp.zeros_like(ggram)
    weights = terms_of(inverse_one)
    loop(per_slice, lambda k: add_gram(apply_terms(weights, both(k)), col * per_slice + k))

    def hand_all():
        for h in range(2):
            loop(half, lambda j: relay(2 + h, j, lambda ch: None))

    upper_two, inverse_two = factorize(gram_sum(collect_gram(), grams[1], row, col, n_col, z_size, hand_all))
    f_ref[...] = jnp.dot(upper_two, upper_one, precision=HIGHEST, preferred_element_type=F32)
    t_ref[...] = jnp.dot(inverse_two, inverse_one, precision=HIGHEST, preferred_element_type=F32)

    for h in range(2):
        gather_rest(2 + h, lambda ch: None)

    def sent_step(k):
        for h in range(2):
            keep(h, k).wait()
        for c in range(4):
            far(c, k, right).wait_send()
            to_right(c, k).wait_send()
            to_left(c, k).wait_send()
        for g in range(4):
            at = targets(g).at[col * per_slice + k]
            give_right(g, at, k, col).wait_send()
            give_left(g, at, k, col).wait_send()
            hand_on(g, k, col, right).wait_send()

    loop(per_slice, sent_step)


def apply_kernel(t_ref, p_ref, o_ref):
    weights = terms_of(t_ref[...])
    for i in range(p_ref.shape[1]):
        p = jnp.concatenate([p_ref[0, i], p_ref[1, i]], axis=0)
        o_ref[:, i * WIDTH : (i + 1) * WIDTH] = apply_terms(weights, p)


def local(n_col, n_row, locked, vectors, mass):
    mine, cols = locked.shape
    new = vectors.shape[0]
    part = new // 2
    chunks = cols // WIDTH
    per_slice = chunks // n_col
    z_size = n_row // GROUP
    dma = pltpu.SemaphoreType.DMA

    def exchange_scratch(rows, width):
        return [
            pltpu.VMEM((GROUP, rows, width), F32), pltpu.VMEM((GROUP, rows, width), F32),
            pltpu.VMEM((GROUP - 1, rows, width), F32), dma((GROUP - 1,)), dma((GROUP - 1,)),
            pltpu.VMEM((rows, width), F32),
            pltpu.VMEM((z_size, rows, width), F32), dma((z_size,)), dma((z_size,)),
            dma((GROUP,)), dma((GROUP,)),
        ]

    def gram_scratch():
        packed = (new // 2, 2 * new)
        return [
            ref
            for size in (n_col, 2, GROUP // 2, z_size)
            for ref in (pltpu.VMEM(packed, F32), pltpu.VMEM((size,) + packed, F32), dma((size,)), dma((size,)))
        ]

    chunk = lambda *n: pltpu.VMEM(n + (part, WIDTH), F32)
    scratch = [
        pltpu.VMEM((SLOTS, mine, WIDTH), F32), dma((SLOTS,)), chunk(2, chunks), dma((2, chunks)),
        pltpu.VMEM((chunks, mine, WIDTH), BF16), pltpu.VMEM((chunks, mine, WIDTH), BF16),
        pltpu.VMEM((3 * new, mine), F32), pltpu.VMEM((2, 3 * part, mine), F32),
        pltpu.VMEM((2, 3 * part, mine), BF16), pltpu.VMEM((3 * new, 3 * new), F32),
        chunk(2, chunks), chunk(2, per_slice), dma((2, per_slice)),
    ]
    scratch += exchange_scratch(new // GROUP, mine) + exchange_scratch(8, part * mine // (8 * GROUP)) * 2
    scratch += gram_scratch() * 2
    ring = [dma((3 * per_slice,)), dma((3 * per_slice,))]
    scratch += ([chunk(per_slice)] * 3 + [chunk(3 * per_slice)] + ring) * 4 + ring * 4
    vmem = pl.BlockSpec(memory_space=pltpu.VMEM)
    hbm = pl.BlockSpec(memory_space=pl.ANY)
    projected, transform, factor = pl.pallas_call(
        functools.partial(fused, n_col, n_row, 1.0 / (cols * n_row)),
        out_shape=(
            jax.ShapeDtypeStruct((2, chunks, part, WIDTH), F32),
            jax.ShapeDtypeStruct((new, new), F32),
            jax.ShapeDtypeStruct((new, new), F32),
        ),
        in_specs=[hbm, hbm, vmem],
        out_specs=(hbm, vmem, vmem),
        scratch_shapes=scratch,
        compiler_params=pltpu.CompilerParams(
            collective_id=0, has_side_effects=True, vmem_limit_bytes=60 << 20
        ),
        name="project_and_factor",
    )(locked, vectors, mass.reshape(1, cols))
    block = 8
    appended = pl.pallas_call(
        apply_kernel,
        grid=(chunks // block,),
        out_shape=jax.ShapeDtypeStruct((new, cols), F32),
        in_specs=[
            pl.BlockSpec((new, new), lambda i: (0, 0)),
            pl.BlockSpec((2, block, part, WIDTH), lambda i: (0, i, 0, 0)),
        ],
        out_specs=pl.BlockSpec((new, block * WIDTH), lambda i: (0, i)),
        name="apply_factors",
    )(transform, projected)
    return (appended, factor)


def solution(mesh):
    return jax.shard_map(
        functools.partial(local, mesh.shape["col"], mesh.shape["row"]),
        mesh=mesh,
        in_specs=(P("col", "row"), P(None, "row"), P("row")),
        out_specs=(P(None, "row"), P()),
        check_vma=False,
    )
```

```python
import functools

import jax
import jax.numpy as jnp
from jax import lax
from jax.experimental import pallas as pl
from jax.experimental.pallas import tpu as pltpu
from jax.sharding import PartitionSpec as P

MESH = pl.DeviceIdType.MESH
F32 = jnp.float32
BF16 = jnp.bfloat16
HIGHEST = lax.Precision.HIGHEST
WIDTH = 1024
GROUP = 8
SLOTS = 4


def split2(x):
    high = x.astype(BF16)
    return high, (x - high.astype(F32)).astype(BF16)


def split3(x):
    high = x.astype(BF16)
    rest = x - high.astype(F32)
    middle = rest.astype(BF16)
    low = (rest - middle.astype(F32)).astype(BF16)
    return high, middle, low


def dot_nt(a, b):
    return lax.dot_general(a, b, (((1,), (1,)), ((), ())), preferred_element_type=F32)


def dot_nn(a, b):
    return lax.dot_general(a, b, (((1,), (0,)), ((), ())), preferred_element_type=F32)


def exchange_sum(scratch, row, z_size, hooks=()):
    (src, out, part, part_s, part_r, red, zbuf, z_s, z_r, full_s, full_r) = scratch
    place = lax.rem(row, GROUP)
    base = row - place
    z = lax.div(row, GROUP)
    hooks = list(hooks) + [None] * (3 - len(hooks))

    copies = []
    for d in range(1, GROUP):
        peer = lax.rem(place + d, GROUP)
        copy = pltpu.make_async_remote_copy(
            src_ref=src.at[peer], dst_ref=part.at[d - 1], send_sem=part_s.at[d - 1], recv_sem=part_r.at[d - 1],
            device_id={"row": base + peer}, device_id_type=MESH,
        )
        copy.start()
        copies.append(copy)
    if hooks[0] is not None:
        hooks[0]()
    total = src[place]
    for d in range(1, GROUP):
        copies[d - 1].wait_recv()
        total = total + part[d - 1]
    red[...] = total
    peers = [lax.rem(z + d, z_size) for d in range(1, z_size)]
    devices = [(p, {"row": p * GROUP + place}) for p in peers]
    out[place] = peer_sum(red, zbuf, z_s, z_r, z, devices, hooks[1])
    for d in range(1, GROUP):
        peer = lax.rem(place + d, GROUP)
        copy = pltpu.make_async_remote_copy(
            src_ref=out.at[place], dst_ref=out.at[place], send_sem=full_s.at[d - 1], recv_sem=full_r.at[place],
            device_id={"row": base + peer}, device_id_type=MESH,
        )
        copy.start()
        copies.append(copy)
    if hooks[2] is not None:
        hooks[2]()
    for d in range(1, GROUP):
        peer = lax.rem(place + d, GROUP)
        pltpu.make_async_remote_copy(
            src_ref=out.at[peer], dst_ref=out.at[peer], send_sem=full_s.at[d - 1], recv_sem=full_r.at[peer],
            device_id={"row": row}, device_id_type=MESH,
        ).wait_recv()
    for copy in copies:
        copy.wait_send()


def peer_copies(src, buf, sems, semr, mine, peers):
    return [
        (
            pltpu.make_async_remote_copy(
                src_ref=src, dst_ref=buf.at[mine], send_sem=sems.at[i], recv_sem=semr.at[mine],
                device_id=device, device_id_type=MESH,
            ),
            pltpu.make_async_remote_copy(
                src_ref=src, dst_ref=buf.at[peer], send_sem=sems.at[i], recv_sem=semr.at[peer],
                device_id=device, device_id_type=MESH,
            ),
        )
        for i, (peer, device) in enumerate(peers)
    ]


def peer_sum(src, buf, sems, semr, mine, peers, between=None):
    copies = peer_copies(src, buf, sems, semr, mine, peers)
    for out, _ in copies:
        out.start()
    buf[mine] = src[...]
    if between is not None:
        between()
    for _, arrival in copies:
        arrival.wait_recv()
    total = buf[0]
    for i in range(1, len(peers) + 1):
        total = total + buf[i]
    for out, _ in copies:
        out.wait_send()
    return total


def gram_sum(gram, scratch, row, col, n_col, z_size, first, last):
    half = gram.shape[0] // 2
    place = lax.rem(row, GROUP)
    base = row - place
    z = lax.div(row, GROUP)
    x, core = lax.div(place, 2), lax.rem(place, 2)
    x_size = GROUP // 2
    stages = [
        (2, core, lambda p: {"row": base + 2 * x + p}, first),
        (x_size, x, lambda p: {"row": base + 2 * p + core}, None),
        (z_size, z, lambda p: {"row": p * GROUP + place}, None),
        (n_col, col, lambda p: {"col": p}, last),
    ]
    total = jnp.concatenate([gram[:half], gram[half:]], axis=1)
    for i, (size, mine, device, between) in enumerate(stages):
        src, buf, sems, semr = scratch[4 * i : 4 * i + 4]
        src[...] = total
        peers = [lax.rem(mine + d, size) for d in range(1, size)]
        total = peer_sum(src, buf, sems, semr, mine, [(p, device(p)) for p in peers], between)
    new = gram.shape[0]
    return jnp.concatenate([total[:, :new], total[:, new:]], axis=0)


def factorize(gram):
    size = gram.shape[0]
    lane = lax.broadcasted_iota(jnp.int32, (size, 2 * size), 1)
    sub = lax.broadcasted_iota(jnp.int32, (size, 2 * size), 0)
    sub8 = lax.broadcasted_iota(jnp.int32, (8, 2 * size), 0)
    wide = jnp.concatenate([gram, jnp.zeros_like(gram)], axis=1)
    wide = jnp.where(lane < size, wide, jnp.where(lane - size == sub, 1.0, 0.0))
    blocks = [wide[8 * i : 8 * i + 8] for i in range(size // 8)]
    full = lambda x: jnp.broadcast_to(x, (8, 2 * size))
    for b in range(size // 8):
        j = 8 * b
        lines = [full(blocks[b][a : a + 1, :]) for a in range(8)]
        square = [[full(line[:, j + c : j + c + 1]) for c in range(8)] for line in lines]
        inverse = []
        for p in range(8):
            inverse.append(1.0 / square[p][p])
            for a in range(p + 1, 8):
                times = square[a][p] * inverse[p]
                lines[a] = lines[a] - times * lines[p]
                for c in range(p + 1, 8):
                    square[a][c] = square[a][c] - times * square[p][c]
        for i in range(b + 1, size // 8):
            column = [full(blocks[i][:, j + c : j + c + 1]) for c in range(8)]
            for p in range(8):
                times = column[p] * inverse[p]
                for q in range(p + 1, 8):
                    column[q] = column[q] - times * square[p][q]
                blocks[i] = blocks[i] - times * lines[p]
        for a in range(8):
            blocks[b] = jnp.where(sub8 == a, lines[a], blocks[b])
    body = jnp.concatenate(blocks, axis=0)
    pivots = jnp.sum(jnp.where(lane == sub, body, 0.0), axis=1, keepdims=True)
    body = body / jnp.sqrt(pivots)
    upper = jnp.where(lane >= sub, body, 0.0)[:, :size]
    return upper, body[:, size:]


def terms_of(matrix):
    a, b, c = split3(matrix)
    zero = jnp.zeros_like(a)
    return jnp.concatenate(
        [
            jnp.concatenate([a, a, a], axis=1),
            jnp.concatenate([b, b, zero], axis=1),
            jnp.concatenate([c, zero, zero], axis=1),
        ],
        axis=0,
    )


def apply_terms(terms, x):
    new = x.shape[0]
    r = dot_nn(terms, jnp.concatenate(split3(x), axis=0))
    return r[:new] + (r[new : 2 * new] + r[2 * new :])


def fused(
    n_col, n_row, scale,
    l_hbm, v_hbm, m_ref, p_hbm, t_ref, f_ref,
    lbuf, lsem, vc, vsem, l1, l2, acc, acc2, wsp, ggram, zf, po, psem,
    *rest,
):
    sums = [rest[11 * i : 11 * i + 11] for i in range(3)]
    grams = [rest[33 + 16 * i : 49 + 16 * i] for i in range(2)]
    scatters = [rest[65 + 6 * i : 71 + 6 * i] for i in range(4)]
    gathers = [rest[89 + 2 * i : 91 + 2 * i] for i in range(4)]
    col, row = lax.axis_index("col"), lax.axis_index("row")
    right, left = lax.rem(col + 1, n_col), lax.rem(col + n_col - 1, n_col)
    across = lax.rem(col + 2, n_col)
    z_size = n_row // GROUP
    place = lax.rem(row, GROUP)
    base = row - place
    z = lax.div(row, GROUP)
    chunks, part = vc.shape[1], vc.shape[2]
    per_slice = chunks // n_col
    half = per_slice // 2
    new = 2 * part

    def columns(ch):
        return pl.ds(pl.multiple_of(ch * WIDTH, WIDTH), WIDTH)

    def load_l(ch, slot):
        pair = pl.ds(pl.multiple_of(ch * 2 * WIDTH, 2 * WIDTH), 2 * WIDTH)
        return pltpu.make_async_copy(l_hbm.at[:, pair], lbuf.at[slot], lsem.at[slot])

    def load_v(h, ch):
        return pltpu.make_async_copy(
            v_hbm.at[h * part : (h + 1) * part, columns(ch)], vc.at[h, ch], vsem.at[h, ch]
        )

    def load(pair, slot):
        for i in range(2):
            for h in range(2):
                load_v(h, 2 * pair + i).start()
        load_l(pair, slot).start()

    for pair in range(SLOTS):
        load(pair, pair)

    barrier = pltpu.get_barrier_semaphore()
    for d in range(1, GROUP):
        pl.semaphore_signal(barrier, inc=1, device_id={"row": base + lax.rem(place + d, GROUP)}, device_id_type=MESH)
    for d in range(1, z_size):
        pl.semaphore_signal(
            barrier, inc=1, device_id={"row": lax.rem(z + d, z_size) * GROUP + place}, device_id_type=MESH
        )
    for d in range(1, n_col):
        pl.semaphore_signal(barrier, inc=1, device_id={"col": lax.rem(col + d, n_col)}, device_id_type=MESH)

    def collect(total):
        n = total.shape[0] // 3
        return (total[0:n] + (total[n : 2 * n] + total[2 * n :])) * scale

    acc[...] = jnp.zeros_like(acc)
    acc2[...] = jnp.zeros_like(acc2)

    def first_step(pair, carry):
        slot = lax.rem(pair, SLOTS)
        load_l(pair, slot).wait()
        high, low = split2(lbuf[slot])
        x = []
        for i in range(2):
            ch = 2 * pair + i
            l1[ch] = high[:, i * WIDTH : (i + 1) * WIDTH]
            l2[ch] = low[:, i * WIDTH : (i + 1) * WIDTH]
            load_v(0, ch).wait()
            load_v(1, ch).wait()
            x.append(jnp.concatenate([vc[0, ch], vc[1, ch]], axis=0) * m_ref[:, columns(ch)])
        a = jnp.concatenate(split3(jnp.concatenate(x, axis=1)), axis=0)
        acc[...] += dot_nt(a, high)
        acc[0 : 2 * new] += dot_nt(a[0 : 2 * new], low)

        @pl.when(pair + SLOTS < chunks // 2)
        def _():
            load(pair + SLOTS, slot)

        return carry

    lax.fori_loop(0, chunks // 2, first_step, 0)
    first = collect(acc[...])
    src = sums[0][0]
    for i in range(GROUP):
        src[i] = first[i * new // GROUP : (i + 1) * new // GROUP]
    pl.semaphore_wait(barrier, (GROUP - 1) + (z_size - 1) + (n_col - 1))
    exchange_sum(sums[0], row, z_size)
    b1 = [jnp.concatenate([sums[0][1][GROUP // 2 * h + i] for i in range(GROUP // 2)], axis=0) for h in range(2)]

    def set_weights(h, b):
        for i, w in enumerate(split3(b)):
            wsp[h, i * part : (i + 1) * part] = w

    def term(h, ch):
        r = dot_nn(wsp[h], l1[ch])
        s = dot_nn(wsp[h, 0 : 2 * part], l2[ch])
        return r[0:part] + ((r[part : 2 * part] + s[0:part]) + (r[2 * part :] + s[part:]))

    def send(src, dst, sems, semr, index, where):
        return pltpu.make_async_remote_copy(
            src_ref=src, dst_ref=dst, send_sem=sems.at[index], recv_sem=semr.at[index],
            device_id={"col": where}, device_id_type=MESH,
        )

    def far(c, k, where):
        d2, fl, fr, stage, ss, sr = scatters[c]
        return send(stage.at[k], d2.at[k], ss, sr, k, where)

    def to_right(c, k):
        d2, fl, fr, stage, ss, sr = scatters[c]
        return send(stage.at[per_slice + k], fl.at[k], ss, sr, per_slice + k, right)

    def to_left(c, k):
        d2, fl, fr, stage, ss, sr = scatters[c]
        return send(stage.at[2 * per_slice + k], fr.at[k], ss, sr, 2 * per_slice + k, left)

    def loop(count, body):
        def step(j, carry):
            body(j)
            return carry

        lax.fori_loop(0, count, step, 0)

    def scatter_start(c):
        h, stage = c % 2, scatters[c][3]

        def far_step(j):
            stage[j] = term(h, across * per_slice + j)
            far(c, j, right).start()
            stage[half + j] = term(h, across * per_slice + half + j)
            far(c, half + j, left).start()

        def pure_step(j):
            stage[per_slice + half + j] = term(h, right * per_slice + half + j)
            to_right(c, half + j).start()
            stage[2 * per_slice + j] = term(h, left * per_slice + j)
            to_left(c, j).start()

        loop(half, far_step)
        loop(half, pure_step)

    def scatter_added(c):
        h, d2, stage = c % 2, scatters[c][0], scatters[c][3]

        def added_step(j):
            own = term(h, right * per_slice + j)
            far(c, j, right).wait_recv()
            stage[per_slice + j] = own + d2[j]
            to_right(c, j).start()
            own = term(h, left * per_slice + half + j)
            far(c, half + j, left).wait_recv()
            stage[2 * per_slice + half + j] = own + d2[half + j]
            to_left(c, half + j).start()

        loop(half, added_step)

    def scatter_own(c, finish, done):
        h, fl, fr = c % 2, scatters[c][1], scatters[c][2]

        def own_step(j):
            for k in (j, half + j):
                own = term(h, col * per_slice + k)
                to_left(c, k).wait_recv()
                to_right(c, k).wait_recv()
                finish(k, own + (fl[k] + fr[k]))
            done(j)

        loop(half, own_step)

    def targets(g):
        return (zf if g < 2 else p_hbm).at[g % 2]

    def give_right(g, src, k, sl):
        return send(src, targets(g).at[sl * per_slice + k], *gathers[g], k, right)

    def give_left(g, src, k, sl):
        return send(src, targets(g).at[sl * per_slice + k], *gathers[g], per_slice + k, left)

    def hand_on(g, k, sl, where):
        at = targets(g).at[sl * per_slice + k]
        return send(at, at, *gathers[g], 2 * per_slice + k, where)

    def relay(g, j, use):
        give_right(g, targets(g).at[left * per_slice + j], j, left).wait_recv()
        hand_on(g, j, left, right).start()
        give_left(g, targets(g).at[right * per_slice + half + j], half + j, right).wait_recv()
        hand_on(g, half + j, right, left).start()
        use(left * per_slice + j)
        use(right * per_slice + half + j)

    def give_first(g, j, src):
        give_right(g, src.at[j], j, col).start()
        give_left(g, src.at[half + j], half + j, col).start()

    def give_last(g, j, src):
        give_left(g, src.at[j], j, col).start()
        give_right(g, src.at[half + j], half + j, col).start()

    def gather_near(g, use):
        def near_step(j):
            give_right(g, targets(g).at[left * per_slice + half + j], half + j, left).wait_recv()
            give_left(g, targets(g).at[right * per_slice + j], j, right).wait_recv()
            use(left * per_slice + half + j)
            use(right * per_slice + j)

        loop(half, near_step)

    def gather_far(g, use):
        def far_step(j):
            for k in (j, half + j):
                hand_on(g, k, across, right).wait_recv()
            for k in (j, half + j):
                use(across * per_slice + k)

        loop(half, far_step)

    def use_once(h):
        def use(ch):
            x = (vc[h, ch] - zf[h, ch]) * m_ref[:, columns(ch)]
            a = jnp.concatenate(split3(x), axis=0)
            acc2[h] += dot_nt(a, l1[ch])
            acc2[h, 0 : 2 * part] += dot_nt(a[0 : 2 * part], l2[ch])

        return use

    def own_first(h):
        mine = zf.at[h, pl.ds(col * per_slice, per_slice)]

        def finish(k, value):
            zf[h, col * per_slice + k] = value

        scatter_own(h, finish, lambda j: give_first(h, j, mine))
        loop(half, lambda j: give_last(h, j, mine))
        loop(per_slice, lambda k: use_once(h)(col * per_slice + k))

    def second_sum(h, hooks):
        second = collect(acc2[h])
        src, out = sums[1 + h][0], sums[1 + h][1]
        wide = second.shape[1] // 2
        for i in range(GROUP):
            r, c = divmod(i, 2)
            src[i] = second[8 * r : 8 * r + 8, c * wide : (c + 1) * wide]
        exchange_sum(sums[1 + h], row, z_size, hooks)
        lines = [jnp.concatenate([out[2 * r], out[2 * r + 1]], axis=1) for r in range(GROUP // 2)]
        set_weights(h, b1[h] + jnp.concatenate(lines, axis=0))

    set_weights(0, b1[0])
    set_weights(1, b1[1])
    scatter_start(0)
    scatter_added(0)
    scatter_start(1)
    own_first(0)
    scatter_added(1)
    loop(half, lambda j: relay(0, j, use_once(0)))
    own_first(1)
    gather_near(0, use_once(0))
    gather_far(0, use_once(0))
    second_sum(0, [lambda j=j: relay(1, j, use_once(1)) for j in range(half)] + [lambda: gather_near(1, use_once(1))])
    scatter_start(2)
    gather_far(1, use_once(1))
    second_sum(1, [None, lambda: scatter_added(2)])
    scatter_start(3)

    ggram[...] = jnp.zeros_like(ggram)

    def add_gram(p, ch):
        a = jnp.concatenate(split3(p * m_ref[:, columns(ch)]), axis=0)
        b = jnp.concatenate(split3(p), axis=0)
        ggram[...] += dot_nt(a, b)

    def collect_gram():
        g = ggram[...]
        rows3 = g[0:new] + (g[new : 2 * new] + g[2 * new :])
        gram = rows3[:, 0:new] + (rows3[:, new : 2 * new] + rows3[:, 2 * new :])
        return gram * scale

    def keep(h, k):
        return pltpu.make_async_copy(po.at[h, k], p_hbm.at[h, col * per_slice + k], psem.at[h, k])

    def both(k):
        return jnp.concatenate([po[0, k], po[1, k]], axis=0)

    def finish_second(h):
        def finish(k, value):
            ch = col * per_slice + k
            po[h, k] = vc[h, ch] - value
            keep(h, k).start()
            if h == 1:
                add_gram(both(k), ch)

        return finish

    nothing = lambda ch: None
    scatter_own(2, finish_second(0), nothing)
    scatter_added(3)

    def give_all(h):
        loop(half, lambda j: give_first(2 + h, j, po.at[h]))
        loop(half, lambda j: give_last(2 + h, j, po.at[h]))

    def hand_all(h):
        loop(half, lambda j: relay(2 + h, j, nothing))

    give_all(0)
    scatter_own(3, finish_second(1), nothing)
    gram = gram_sum(collect_gram(), grams[0], row, col, n_col, z_size, None, lambda: give_all(1))
    upper_one, inverse_one = factorize(gram)

    ggram[...] = jnp.zeros_like(ggram)
    weights = terms_of(inverse_one)
    loop(per_slice, lambda k: add_gram(apply_terms(weights, both(k)), col * per_slice + k))
    gram = gram_sum(collect_gram(), grams[1], row, col, n_col, z_size, lambda: hand_all(0), lambda: hand_all(1))
    upper_two, inverse_two = factorize(gram)
    f_ref[...] = jnp.dot(upper_two, upper_one, precision=HIGHEST, preferred_element_type=F32)
    t_ref[...] = jnp.dot(inverse_two, inverse_one, precision=HIGHEST, preferred_element_type=F32)

    for h in range(2):
        gather_near(2 + h, nothing)
        gather_far(2 + h, nothing)

    def sent_step(k):
        for h in range(2):
            keep(h, k).wait()
        for c in range(4):
            far(c, k, right).wait_send()
            to_right(c, k).wait_send()
            to_left(c, k).wait_send()
        for g in range(4):
            at = targets(g).at[col * per_slice + k]
            give_right(g, at, k, col).wait_send()
            give_left(g, at, k, col).wait_send()
            hand_on(g, k, col, right).wait_send()

    loop(per_slice, sent_step)


def apply_kernel(t_ref, p_ref, o_ref):
    weights = terms_of(t_ref[...])
    for i in range(p_ref.shape[1]):
        p = jnp.concatenate([p_ref[0, i], p_ref[1, i]], axis=0)
        o_ref[:, i * WIDTH : (i + 1) * WIDTH] = apply_terms(weights, p)


def local(n_col, n_row, locked, vectors, mass):
    mine, cols = locked.shape
    new = vectors.shape[0]
    part = new // 2
    chunks = cols // WIDTH
    per_slice = chunks // n_col
    z_size = n_row // GROUP
    dma = pltpu.SemaphoreType.DMA

    def exchange_scratch(rows, width):
        return [
            pltpu.VMEM((GROUP, rows, width), F32), pltpu.VMEM((GROUP, rows, width), F32),
            pltpu.VMEM((GROUP - 1, rows, width), F32), dma((GROUP - 1,)), dma((GROUP - 1,)),
            pltpu.VMEM((rows, width), F32),
            pltpu.VMEM((z_size, rows, width), F32), dma((z_size,)), dma((z_size,)),
            dma((GROUP,)), dma((GROUP,)),
        ]

    def gram_scratch():
        packed = (new // 2, 2 * new)
        return [
            ref
            for size in (2, GROUP // 2, z_size, n_col)
            for ref in (pltpu.VMEM(packed, F32), pltpu.VMEM((size,) + packed, F32), dma((size,)), dma((size,)))
        ]

    chunk = lambda *n: pltpu.VMEM(n + (part, WIDTH), F32)
    scratch = [
        pltpu.VMEM((SLOTS, mine, 2 * WIDTH), F32), dma((SLOTS,)), chunk(2, chunks), dma((2, chunks)),
        pltpu.VMEM((chunks, mine, WIDTH), BF16), pltpu.VMEM((chunks, mine, WIDTH), BF16),
        pltpu.VMEM((3 * new, mine), F32), pltpu.VMEM((2, 3 * part, mine), F32),
        pltpu.VMEM((2, 3 * part, mine), BF16), pltpu.VMEM((3 * new, 3 * new), F32),
        chunk(2, chunks), chunk(2, per_slice), dma((2, per_slice)),
    ]
    scratch += exchange_scratch(new // GROUP, mine) + exchange_scratch(8, part * mine // (8 * GROUP)) * 2
    scratch += gram_scratch() * 2
    ring = [dma((3 * per_slice,)), dma((3 * per_slice,))]
    scratch += ([chunk(per_slice)] * 3 + [chunk(3 * per_slice)] + ring) * 4 + ring * 4
    vmem = pl.BlockSpec(memory_space=pltpu.VMEM)
    hbm = pl.BlockSpec(memory_space=pl.ANY)
    projected, transform, factor = pl.pallas_call(
        functools.partial(fused, n_col, n_row, 1.0 / (cols * n_row)),
        out_shape=(
            jax.ShapeDtypeStruct((2, chunks, part, WIDTH), F32),
            jax.ShapeDtypeStruct((new, new), F32),
            jax.ShapeDtypeStruct((new, new), F32),
        ),
        in_specs=[hbm, hbm, vmem],
        out_specs=(hbm, vmem, vmem),
        scratch_shapes=scratch,
        compiler_params=pltpu.CompilerParams(
            collective_id=0, has_side_effects=True, vmem_limit_bytes=60 << 20
        ),
        name="project_and_factor",
    )(locked, vectors, mass.reshape(1, cols))
    block = 8
    appended = pl.pallas_call(
        apply_kernel,
        grid=(chunks // block,),
        out_shape=jax.ShapeDtypeStruct((new, cols), F32),
        in_specs=[
            pl.BlockSpec((new, new), lambda i: (0, 0)),
            pl.BlockSpec((2, block, part, WIDTH), lambda i: (0, i, 0, 0)),
        ],
        out_specs=pl.BlockSpec((new, block * WIDTH), lambda i: (0, i)),
        name="apply_factors",
    )(transform, projected)
    return (appended, factor)


def solution(mesh):
    return jax.shard_map(
        functools.partial(local, mesh.shape["col"], mesh.shape["row"]),
        mesh=mesh,
        in_specs=(P("col", "row"), P(None, "row"), P("row")),
        out_specs=(P(None, "row"), P()),
        check_vma=False,
    )
```

```python
import functools

import jax
import jax.numpy as jnp
from jax import lax
from jax.experimental import pallas as pl
from jax.experimental.pallas import tpu as pltpu
from jax.sharding import PartitionSpec as P

MESH = pl.DeviceIdType.MESH
F32 = jnp.float32
BF16 = jnp.bfloat16
HIGHEST = lax.Precision.HIGHEST
WIDTH = 1024
GROUP = 8
SLOTS = 4


def split2(x):
    high = x.astype(BF16)
    return high, (x - high.astype(F32)).astype(BF16)


def split3(x):
    high = x.astype(BF16)
    rest = x - high.astype(F32)
    middle = rest.astype(BF16)
    low = (rest - middle.astype(F32)).astype(BF16)
    return high, middle, low


def dot_nt(a, b):
    return lax.dot_general(a, b, (((1,), (1,)), ((), ())), preferred_element_type=F32)


def dot_nn(a, b):
    return lax.dot_general(a, b, (((1,), (0,)), ((), ())), preferred_element_type=F32)


def exchange_sum(scratch, row, z_size, hooks=()):
    (src, out, part, part_s, part_r, cred, cbuf, c_s, c_r, zred, zbuf, z_s, z_r, full_s, full_r) = scratch
    place = lax.rem(row, GROUP)
    base = row - place
    z = lax.div(row, GROUP)
    x, core = lax.div(place, 2), lax.rem(place, 2)
    x_size = GROUP // 2
    hooks = list(hooks) + [None] * (4 - len(hooks))

    copies = []
    for d in range(1, x_size):
        peer = lax.rem(x + d, x_size)
        copy = pltpu.make_async_remote_copy(
            src_ref=src.at[peer], dst_ref=part.at[d - 1], send_sem=part_s.at[d - 1], recv_sem=part_r.at[d - 1],
            device_id={"row": base + 2 * peer + core}, device_id_type=MESH,
        )
        copy.start()
        copies.append(copy)
    if hooks[0] is not None:
        hooks[0]()
    total = src[x]
    for d in range(1, x_size):
        copies[d - 1].wait_recv()
        total = total + part[d - 1]
    cred[...] = total
    zred[...] = peer_sum(cred, cbuf, c_s, c_r, core, [(1 - core, {"row": base + 2 * x + 1 - core})], hooks[1])
    peers = [lax.rem(z + d, z_size) for d in range(1, z_size)]
    devices = [(p, {"row": p * GROUP + place}) for p in peers]
    out[x] = peer_sum(zred, zbuf, z_s, z_r, z, devices, hooks[2])
    for d in range(1, x_size):
        peer = lax.rem(x + d, x_size)
        copy = pltpu.make_async_remote_copy(
            src_ref=out.at[x], dst_ref=out.at[x], send_sem=full_s.at[d - 1], recv_sem=full_r.at[x],
            device_id={"row": base + 2 * peer + core}, device_id_type=MESH,
        )
        copy.start()
        copies.append(copy)
    if hooks[3] is not None:
        hooks[3]()
    for d in range(1, x_size):
        peer = lax.rem(x + d, x_size)
        pltpu.make_async_remote_copy(
            src_ref=out.at[peer], dst_ref=out.at[peer], send_sem=full_s.at[d - 1], recv_sem=full_r.at[peer],
            device_id={"row": row}, device_id_type=MESH,
        ).wait_recv()
    for copy in copies:
        copy.wait_send()


def peer_copies(src, buf, sems, semr, mine, peers):
    return [
        (
            pltpu.make_async_remote_copy(
                src_ref=src, dst_ref=buf.at[mine], send_sem=sems.at[i], recv_sem=semr.at[mine],
                device_id=device, device_id_type=MESH,
            ),
            pltpu.make_async_remote_copy(
                src_ref=src, dst_ref=buf.at[peer], send_sem=sems.at[i], recv_sem=semr.at[peer],
                device_id=device, device_id_type=MESH,
            ),
        )
        for i, (peer, device) in enumerate(peers)
    ]


def peer_sum(src, buf, sems, semr, mine, peers, between=None):
    copies = peer_copies(src, buf, sems, semr, mine, peers)
    for out, _ in copies:
        out.start()
    buf[mine] = src[...]
    if between is not None:
        between()
    for _, arrival in copies:
        arrival.wait_recv()
    total = buf[0]
    for i in range(1, len(peers) + 1):
        total = total + buf[i]
    for out, _ in copies:
        out.wait_send()
    return total


def gram_sum(gram, scratch, row, col, n_col, z_size, first, last):
    half = gram.shape[0] // 2
    place = lax.rem(row, GROUP)
    base = row - place
    z = lax.div(row, GROUP)
    x, core = lax.div(place, 2), lax.rem(place, 2)
    x_size = GROUP // 2
    stages = [
        (2, core, lambda p: {"row": base + 2 * x + p}, first),
        (x_size, x, lambda p: {"row": base + 2 * p + core}, None),
        (z_size, z, lambda p: {"row": p * GROUP + place}, None),
        (n_col, col, lambda p: {"col": p}, last),
    ]
    total = jnp.concatenate([gram[:half], gram[half:]], axis=1)
    for i, (size, mine, device, between) in enumerate(stages):
        src, buf, sems, semr = scratch[4 * i : 4 * i + 4]
        src[...] = total
        peers = [lax.rem(mine + d, size) for d in range(1, size)]
        total = peer_sum(src, buf, sems, semr, mine, [(p, device(p)) for p in peers], between)
    new = gram.shape[0]
    return jnp.concatenate([total[:, :new], total[:, new:]], axis=0)


def factorize(gram):
    size = gram.shape[0]
    lane = lax.broadcasted_iota(jnp.int32, (size, 2 * size), 1)
    sub = lax.broadcasted_iota(jnp.int32, (size, 2 * size), 0)
    sub8 = lax.broadcasted_iota(jnp.int32, (8, 2 * size), 0)
    wide = jnp.concatenate([gram, jnp.zeros_like(gram)], axis=1)
    wide = jnp.where(lane < size, wide, jnp.where(lane - size == sub, 1.0, 0.0))
    blocks = [wide[8 * i : 8 * i + 8] for i in range(size // 8)]
    full = lambda x: jnp.broadcast_to(x, (8, 2 * size))
    for b in range(size // 8):
        j = 8 * b
        lines = [full(blocks[b][a : a + 1, :]) for a in range(8)]
        square = [[full(line[:, j + c : j + c + 1]) for c in range(8)] for line in lines]
        inverse = []
        for p in range(8):
            inverse.append(1.0 / square[p][p])
            for a in range(p + 1, 8):
                times = square[a][p] * inverse[p]
                lines[a] = lines[a] - times * lines[p]
                for c in range(p + 1, 8):
                    square[a][c] = square[a][c] - times * square[p][c]
        for i in range(b + 1, size // 8):
            column = [full(blocks[i][:, j + c : j + c + 1]) for c in range(8)]
            for p in range(8):
                times = column[p] * inverse[p]
                for q in range(p + 1, 8):
                    column[q] = column[q] - times * square[p][q]
                blocks[i] = blocks[i] - times * lines[p]
        for a in range(8):
            blocks[b] = jnp.where(sub8 == a, lines[a], blocks[b])
    body = jnp.concatenate(blocks, axis=0)
    pivots = jnp.sum(jnp.where(lane == sub, body, 0.0), axis=1, keepdims=True)
    body = body / jnp.sqrt(pivots)
    upper = jnp.where(lane >= sub, body, 0.0)[:, :size]
    return upper, body[:, size:]


def terms_of(matrix):
    a, b, c = split3(matrix)
    zero = jnp.zeros_like(a)
    return jnp.concatenate(
        [
            jnp.concatenate([a, a, a], axis=1),
            jnp.concatenate([b, b, zero], axis=1),
            jnp.concatenate([c, zero, zero], axis=1),
        ],
        axis=0,
    )


def apply_terms(terms, x):
    new = x.shape[0]
    r = dot_nn(terms, jnp.concatenate(split3(x), axis=0))
    return r[:new] + (r[new : 2 * new] + r[2 * new :])


def fused(
    n_col, n_row, scale,
    l_hbm, v_hbm, m_ref, p_hbm, t_ref, f_ref,
    lbuf, lsem, vc, vsem, l1, l2, acc, acc2, wsp, ggram, zf, po, psem,
    *rest,
):
    sums = [rest[15 * i : 15 * i + 15] for i in range(3)]
    grams = [rest[45 + 16 * i : 61 + 16 * i] for i in range(2)]
    scatters = [rest[77 + 6 * i : 83 + 6 * i] for i in range(4)]
    gathers = [rest[101 + 2 * i : 103 + 2 * i] for i in range(4)]
    col, row = lax.axis_index("col"), lax.axis_index("row")
    right, left = lax.rem(col + 1, n_col), lax.rem(col + n_col - 1, n_col)
    across = lax.rem(col + 2, n_col)
    z_size = n_row // GROUP
    place = lax.rem(row, GROUP)
    base = row - place
    z = lax.div(row, GROUP)
    chunks, part = vc.shape[1], vc.shape[2]
    per_slice = chunks // n_col
    half = per_slice // 2
    new = 2 * part

    def columns(ch):
        return pl.ds(pl.multiple_of(ch * WIDTH, WIDTH), WIDTH)

    def load_l(ch, slot):
        pair = pl.ds(pl.multiple_of(ch * 2 * WIDTH, 2 * WIDTH), 2 * WIDTH)
        return pltpu.make_async_copy(l_hbm.at[:, pair], lbuf.at[slot], lsem.at[slot])

    def load_v(h, ch):
        return pltpu.make_async_copy(
            v_hbm.at[h * part : (h + 1) * part, columns(ch)], vc.at[h, ch], vsem.at[h, ch]
        )

    def load(pair, slot):
        for i in range(2):
            for h in range(2):
                load_v(h, 2 * pair + i).start()
        load_l(pair, slot).start()

    for pair in range(SLOTS):
        load(pair, pair)

    barrier = pltpu.get_barrier_semaphore()
    for d in range(1, GROUP):
        pl.semaphore_signal(barrier, inc=1, device_id={"row": base + lax.rem(place + d, GROUP)}, device_id_type=MESH)
    for d in range(1, z_size):
        pl.semaphore_signal(
            barrier, inc=1, device_id={"row": lax.rem(z + d, z_size) * GROUP + place}, device_id_type=MESH
        )
    for d in range(1, n_col):
        pl.semaphore_signal(barrier, inc=1, device_id={"col": lax.rem(col + d, n_col)}, device_id_type=MESH)

    def collect(total):
        n = total.shape[0] // 3
        return (total[0:n] + (total[n : 2 * n] + total[2 * n :])) * scale

    acc[...] = jnp.zeros_like(acc)
    acc2[...] = jnp.zeros_like(acc2)

    def first_step(pair, carry):
        slot = lax.rem(pair, SLOTS)
        load_l(pair, slot).wait()
        high, low = split2(lbuf[slot])
        x = []
        for i in range(2):
            ch = 2 * pair + i
            l1[ch] = high[:, i * WIDTH : (i + 1) * WIDTH]
            l2[ch] = low[:, i * WIDTH : (i + 1) * WIDTH]
            load_v(0, ch).wait()
            load_v(1, ch).wait()
            x.append(jnp.concatenate([vc[0, ch], vc[1, ch]], axis=0) * m_ref[:, columns(ch)])
        a = jnp.concatenate(split3(jnp.concatenate(x, axis=1)), axis=0)
        acc[...] += dot_nt(a, high)
        acc[0 : 2 * new] += dot_nt(a[0 : 2 * new], low)

        @pl.when(pair + SLOTS < chunks // 2)
        def _():
            load(pair + SLOTS, slot)

        return carry

    lax.fori_loop(0, chunks // 2, first_step, 0)
    first = collect(acc[...])
    src = sums[0][0]
    parts = src.shape[0]
    for i in range(parts):
        src[i] = first[i * new // parts : (i + 1) * new // parts]
    pl.semaphore_wait(barrier, (GROUP - 1) + (z_size - 1) + (n_col - 1))
    exchange_sum(sums[0], row, z_size)
    out = sums[0][1]
    b1 = [jnp.concatenate([out[parts // 2 * h + i] for i in range(parts // 2)], axis=0) for h in range(2)]

    def set_weights(h, b):
        for i, w in enumerate(split3(b)):
            wsp[h, i * part : (i + 1) * part] = w

    def term(h, ch):
        r = dot_nn(wsp[h], l1[ch])
        s = dot_nn(wsp[h, 0 : 2 * part], l2[ch])
        return r[0:part] + ((r[part : 2 * part] + s[0:part]) + (r[2 * part :] + s[part:]))

    def send(src, dst, sems, semr, index, where):
        return pltpu.make_async_remote_copy(
            src_ref=src, dst_ref=dst, send_sem=sems.at[index], recv_sem=semr.at[index],
            device_id={"col": where}, device_id_type=MESH,
        )

    def far(c, k, where):
        d2, fl, fr, stage, ss, sr = scatters[c]
        return send(stage.at[k], d2.at[k], ss, sr, k, where)

    def to_right(c, k):
        d2, fl, fr, stage, ss, sr = scatters[c]
        return send(stage.at[per_slice + k], fl.at[k], ss, sr, per_slice + k, right)

    def to_left(c, k):
        d2, fl, fr, stage, ss, sr = scatters[c]
        return send(stage.at[2 * per_slice + k], fr.at[k], ss, sr, 2 * per_slice + k, left)

    def loop(count, body):
        def step(j, carry):
            body(j)
            return carry

        lax.fori_loop(0, count, step, 0)

    def scatter_start(c):
        h, stage = c % 2, scatters[c][3]

        def far_step(j):
            stage[j] = term(h, across * per_slice + j)
            far(c, j, right).start()
            stage[half + j] = term(h, across * per_slice + half + j)
            far(c, half + j, left).start()

        def pure_step(j):
            stage[per_slice + half + j] = term(h, right * per_slice + half + j)
            to_right(c, half + j).start()
            stage[2 * per_slice + j] = term(h, left * per_slice + j)
            to_left(c, j).start()

        loop(half, far_step)
        loop(half, pure_step)

    def scatter_added(c):
        h, d2, stage = c % 2, scatters[c][0], scatters[c][3]

        def added_step(j):
            own = term(h, right * per_slice + j)
            far(c, j, right).wait_recv()
            stage[per_slice + j] = own + d2[j]
            to_right(c, j).start()
            own = term(h, left * per_slice + half + j)
            far(c, half + j, left).wait_recv()
            stage[2 * per_slice + half + j] = own + d2[half + j]
            to_left(c, half + j).start()

        loop(half, added_step)

    def scatter_own(c, finish, done):
        h, fl, fr = c % 2, scatters[c][1], scatters[c][2]

        def own_step(j):
            for k in (j, half + j):
                own = term(h, col * per_slice + k)
                to_left(c, k).wait_recv()
                to_right(c, k).wait_recv()
                finish(k, own + (fl[k] + fr[k]))
            done(j)

        loop(half, own_step)

    def targets(g):
        return (zf if g < 2 else p_hbm).at[g % 2]

    def give_right(g, src, k, sl):
        return send(src, targets(g).at[sl * per_slice + k], *gathers[g], k, right)

    def give_left(g, src, k, sl):
        return send(src, targets(g).at[sl * per_slice + k], *gathers[g], per_slice + k, left)

    def hand_on(g, k, sl, where):
        at = targets(g).at[sl * per_slice + k]
        return send(at, at, *gathers[g], 2 * per_slice + k, where)

    def relay(g, j, use):
        give_right(g, targets(g).at[left * per_slice + j], j, left).wait_recv()
        hand_on(g, j, left, right).start()
        give_left(g, targets(g).at[right * per_slice + half + j], half + j, right).wait_recv()
        hand_on(g, half + j, right, left).start()
        use(left * per_slice + j)
        use(right * per_slice + half + j)

    def give_first(g, j, src):
        give_right(g, src.at[j], j, col).start()
        give_left(g, src.at[half + j], half + j, col).start()

    def give_last(g, j, src):
        give_left(g, src.at[j], j, col).start()
        give_right(g, src.at[half + j], half + j, col).start()

    def gather_near(g, use):
        def near_step(j):
            give_right(g, targets(g).at[left * per_slice + half + j], half + j, left).wait_recv()
            give_left(g, targets(g).at[right * per_slice + j], j, right).wait_recv()
            use(left * per_slice + half + j)
            use(right * per_slice + j)

        loop(half, near_step)

    def gather_far(g, use):
        def far_step(j):
            for k in (j, half + j):
                hand_on(g, k, across, right).wait_recv()
            for k in (j, half + j):
                use(across * per_slice + k)

        loop(half, far_step)

    def use_once(h):
        def use(ch):
            x = (vc[h, ch] - zf[h, ch]) * m_ref[:, columns(ch)]
            a = jnp.concatenate(split3(x), axis=0)
            acc2[h] += dot_nt(a, l1[ch])
            acc2[h, 0 : 2 * part] += dot_nt(a[0 : 2 * part], l2[ch])

        return use

    def own_first(h):
        mine = zf.at[h, pl.ds(col * per_slice, per_slice)]

        def finish(k, value):
            zf[h, col * per_slice + k] = value

        scatter_own(h, finish, lambda j: give_first(h, j, mine))
        loop(half, lambda j: give_last(h, j, mine))
        loop(per_slice, lambda k: use_once(h)(col * per_slice + k))

    def second_sum(h, hooks):
        second = collect(acc2[h])
        src, out = sums[1 + h][0], sums[1 + h][1]
        for i in range(parts):
            src[i] = second[i * part // parts : (i + 1) * part // parts]
        exchange_sum(sums[1 + h], row, z_size, hooks)
        set_weights(h, b1[h] + jnp.concatenate([out[i] for i in range(parts)], axis=0))

    set_weights(0, b1[0])
    set_weights(1, b1[1])
    scatter_start(0)
    scatter_added(0)
    scatter_start(1)
    own_first(0)
    scatter_added(1)
    loop(half, lambda j: relay(0, j, use_once(0)))
    own_first(1)
    gather_near(0, use_once(0))
    gather_far(0, use_once(0))
    relays = [lambda j=j: relay(1, j, use_once(1)) for j in range(half)]
    second_sum(0, [relays[0], None, relays[1], lambda: gather_near(1, use_once(1))])
    scatter_start(2)
    gather_far(1, use_once(1))
    second_sum(1, [None, None, lambda: scatter_added(2)])
    scatter_start(3)

    ggram[...] = jnp.zeros_like(ggram)

    def add_gram(p, ch):
        a = jnp.concatenate(split3(p * m_ref[:, columns(ch)]), axis=0)
        b = jnp.concatenate(split3(p), axis=0)
        ggram[...] += dot_nt(a, b)

    def collect_gram():
        g = ggram[...]
        rows3 = g[0:new] + (g[new : 2 * new] + g[2 * new :])
        gram = rows3[:, 0:new] + (rows3[:, new : 2 * new] + rows3[:, 2 * new :])
        return gram * scale

    def keep(h, k):
        return pltpu.make_async_copy(po.at[h, k], p_hbm.at[h, col * per_slice + k], psem.at[h, k])

    def both(k):
        return jnp.concatenate([po[0, k], po[1, k]], axis=0)

    def finish_second(h):
        def finish(k, value):
            ch = col * per_slice + k
            po[h, k] = vc[h, ch] - value
            keep(h, k).start()
            if h == 1:
                add_gram(both(k), ch)

        return finish

    nothing = lambda ch: None
    scatter_own(2, finish_second(0), nothing)
    scatter_added(3)

    def give_all(h):
        loop(half, lambda j: give_first(2 + h, j, po.at[h]))
        loop(half, lambda j: give_last(2 + h, j, po.at[h]))

    def hand_all(h):
        loop(half, lambda j: relay(2 + h, j, nothing))

    give_all(0)
    scatter_own(3, finish_second(1), nothing)
    gram = gram_sum(collect_gram(), grams[0], row, col, n_col, z_size, None, lambda: give_all(1))
    upper_one, inverse_one = factorize(gram)

    ggram[...] = jnp.zeros_like(ggram)
    weights = terms_of(inverse_one)
    loop(per_slice, lambda k: add_gram(apply_terms(weights, both(k)), col * per_slice + k))
    gram = gram_sum(collect_gram(), grams[1], row, col, n_col, z_size, lambda: hand_all(0), lambda: hand_all(1))
    upper_two, inverse_two = factorize(gram)
    f_ref[...] = jnp.dot(upper_two, upper_one, precision=HIGHEST, preferred_element_type=F32)
    t_ref[...] = terms_of(jnp.dot(inverse_two, inverse_one, precision=HIGHEST, preferred_element_type=F32))

    for h in range(2):
        gather_near(2 + h, nothing)
        gather_far(2 + h, nothing)

    def sent_step(k):
        for h in range(2):
            keep(h, k).wait()
        for c in range(4):
            far(c, k, right).wait_send()
            to_right(c, k).wait_send()
            to_left(c, k).wait_send()
        for g in range(4):
            at = targets(g).at[col * per_slice + k]
            give_right(g, at, k, col).wait_send()
            give_left(g, at, k, col).wait_send()
            hand_on(g, k, col, right).wait_send()

    loop(per_slice, sent_step)


def apply_kernel(t_ref, p_ref, f_ref, o_ref, fo_ref):
    fo_ref[...] = f_ref[...]
    weights = t_ref[...]
    for i in range(p_ref.shape[1]):
        p = jnp.concatenate([p_ref[0, i], p_ref[1, i]], axis=0)
        o_ref[:, i * WIDTH : (i + 1) * WIDTH] = apply_terms(weights, p)


def local(n_col, n_row, locked, vectors, mass):
    mine, cols = locked.shape
    new = vectors.shape[0]
    part = new // 2
    chunks = cols // WIDTH
    per_slice = chunks // n_col
    z_size = n_row // GROUP
    dma = pltpu.SemaphoreType.DMA

    def exchange_scratch(rows):
        many = lambda n: pltpu.VMEM((n, rows, mine), F32)
        one = pltpu.VMEM((rows, mine), F32)
        x_size = GROUP // 2
        return [
            many(x_size), many(x_size), many(x_size - 1), dma((x_size - 1,)), dma((x_size - 1,)),
            one, many(2), dma((2,)), dma((2,)),
            one, many(z_size), dma((z_size,)), dma((z_size,)),
            dma((x_size,)), dma((x_size,)),
        ]

    def gram_scratch():
        packed = (new // 2, 2 * new)
        return [
            ref
            for size in (2, GROUP // 2, z_size, n_col)
            for ref in (pltpu.VMEM(packed, F32), pltpu.VMEM((size,) + packed, F32), dma((size,)), dma((size,)))
        ]

    chunk = lambda *n: pltpu.VMEM(n + (part, WIDTH), F32)
    scratch = [
        pltpu.VMEM((SLOTS, mine, 2 * WIDTH), F32), dma((SLOTS,)), chunk(2, chunks), dma((2, chunks)),
        pltpu.VMEM((chunks, mine, WIDTH), BF16), pltpu.VMEM((chunks, mine, WIDTH), BF16),
        pltpu.VMEM((3 * new, mine), F32), pltpu.VMEM((2, 3 * part, mine), F32),
        pltpu.VMEM((2, 3 * part, mine), BF16), pltpu.VMEM((3 * new, 3 * new), F32),
        chunk(2, chunks), chunk(2, per_slice), dma((2, per_slice)),
    ]
    scratch += exchange_scratch(2 * new // GROUP) + exchange_scratch(2 * part // GROUP) * 2
    scratch += gram_scratch() * 2
    ring = [dma((3 * per_slice,)), dma((3 * per_slice,))]
    scratch += ([chunk(per_slice)] * 3 + [chunk(3 * per_slice)] + ring) * 4 + ring * 4
    vmem = pl.BlockSpec(memory_space=pltpu.VMEM)
    hbm = pl.BlockSpec(memory_space=pl.ANY)
    projected, transform, factor = pl.pallas_call(
        functools.partial(fused, n_col, n_row, 1.0 / (cols * n_row)),
        out_shape=(
            jax.ShapeDtypeStruct((2, chunks, part, WIDTH), F32),
            jax.ShapeDtypeStruct((3 * new, 3 * new), BF16),
            jax.ShapeDtypeStruct((new, new), F32),
        ),
        in_specs=[hbm, hbm, vmem],
        out_specs=(hbm, vmem, vmem),
        scratch_shapes=scratch,
        compiler_params=pltpu.CompilerParams(
            collective_id=0, has_side_effects=True, vmem_limit_bytes=60 << 20
        ),
        name="project_and_factor",
    )(locked, vectors, mass.reshape(1, cols))
    block = 8
    still = lambda n: pl.BlockSpec((n, n), lambda i: (0, 0))
    return tuple(
        pl.pallas_call(
            apply_kernel,
            grid=(chunks // block,),
            out_shape=(jax.ShapeDtypeStruct((new, cols), F32), jax.ShapeDtypeStruct((new, new), F32)),
            in_specs=[
                still(3 * new),
                pl.BlockSpec((2, block, part, WIDTH), lambda i: (0, i, 0, 0)),
                still(new),
            ],
            out_specs=(pl.BlockSpec((new, block * WIDTH), lambda i: (0, i)), still(new)),
            name="apply_factors",
        )(transform, projected, factor)
    )


def solution(mesh):
    return jax.shard_map(
        functools.partial(local, mesh.shape["col"], mesh.shape["row"]),
        mesh=mesh,
        in_specs=(P("col", "row"), P(None, "row"), P("row")),
        out_specs=(P(None, "row"), P()),
        check_vma=False,
    )
```

```python
import functools

import jax
import jax.numpy as jnp
from jax import lax
from jax.experimental import pallas as pl
from jax.experimental.pallas import tpu as pltpu
from jax.sharding import PartitionSpec as P

MESH = pl.DeviceIdType.MESH
F32 = jnp.float32
BF16 = jnp.bfloat16
HIGHEST = lax.Precision.HIGHEST
WIDTH = 1024
GROUP = 8
SLOTS = 4


def split2(x):
    high = x.astype(BF16)
    return high, (x - high.astype(F32)).astype(BF16)


def split3(x):
    high = x.astype(BF16)
    rest = x - high.astype(F32)
    middle = rest.astype(BF16)
    low = (rest - middle.astype(F32)).astype(BF16)
    return high, middle, low


def dot_nt(a, b):
    return lax.dot_general(a, b, (((1,), (1,)), ((), ())), preferred_element_type=F32)


def dot_nn(a, b):
    return lax.dot_general(a, b, (((1,), (0,)), ((), ())), preferred_element_type=F32)


def exchange_sum(scratch, row, z_size, sent, hooks=()):
    (src, out, part, part_s, part_r, cred, cbuf, c_s, c_r, zred, zbuf, z_s, z_r, full_s, full_r) = scratch
    place = lax.rem(row, GROUP)
    base = row - place
    z = lax.div(row, GROUP)
    x, core = lax.div(place, 2), lax.rem(place, 2)
    x_size = GROUP // 2
    hooks = list(hooks) + [None] * (4 - len(hooks))

    copies = []
    for d in range(1, x_size):
        peer = lax.rem(x + d, x_size)
        copy = pltpu.make_async_remote_copy(
            src_ref=src.at[peer], dst_ref=part.at[d - 1], send_sem=part_s.at[d - 1], recv_sem=part_r.at[d - 1],
            device_id={"row": base + 2 * peer + core}, device_id_type=MESH,
        )
        copy.start()
        copies.append(copy)
    if hooks[0] is not None:
        hooks[0]()
    total = src[x]
    for d in range(1, x_size):
        copies[d - 1].wait_recv()
        total = total + part[d - 1]
    cred[...] = total
    other = [(1 - core, {"row": base + 2 * x + 1 - core})]
    zred[...] = peer_sum(cred, cbuf, c_s, c_r, core, other, sent, hooks[1])
    peers = [lax.rem(z + d, z_size) for d in range(1, z_size)]
    devices = [(p, {"row": p * GROUP + place}) for p in peers]
    out[x] = peer_sum(zred, zbuf, z_s, z_r, z, devices, sent, hooks[2])
    for d in range(1, x_size):
        peer = lax.rem(x + d, x_size)
        copy = pltpu.make_async_remote_copy(
            src_ref=out.at[x], dst_ref=out.at[x], send_sem=full_s.at[d - 1], recv_sem=full_r.at[x],
            device_id={"row": base + 2 * peer + core}, device_id_type=MESH,
        )
        copy.start()
        copies.append(copy)
    if hooks[3] is not None:
        hooks[3]()
    for d in range(1, x_size):
        peer = lax.rem(x + d, x_size)
        pltpu.make_async_remote_copy(
            src_ref=out.at[peer], dst_ref=out.at[peer], send_sem=full_s.at[d - 1], recv_sem=full_r.at[peer],
            device_id={"row": row}, device_id_type=MESH,
        ).wait_recv()
    sent += copies


def peer_copies(src, buf, sems, semr, mine, peers):
    return [
        (
            pltpu.make_async_remote_copy(
                src_ref=src, dst_ref=buf.at[mine], send_sem=sems.at[i], recv_sem=semr.at[mine],
                device_id=device, device_id_type=MESH,
            ),
            pltpu.make_async_remote_copy(
                src_ref=src, dst_ref=buf.at[peer], send_sem=sems.at[i], recv_sem=semr.at[peer],
                device_id=device, device_id_type=MESH,
            ),
        )
        for i, (peer, device) in enumerate(peers)
    ]


def peer_sum(src, buf, sems, semr, mine, peers, sent, between=None):
    copies = peer_copies(src, buf, sems, semr, mine, peers)
    for out, _ in copies:
        out.start()
    buf[mine] = src[...]
    if between is not None:
        between()
    for _, arrival in copies:
        arrival.wait_recv()
    total = buf[0]
    for i in range(1, len(peers) + 1):
        total = total + buf[i]
    sent += [out for out, _ in copies]
    return total


def gram_sum(gram, scratch, row, col, n_col, z_size, sent, first, last):
    half = gram.shape[0] // 2
    place = lax.rem(row, GROUP)
    base = row - place
    z = lax.div(row, GROUP)
    x, core = lax.div(place, 2), lax.rem(place, 2)
    x_size = GROUP // 2
    stages = [
        (2, core, lambda p: {"row": base + 2 * x + p}, first),
        (x_size, x, lambda p: {"row": base + 2 * p + core}, None),
        (z_size, z, lambda p: {"row": p * GROUP + place}, None),
        (n_col, col, lambda p: {"col": p}, last),
    ]
    total = jnp.concatenate([gram[:half], gram[half:]], axis=1)
    for i, (size, mine, device, between) in enumerate(stages):
        src, buf, sems, semr = scratch[4 * i : 4 * i + 4]
        src[...] = total
        peers = [lax.rem(mine + d, size) for d in range(1, size)]
        total = peer_sum(src, buf, sems, semr, mine, [(p, device(p)) for p in peers], sent, between)
    new = gram.shape[0]
    return jnp.concatenate([total[:, :new], total[:, new:]], axis=0)


def factorize(gram):
    size = gram.shape[0]
    lane = lax.broadcasted_iota(jnp.int32, (size, 2 * size), 1)
    sub = lax.broadcasted_iota(jnp.int32, (size, 2 * size), 0)
    sub8 = lax.broadcasted_iota(jnp.int32, (8, 2 * size), 0)
    wide = jnp.concatenate([gram, jnp.zeros_like(gram)], axis=1)
    wide = jnp.where(lane < size, wide, jnp.where(lane - size == sub, 1.0, 0.0))
    blocks = [wide[8 * i : 8 * i + 8] for i in range(size // 8)]
    full = lambda x: jnp.broadcast_to(x, (8, 2 * size))
    for b in range(size // 8):
        j = 8 * b
        lines = [full(blocks[b][a : a + 1, :]) for a in range(8)]
        square = [[full(line[:, j + c : j + c + 1]) for c in range(8)] for line in lines]
        inverse = []
        for p in range(8):
            inverse.append(1.0 / square[p][p])
            for a in range(p + 1, 8):
                times = square[a][p] * inverse[p]
                lines[a] = lines[a] - times * lines[p]
                for c in range(p + 1, 8):
                    square[a][c] = square[a][c] - times * square[p][c]
        for i in range(b + 1, size // 8):
            column = [full(blocks[i][:, j + c : j + c + 1]) for c in range(8)]
            for p in range(8):
                times = column[p] * inverse[p]
                for q in range(p + 1, 8):
                    column[q] = column[q] - times * square[p][q]
                blocks[i] = blocks[i] - times * lines[p]
        for a in range(8):
            blocks[b] = jnp.where(sub8 == a, lines[a], blocks[b])
    body = jnp.concatenate(blocks, axis=0)
    pivots = jnp.sum(jnp.where(lane == sub, body, 0.0), axis=1, keepdims=True)
    body = body / jnp.sqrt(pivots)
    upper = jnp.where(lane >= sub, body, 0.0)[:, :size]
    return upper, body[:, size:]


def terms_of(matrix):
    a, b, c = split3(matrix)
    zero = jnp.zeros_like(a)
    return jnp.concatenate(
        [
            jnp.concatenate([a, a, a], axis=1),
            jnp.concatenate([b, b, zero], axis=1),
            jnp.concatenate([c, zero, zero], axis=1),
        ],
        axis=0,
    )


def apply_terms(terms, x):
    new = x.shape[0]
    r = dot_nn(terms, jnp.concatenate(split3(x), axis=0))
    return r[:new] + (r[new : 2 * new] + r[2 * new :])


def fused(
    n_col, n_row, scale,
    l_hbm, v_hbm, m_ref, p_hbm, t_ref, f_ref,
    lbuf, lsem, vc, vsem, l1, l2, acc, acc2, wsp, ggram, zf, po, psem,
    *rest,
):
    sums = [rest[15 * i : 15 * i + 15] for i in range(3)]
    grams = [rest[45 + 16 * i : 61 + 16 * i] for i in range(2)]
    scatters = [rest[77 + 6 * i : 83 + 6 * i] for i in range(4)]
    gathers = [rest[101 + 2 * i : 103 + 2 * i] for i in range(4)]
    col, row = lax.axis_index("col"), lax.axis_index("row")
    right, left = lax.rem(col + 1, n_col), lax.rem(col + n_col - 1, n_col)
    across = lax.rem(col + 2, n_col)
    z_size = n_row // GROUP
    place = lax.rem(row, GROUP)
    base = row - place
    z = lax.div(row, GROUP)
    chunks, part = vc.shape[1], vc.shape[2]
    per_slice = chunks // n_col
    half = per_slice // 2
    new = 2 * part

    def columns(ch):
        return pl.ds(pl.multiple_of(ch * WIDTH, WIDTH), WIDTH)

    def load_l(ch, slot):
        pair = pl.ds(pl.multiple_of(ch * 2 * WIDTH, 2 * WIDTH), 2 * WIDTH)
        return pltpu.make_async_copy(l_hbm.at[:, pair], lbuf.at[slot], lsem.at[slot])

    def load_v(h, ch):
        return pltpu.make_async_copy(
            v_hbm.at[h * part : (h + 1) * part, columns(ch)], vc.at[h, ch], vsem.at[h, ch]
        )

    def load(pair, slot):
        for i in range(2):
            for h in range(2):
                load_v(h, 2 * pair + i).start()
        load_l(pair, slot).start()

    for pair in range(SLOTS):
        load(pair, pair)

    barrier = pltpu.get_barrier_semaphore()
    for d in range(1, GROUP):
        pl.semaphore_signal(barrier, inc=1, device_id={"row": base + lax.rem(place + d, GROUP)}, device_id_type=MESH)
    for d in range(1, z_size):
        pl.semaphore_signal(
            barrier, inc=1, device_id={"row": lax.rem(z + d, z_size) * GROUP + place}, device_id_type=MESH
        )
    for d in range(1, n_col):
        pl.semaphore_signal(barrier, inc=1, device_id={"col": lax.rem(col + d, n_col)}, device_id_type=MESH)

    def collect(total):
        n = total.shape[0] // 3
        return (total[0:n] + (total[n : 2 * n] + total[2 * n :])) * scale

    acc[...] = jnp.zeros_like(acc)
    acc2[...] = jnp.zeros_like(acc2)

    def first_step(pair, carry):
        slot = lax.rem(pair, SLOTS)
        load_l(pair, slot).wait()
        high, low = split2(lbuf[slot])
        x = []
        for i in range(2):
            ch = 2 * pair + i
            l1[ch] = high[:, i * WIDTH : (i + 1) * WIDTH]
            l2[ch] = low[:, i * WIDTH : (i + 1) * WIDTH]
            load_v(0, ch).wait()
            load_v(1, ch).wait()
            x.append(jnp.concatenate([vc[0, ch], vc[1, ch]], axis=0) * m_ref[:, columns(ch)])
        a = jnp.concatenate(split3(jnp.concatenate(x, axis=1)), axis=0)
        acc[...] += dot_nt(a, high)
        acc[0 : 2 * new] += dot_nt(a[0 : 2 * new], low)

        @pl.when(pair + SLOTS < chunks // 2)
        def _():
            load(pair + SLOTS, slot)

        return carry

    lax.fori_loop(0, chunks // 2, first_step, 0)
    first = collect(acc[...])
    src = sums[0][0]
    parts = src.shape[0]
    for i in range(parts):
        src[i] = first[i * new // parts : (i + 1) * new // parts]
    pl.semaphore_wait(barrier, (GROUP - 1) + (z_size - 1) + (n_col - 1))
    sent = []
    exchange_sum(sums[0], row, z_size, sent)
    out = sums[0][1]
    b1 = [jnp.concatenate([out[parts // 2 * h + i] for i in range(parts // 2)], axis=0) for h in range(2)]

    def set_weights(h, b):
        for i, w in enumerate(split3(b)):
            wsp[h, i * part : (i + 1) * part] = w

    def term(h, ch):
        r = dot_nn(wsp[h], l1[ch])
        s = dot_nn(wsp[h, 0 : 2 * part], l2[ch])
        return r[0:part] + ((r[part : 2 * part] + s[0:part]) + (r[2 * part :] + s[part:]))

    def send(src, dst, sems, semr, index, where):
        return pltpu.make_async_remote_copy(
            src_ref=src, dst_ref=dst, send_sem=sems.at[index], recv_sem=semr.at[index],
            device_id={"col": where}, device_id_type=MESH,
        )

    def far(c, k, where):
        d2, fl, fr, stage, ss, sr = scatters[c]
        return send(stage.at[k], d2.at[k], ss, sr, k, where)

    def to_right(c, k):
        d2, fl, fr, stage, ss, sr = scatters[c]
        return send(stage.at[per_slice + k], fl.at[k], ss, sr, per_slice + k, right)

    def to_left(c, k):
        d2, fl, fr, stage, ss, sr = scatters[c]
        return send(stage.at[2 * per_slice + k], fr.at[k], ss, sr, 2 * per_slice + k, left)

    def loop(count, body):
        def step(j, carry):
            body(j)
            return carry

        lax.fori_loop(0, count, step, 0)

    def scatter_start(c):
        h, stage = c % 2, scatters[c][3]

        def far_step(j):
            stage[j] = term(h, across * per_slice + j)
            far(c, j, right).start()
            stage[half + j] = term(h, across * per_slice + half + j)
            far(c, half + j, left).start()

        def pure_step(j):
            stage[per_slice + half + j] = term(h, right * per_slice + half + j)
            to_right(c, half + j).start()
            stage[2 * per_slice + j] = term(h, left * per_slice + j)
            to_left(c, j).start()

        loop(half, far_step)
        loop(half, pure_step)

    def scatter_added(c):
        h, d2, stage = c % 2, scatters[c][0], scatters[c][3]

        def added_step(j):
            own = term(h, right * per_slice + j)
            far(c, j, right).wait_recv()
            stage[per_slice + j] = own + d2[j]
            to_right(c, j).start()
            own = term(h, left * per_slice + half + j)
            far(c, half + j, left).wait_recv()
            stage[2 * per_slice + half + j] = own + d2[half + j]
            to_left(c, half + j).start()

        loop(half, added_step)

    def scatter_own(c, finish, done):
        h, fl, fr = c % 2, scatters[c][1], scatters[c][2]

        def own_step(j):
            for k in (j, half + j):
                own = term(h, col * per_slice + k)
                to_left(c, k).wait_recv()
                to_right(c, k).wait_recv()
                finish(k, own + (fl[k] + fr[k]))
            done(j)

        loop(half, own_step)

    def targets(g):
        return (zf if g < 2 else p_hbm).at[g % 2]

    def give_right(g, src, k, sl):
        return send(src, targets(g).at[sl * per_slice + k], *gathers[g], k, right)

    def give_left(g, src, k, sl):
        return send(src, targets(g).at[sl * per_slice + k], *gathers[g], per_slice + k, left)

    def hand_on(g, k, sl, where):
        at = targets(g).at[sl * per_slice + k]
        return send(at, at, *gathers[g], 2 * per_slice + k, where)

    def relay(g, j, use):
        give_right(g, targets(g).at[left * per_slice + j], j, left).wait_recv()
        hand_on(g, j, left, right).start()
        give_left(g, targets(g).at[right * per_slice + half + j], half + j, right).wait_recv()
        hand_on(g, half + j, right, left).start()
        use(left * per_slice + j)
        use(right * per_slice + half + j)

    def give_first(g, j, src):
        give_right(g, src.at[j], j, col).start()
        give_left(g, src.at[half + j], half + j, col).start()

    def give_last(g, j, src):
        give_left(g, src.at[j], j, col).start()
        give_right(g, src.at[half + j], half + j, col).start()

    def gather_near(g, use):
        def near_step(j):
            give_right(g, targets(g).at[left * per_slice + half + j], half + j, left).wait_recv()
            give_left(g, targets(g).at[right * per_slice + j], j, right).wait_recv()
            use(left * per_slice + half + j)
            use(right * per_slice + j)

        loop(half, near_step)

    def gather_far(g, use):
        def far_step(j):
            for k in (j, half + j):
                hand_on(g, k, across, right).wait_recv()
            for k in (j, half + j):
                use(across * per_slice + k)

        loop(half, far_step)

    def use_once(h):
        def use(ch):
            x = (vc[h, ch] - zf[h, ch]) * m_ref[:, columns(ch)]
            a = jnp.concatenate(split3(x), axis=0)
            acc2[h] += dot_nt(a, l1[ch])
            acc2[h, 0 : 2 * part] += dot_nt(a[0 : 2 * part], l2[ch])

        return use

    def own_first(h):
        mine = zf.at[h, pl.ds(col * per_slice, per_slice)]

        def finish(k, value):
            zf[h, col * per_slice + k] = value

        scatter_own(h, finish, lambda j: give_first(h, j, mine))
        loop(half, lambda j: give_last(h, j, mine))
        loop(per_slice, lambda k: use_once(h)(col * per_slice + k))

    def second_sum(h, hooks):
        second = collect(acc2[h])
        src, out = sums[1 + h][0], sums[1 + h][1]
        for i in range(parts):
            src[i] = second[i * part // parts : (i + 1) * part // parts]
        exchange_sum(sums[1 + h], row, z_size, sent, hooks)
        set_weights(h, b1[h] + jnp.concatenate([out[i] for i in range(parts)], axis=0))

    set_weights(0, b1[0])
    scatter_start(0)
    set_weights(1, b1[1])
    scatter_added(0)
    scatter_start(1)
    own_first(0)
    scatter_added(1)
    loop(half, lambda j: relay(0, j, use_once(0)))
    own_first(1)
    gather_near(0, use_once(0))
    gather_far(0, use_once(0))
    relays = [lambda j=j: relay(1, j, use_once(1)) for j in range(half)]
    second_sum(0, [relays[0], None, relays[1], lambda: gather_near(1, use_once(1))])
    scatter_start(2)
    gather_far(1, use_once(1))
    second_sum(1, [None, None, lambda: scatter_added(2)])
    scatter_start(3)

    ggram[...] = jnp.zeros_like(ggram)

    def add_gram(p, ch):
        a = jnp.concatenate(split3(p * m_ref[:, columns(ch)]), axis=0)
        b = jnp.concatenate(split3(p), axis=0)
        ggram[...] += dot_nt(a, b)

    def collect_gram():
        g = ggram[...]
        rows3 = g[0:new] + (g[new : 2 * new] + g[2 * new :])
        gram = rows3[:, 0:new] + (rows3[:, new : 2 * new] + rows3[:, 2 * new :])
        return gram * scale

    def keep(h, k):
        return pltpu.make_async_copy(po.at[h, k], p_hbm.at[h, col * per_slice + k], psem.at[h, k])

    def both(k):
        return jnp.concatenate([po[0, k], po[1, k]], axis=0)

    def finish_second(h):
        def finish(k, value):
            ch = col * per_slice + k
            po[h, k] = vc[h, ch] - value
            keep(h, k).start()
            if h == 1:
                add_gram(both(k), ch)

        return finish

    nothing = lambda ch: None
    scatter_own(2, finish_second(0), nothing)
    scatter_added(3)

    def give_all(h):
        loop(half, lambda j: give_first(2 + h, j, po.at[h]))
        loop(half, lambda j: give_last(2 + h, j, po.at[h]))

    def hand_all(h):
        loop(half, lambda j: relay(2 + h, j, nothing))

    give_all(0)
    scatter_own(3, finish_second(1), nothing)
    gram = gram_sum(collect_gram(), grams[0], row, col, n_col, z_size, sent, None, lambda: give_all(1))
    upper_one, inverse_one = factorize(gram)

    ggram[...] = jnp.zeros_like(ggram)
    weights = terms_of(inverse_one)
    loop(per_slice, lambda k: add_gram(apply_terms(weights, both(k)), col * per_slice + k))
    gram = gram_sum(collect_gram(), grams[1], row, col, n_col, z_size, sent, lambda: hand_all(0), lambda: hand_all(1))
    upper_two, inverse_two = factorize(gram)
    f_ref[...] = jnp.dot(upper_two, upper_one, precision=HIGHEST, preferred_element_type=F32)
    t_ref[...] = terms_of(jnp.dot(inverse_two, inverse_one, precision=HIGHEST, preferred_element_type=F32))

    for copy in sent:
        copy.wait_send()

    def handed(g, k):
        hand_on(g, k, col, right).wait_send()

    def sent_step(k):
        for h in range(2):
            keep(h, k).wait()
        for c in range(4):
            far(c, k, right).wait_send()
            to_right(c, k).wait_send()
            to_left(c, k).wait_send()
        for g in range(4):
            at = targets(g).at[col * per_slice + k]
            give_right(g, at, k, col).wait_send()
            give_left(g, at, k, col).wait_send()
        for g in range(3):
            handed(g, k)

    loop(per_slice, sent_step)
    for h in range(2):
        gather_near(2 + h, nothing)
        gather_far(2 + h, nothing)
    loop(per_slice, lambda k: handed(3, k))


def apply_kernel(t_ref, p_hbm, f_ref, o_hbm, fo_ref, p, o, p_sem, o_sem):
    groups = p_sem.shape[0]
    size = p.shape[1] // groups

    def read(i):
        at = pl.ds(i * size, size)
        return pltpu.make_async_copy(p_hbm.at[:, at], p.at[:, at], p_sem.at[i])

    def write(i):
        at = pl.ds(i * size * WIDTH, size * WIDTH)
        return pltpu.make_async_copy(o.at[:, at], o_hbm.at[:, at], o_sem.at[i])

    for i in range(groups):
        read(i).start()
    fo_ref[...] = f_ref[...]
    weights = t_ref[...]
    for i in range(groups):
        read(i).wait()
        for k in range(i * size, (i + 1) * size):
            x = jnp.concatenate([p[0, k], p[1, k]], axis=0)
            o[:, k * WIDTH : (k + 1) * WIDTH] = apply_terms(weights, x)
        write(i).start()
    for i in range(groups):
        write(i).wait()


def local(n_col, n_row, locked, vectors, mass):
    mine, cols = locked.shape
    new = vectors.shape[0]
    part = new // 2
    chunks = cols // WIDTH
    per_slice = chunks // n_col
    z_size = n_row // GROUP
    dma = pltpu.SemaphoreType.DMA

    def exchange_scratch(rows):
        many = lambda n: pltpu.VMEM((n, rows, mine), F32)
        one = pltpu.VMEM((rows, mine), F32)
        x_size = GROUP // 2
        return [
            many(x_size), many(x_size), many(x_size - 1), dma((x_size - 1,)), dma((x_size - 1,)),
            one, many(2), dma((2,)), dma((2,)),
            one, many(z_size), dma((z_size,)), dma((z_size,)),
            dma((x_size,)), dma((x_size,)),
        ]

    def gram_scratch():
        packed = (new // 2, 2 * new)
        return [
            ref
            for size in (2, GROUP // 2, z_size, n_col)
            for ref in (pltpu.VMEM(packed, F32), pltpu.VMEM((size,) + packed, F32), dma((size,)), dma((size,)))
        ]

    chunk = lambda *n: pltpu.VMEM(n + (part, WIDTH), F32)
    scratch = [
        pltpu.VMEM((SLOTS, mine, 2 * WIDTH), F32), dma((SLOTS,)), chunk(2, chunks), dma((2, chunks)),
        pltpu.VMEM((chunks, mine, WIDTH), BF16), pltpu.VMEM((chunks, mine, WIDTH), BF16),
        pltpu.VMEM((3 * new, mine), F32), pltpu.VMEM((2, 3 * part, mine), F32),
        pltpu.VMEM((2, 3 * part, mine), BF16), pltpu.VMEM((3 * new, 3 * new), F32),
        chunk(2, chunks), chunk(2, per_slice), dma((2, per_slice)),
    ]
    scratch += exchange_scratch(2 * new // GROUP) + exchange_scratch(2 * part // GROUP) * 2
    scratch += gram_scratch() * 2
    ring = [dma((3 * per_slice,)), dma((3 * per_slice,))]
    scratch += ([chunk(per_slice)] * 3 + [chunk(3 * per_slice)] + ring) * 4 + ring * 4
    vmem = pl.BlockSpec(memory_space=pltpu.VMEM)
    hbm = pl.BlockSpec(memory_space=pl.ANY)
    projected, transform, factor = pl.pallas_call(
        functools.partial(fused, n_col, n_row, 1.0 / (cols * n_row)),
        out_shape=(
            jax.ShapeDtypeStruct((2, chunks, part, WIDTH), F32),
            jax.ShapeDtypeStruct((3 * new, 3 * new), BF16),
            jax.ShapeDtypeStruct((new, new), F32),
        ),
        in_specs=[hbm, hbm, vmem],
        out_specs=(hbm, vmem, vmem),
        scratch_shapes=scratch,
        compiler_params=pltpu.CompilerParams(
            collective_id=0, has_side_effects=True, vmem_limit_bytes=60 << 20
        ),
        name="project_and_factor",
    )(locked, vectors, mass.reshape(1, cols))
    groups = 4
    return tuple(
        pl.pallas_call(
            apply_kernel,
            out_shape=(jax.ShapeDtypeStruct((new, cols), F32), jax.ShapeDtypeStruct((new, new), F32)),
            in_specs=[vmem, hbm, vmem],
            out_specs=(hbm, vmem),
            scratch_shapes=[chunk(2, chunks), pltpu.VMEM((new, cols), F32), dma((groups,)), dma((groups,))],
            compiler_params=pltpu.CompilerParams(vmem_limit_bytes=62 << 20),
            name="apply_factors",
        )(transform, projected, factor)
    )


def solution(mesh):
    return jax.shard_map(
        functools.partial(local, mesh.shape["col"], mesh.shape["row"]),
        mesh=mesh,
        in_specs=(P("col", "row"), P(None, "row"), P("row")),
        out_specs=(P(None, "row"), P()),
        check_vma=False,
    )
```

```python
import functools

import jax
import jax.numpy as jnp
from jax import lax
from jax.experimental import pallas as pl
from jax.experimental.pallas import tpu as pltpu
from jax.sharding import PartitionSpec as P

MESH = pl.DeviceIdType.MESH
F32 = jnp.float32
BF16 = jnp.bfloat16
HIGHEST = lax.Precision.HIGHEST
WIDTH = 1024
GROUP = 8
SLOTS = 4


def split2(x):
    high = x.astype(BF16)
    return high, (x - high.astype(F32)).astype(BF16)


def split3(x):
    high = x.astype(BF16)
    rest = x - high.astype(F32)
    middle = rest.astype(BF16)
    low = (rest - middle.astype(F32)).astype(BF16)
    return high, middle, low


def dot_nt(a, b):
    return lax.dot_general(a, b, (((1,), (1,)), ((), ())), preferred_element_type=F32)


def dot_nn(a, b):
    return lax.dot_general(a, b, (((1,), (0,)), ((), ())), preferred_element_type=F32)


def exchange_steps(scratch, row, z_size, sent):
    (src, out, part, part_s, part_r, cred, cbuf, c_s, c_r, zred, zbuf, z_s, z_r, full_s, full_r) = scratch
    place = lax.rem(row, GROUP)
    base = row - place
    z = lax.div(row, GROUP)
    x, core = lax.div(place, 2), lax.rem(place, 2)
    x_size = GROUP // 2

    copies = []
    for d in range(1, x_size):
        peer = lax.rem(x + d, x_size)
        copy = pltpu.make_async_remote_copy(
            src_ref=src.at[peer], dst_ref=part.at[d - 1], send_sem=part_s.at[d - 1], recv_sem=part_r.at[d - 1],
            device_id={"row": base + 2 * peer + core}, device_id_type=MESH,
        )
        copy.start()
        copies.append(copy)
    yield
    total = src[x]
    for d in range(1, x_size):
        copies[d - 1].wait_recv()
        total = total + part[d - 1]
    cred[...] = total
    other = [(1 - core, {"row": base + 2 * x + 1 - core})]
    pairs = peer_start(cred, cbuf, c_s, c_r, core, other)
    yield
    zred[...] = peer_finish(pairs, cbuf, sent)
    peers = [lax.rem(z + d, z_size) for d in range(1, z_size)]
    pairs = peer_start(zred, zbuf, z_s, z_r, z, [(p, {"row": p * GROUP + place}) for p in peers])
    yield
    out[x] = peer_finish(pairs, zbuf, sent)
    for d in range(1, x_size):
        peer = lax.rem(x + d, x_size)
        copy = pltpu.make_async_remote_copy(
            src_ref=out.at[x], dst_ref=out.at[x], send_sem=full_s.at[d - 1], recv_sem=full_r.at[x],
            device_id={"row": base + 2 * peer + core}, device_id_type=MESH,
        )
        copy.start()
        copies.append(copy)
    yield
    for d in range(1, x_size):
        peer = lax.rem(x + d, x_size)
        pltpu.make_async_remote_copy(
            src_ref=out.at[peer], dst_ref=out.at[peer], send_sem=full_s.at[d - 1], recv_sem=full_r.at[peer],
            device_id={"row": row}, device_id_type=MESH,
        ).wait_recv()
    sent += copies


def peer_copies(src, buf, sems, semr, mine, peers):
    return [
        (
            pltpu.make_async_remote_copy(
                src_ref=src, dst_ref=buf.at[mine], send_sem=sems.at[i], recv_sem=semr.at[mine],
                device_id=device, device_id_type=MESH,
            ),
            pltpu.make_async_remote_copy(
                src_ref=src, dst_ref=buf.at[peer], send_sem=sems.at[i], recv_sem=semr.at[peer],
                device_id=device, device_id_type=MESH,
            ),
        )
        for i, (peer, device) in enumerate(peers)
    ]


def peer_start(src, buf, sems, semr, mine, peers):
    copies = peer_copies(src, buf, sems, semr, mine, peers)
    for out, _ in copies:
        out.start()
    buf[mine] = src[...]
    return copies


def peer_finish(copies, buf, sent):
    for _, arrival in copies:
        arrival.wait_recv()
    total = buf[0]
    for i in range(1, len(copies) + 1):
        total = total + buf[i]
    sent += [out for out, _ in copies]
    return total


def gram_sum(gram, scratch, row, col, n_col, z_size, sent, first, last):
    half = gram.shape[0] // 2
    place = lax.rem(row, GROUP)
    base = row - place
    z = lax.div(row, GROUP)
    x, core = lax.div(place, 2), lax.rem(place, 2)
    x_size = GROUP // 2
    stages = [
        (2, core, lambda p: {"row": base + 2 * x + p}, first),
        (x_size, x, lambda p: {"row": base + 2 * p + core}, None),
        (z_size, z, lambda p: {"row": p * GROUP + place}, None),
        (n_col, col, lambda p: {"col": p}, last),
    ]
    total = jnp.concatenate([gram[:half], gram[half:]], axis=1)
    for i, (size, mine, device, between) in enumerate(stages):
        src, buf, sems, semr = scratch[4 * i : 4 * i + 4]
        src[...] = total
        peers = [lax.rem(mine + d, size) for d in range(1, size)]
        pairs = peer_start(src, buf, sems, semr, mine, [(p, device(p)) for p in peers])
        if between is not None:
            between()
        total = peer_finish(pairs, buf, sent)
    new = gram.shape[0]
    return jnp.concatenate([total[:, :new], total[:, new:]], axis=0)


def factorize(gram):
    size = gram.shape[0]
    lane = lax.broadcasted_iota(jnp.int32, (size, 2 * size), 1)
    sub = lax.broadcasted_iota(jnp.int32, (size, 2 * size), 0)
    sub8 = lax.broadcasted_iota(jnp.int32, (8, 2 * size), 0)
    wide = jnp.concatenate([gram, jnp.zeros_like(gram)], axis=1)
    wide = jnp.where(lane < size, wide, jnp.where(lane - size == sub, 1.0, 0.0))
    blocks = [wide[8 * i : 8 * i + 8] for i in range(size // 8)]
    full = lambda x: jnp.broadcast_to(x, (8, 2 * size))
    for b in range(size // 8):
        j = 8 * b
        lines = [full(blocks[b][a : a + 1, :]) for a in range(8)]
        square = [[full(line[:, j + c : j + c + 1]) for c in range(8)] for line in lines]
        inverse = []
        for p in range(8):
            inverse.append(1.0 / square[p][p])
            for a in range(p + 1, 8):
                times = square[a][p] * inverse[p]
                lines[a] = lines[a] - times * lines[p]
                for c in range(p + 1, 8):
                    square[a][c] = square[a][c] - times * square[p][c]
        for i in range(b + 1, size // 8):
            column = [full(blocks[i][:, j + c : j + c + 1]) for c in range(8)]
            for p in range(8):
                times = column[p] * inverse[p]
                for q in range(p + 1, 8):
                    column[q] = column[q] - times * square[p][q]
                blocks[i] = blocks[i] - times * lines[p]
        for a in range(8):
            blocks[b] = jnp.where(sub8 == a, lines[a], blocks[b])
    body = jnp.concatenate(blocks, axis=0)
    pivots = jnp.sum(jnp.where(lane == sub, body, 0.0), axis=1, keepdims=True)
    body = body / jnp.sqrt(pivots)
    upper = jnp.where(lane >= sub, body, 0.0)[:, :size]
    return upper, body[:, size:]


def terms_of(matrix):
    a, b, c = split3(matrix)
    zero = jnp.zeros_like(a)
    return jnp.concatenate(
        [jnp.concatenate([a, a, a, b], axis=1), jnp.concatenate([c, b, zero, zero], axis=1)], axis=0
    )


def apply_terms(terms, x):
    new = x.shape[0]
    a, b, c = split3(x)
    r = dot_nn(terms, jnp.concatenate([a, b, c, a], axis=0))
    return r[:new] + r[new:]


def fused(
    n_col, n_row, scale,
    l_hbm, v_hbm, m_ref, p_hbm, t_ref, f_ref,
    lbuf, lsem, vc, vsem, l1, l2, acc, acc2, wsp, ggram, zf, po, psem,
    *rest,
):
    sums = [rest[15 * i : 15 * i + 15] for i in range(4)]
    grams = [rest[60 + 16 * i : 76 + 16 * i] for i in range(2)]
    scatters = [rest[92 + 6 * i : 98 + 6 * i] for i in range(4)]
    gathers = [rest[116 + 2 * i : 118 + 2 * i] for i in range(4)]
    col, row = lax.axis_index("col"), lax.axis_index("row")
    right, left = lax.rem(col + 1, n_col), lax.rem(col + n_col - 1, n_col)
    across = lax.rem(col + 2, n_col)
    z_size = n_row // GROUP
    place = lax.rem(row, GROUP)
    base = row - place
    z = lax.div(row, GROUP)
    chunks, part = vc.shape[1], vc.shape[2]
    per_slice = chunks // n_col
    half = per_slice // 2
    new = 2 * part

    def columns(ch):
        return pl.ds(pl.multiple_of(ch * WIDTH, WIDTH), WIDTH)

    def load_l(ch, slot):
        pair = pl.ds(pl.multiple_of(ch * 2 * WIDTH, 2 * WIDTH), 2 * WIDTH)
        return pltpu.make_async_copy(l_hbm.at[:, pair], lbuf.at[slot], lsem.at[slot])

    def load_v(h, ch):
        return pltpu.make_async_copy(
            v_hbm.at[h * part : (h + 1) * part, columns(ch)], vc.at[h, ch], vsem.at[h, ch]
        )

    def load(pair, slot):
        for i in range(2):
            for h in range(2):
                load_v(h, 2 * pair + i).start()
        load_l(pair, slot).start()

    for pair in range(SLOTS):
        load(pair, pair)

    barrier = pltpu.get_barrier_semaphore()
    for d in range(1, GROUP):
        pl.semaphore_signal(barrier, inc=1, device_id={"row": base + lax.rem(place + d, GROUP)}, device_id_type=MESH)
    for d in range(1, z_size):
        pl.semaphore_signal(
            barrier, inc=1, device_id={"row": lax.rem(z + d, z_size) * GROUP + place}, device_id_type=MESH
        )
    for d in range(1, n_col):
        pl.semaphore_signal(barrier, inc=1, device_id={"col": lax.rem(col + d, n_col)}, device_id_type=MESH)

    def collect(total):
        n = total.shape[0] // 3
        return (total[0:n] + (total[n : 2 * n] + total[2 * n :])) * scale

    acc[...] = jnp.zeros_like(acc)
    acc2[...] = jnp.zeros_like(acc2)

    def first_step(pair, carry):
        slot = lax.rem(pair, SLOTS)
        load_l(pair, slot).wait()
        high, low = split2(lbuf[slot])
        x = []
        for i in range(2):
            ch = 2 * pair + i
            l1[ch] = high[:, i * WIDTH : (i + 1) * WIDTH]
            l2[ch] = low[:, i * WIDTH : (i + 1) * WIDTH]
            load_v(0, ch).wait()
            load_v(1, ch).wait()
            x.append(jnp.concatenate([vc[0, ch], vc[1, ch]], axis=0) * m_ref[:, columns(ch)])
        a = jnp.concatenate(split3(jnp.concatenate(x, axis=1)), axis=0)
        acc[...] += dot_nt(a, high)
        acc[0 : 2 * new] += dot_nt(a[0 : 2 * new], low)

        @pl.when(pair + SLOTS < chunks // 2)
        def _():
            load(pair + SLOTS, slot)

        return carry

    lax.fori_loop(0, chunks // 2, first_step, 0)
    first = collect(acc[...])
    parts = sums[0][0].shape[0]
    for h in range(2):
        for i in range(parts):
            at = h * part + i * part // parts
            sums[h][0][i] = first[at : at + part // parts]
    pl.semaphore_wait(barrier, (GROUP - 1) + (z_size - 1) + (n_col - 1))
    sent = []
    firsts = [exchange_steps(sums[h], row, z_size, sent) for h in range(2)]
    for _ in range(4):
        for steps in firsts:
            next(steps)

    def summed(i):
        return jnp.concatenate([sums[i][1][k] for k in range(parts)], axis=0)

    def set_weights(h, b):
        for i, w in enumerate(split3(b)):
            wsp[h, i * part : (i + 1) * part] = w

    def term(h, ch):
        r = dot_nn(wsp[h], l1[ch])
        s = dot_nn(wsp[h, 0 : 2 * part], l2[ch])
        return r[0:part] + ((r[part : 2 * part] + s[0:part]) + (r[2 * part :] + s[part:]))

    def send(src, dst, sems, semr, index, where):
        return pltpu.make_async_remote_copy(
            src_ref=src, dst_ref=dst, send_sem=sems.at[index], recv_sem=semr.at[index],
            device_id={"col": where}, device_id_type=MESH,
        )

    def far(c, k, where):
        d2, fl, fr, stage, ss, sr = scatters[c]
        return send(stage.at[k], d2.at[k], ss, sr, k, where)

    def to_right(c, k):
        d2, fl, fr, stage, ss, sr = scatters[c]
        return send(stage.at[per_slice + k], fl.at[k], ss, sr, per_slice + k, right)

    def to_left(c, k):
        d2, fl, fr, stage, ss, sr = scatters[c]
        return send(stage.at[2 * per_slice + k], fr.at[k], ss, sr, 2 * per_slice + k, left)

    def loop(count, body):
        def step(j, carry):
            body(j)
            return carry

        lax.fori_loop(0, count, step, 0)

    def scatter_start(c):
        h, stage = c % 2, scatters[c][3]

        def far_step(j):
            stage[j] = term(h, across * per_slice + j)
            far(c, j, right).start()
            stage[half + j] = term(h, across * per_slice + half + j)
            far(c, half + j, left).start()

        def pure_step(j):
            stage[per_slice + half + j] = term(h, right * per_slice + half + j)
            to_right(c, half + j).start()
            stage[2 * per_slice + j] = term(h, left * per_slice + j)
            to_left(c, j).start()

        loop(half, far_step)
        loop(half, pure_step)

    def scatter_added(c):
        h, d2, stage = c % 2, scatters[c][0], scatters[c][3]

        def added_step(j):
            own = term(h, right * per_slice + j)
            far(c, j, right).wait_recv()
            stage[per_slice + j] = own + d2[j]
            to_right(c, j).start()
            own = term(h, left * per_slice + half + j)
            far(c, half + j, left).wait_recv()
            stage[2 * per_slice + half + j] = own + d2[half + j]
            to_left(c, half + j).start()

        loop(half, added_step)

    def scatter_own(c, finish, done):
        h, fl, fr = c % 2, scatters[c][1], scatters[c][2]

        def own_step(j):
            for k in (j, half + j):
                own = term(h, col * per_slice + k)
                to_left(c, k).wait_recv()
                to_right(c, k).wait_recv()
                finish(k, own + (fl[k] + fr[k]))
            done(j)

        loop(half, own_step)

    def targets(g):
        return (zf if g < 2 else p_hbm).at[g % 2]

    def give_right(g, src, k, sl):
        return send(src, targets(g).at[sl * per_slice + k], *gathers[g], k, right)

    def give_left(g, src, k, sl):
        return send(src, targets(g).at[sl * per_slice + k], *gathers[g], per_slice + k, left)

    def hand_on(g, k, sl, where):
        at = targets(g).at[sl * per_slice + k]
        return send(at, at, *gathers[g], 2 * per_slice + k, where)

    def relay(g, j, use):
        give_right(g, targets(g).at[left * per_slice + j], j, left).wait_recv()
        hand_on(g, j, left, right).start()
        give_left(g, targets(g).at[right * per_slice + half + j], half + j, right).wait_recv()
        hand_on(g, half + j, right, left).start()
        use(left * per_slice + j)
        use(right * per_slice + half + j)

    def give_first(g, j, src):
        give_right(g, src.at[j], j, col).start()
        give_left(g, src.at[half + j], half + j, col).start()

    def give_last(g, j, src):
        give_left(g, src.at[j], j, col).start()
        give_right(g, src.at[half + j], half + j, col).start()

    def gather_near(g, use):
        def near_step(j):
            give_right(g, targets(g).at[left * per_slice + half + j], half + j, left).wait_recv()
            give_left(g, targets(g).at[right * per_slice + j], j, right).wait_recv()
            use(left * per_slice + half + j)
            use(right * per_slice + j)

        loop(half, near_step)

    def gather_far(g, use):
        def far_step(j):
            for k in (j, half + j):
                hand_on(g, k, across, right).wait_recv()
            for k in (j, half + j):
                use(across * per_slice + k)

        loop(half, far_step)

    def use_once(h):
        def use(ch):
            x = (vc[h, ch] - zf[h, ch]) * m_ref[:, columns(ch)]
            a = jnp.concatenate(split3(x), axis=0)
            acc2[h] += dot_nt(a, l1[ch])
            acc2[h, 0 : 2 * part] += dot_nt(a[0 : 2 * part], l2[ch])

        return use

    def own_first(h):
        mine = zf.at[h, pl.ds(col * per_slice, per_slice)]

        def finish(k, value):
            zf[h, col * per_slice + k] = value

        scatter_own(h, finish, lambda j: give_first(h, j, mine))
        loop(half, lambda j: give_last(h, j, mine))
        loop(per_slice, lambda k: use_once(h)(col * per_slice + k))

    def second_sum(h, hooks):
        second = collect(acc2[h])
        for i in range(parts):
            sums[2 + h][0][i] = second[i * part // parts : (i + 1) * part // parts]
        for i, _ in enumerate(exchange_steps(sums[2 + h], row, z_size, sent)):
            if hooks[i] is not None:
                hooks[i]()
        set_weights(h, summed(h) + summed(2 + h))

    next(firsts[0], None)
    set_weights(0, summed(0))
    scatter_start(0)
    next(firsts[1], None)
    set_weights(1, summed(1))
    scatter_added(0)
    scatter_start(1)
    own_first(0)
    scatter_added(1)
    loop(half, lambda j: relay(0, j, use_once(0)))
    own_first(1)
    gather_near(0, use_once(0))
    gather_far(0, use_once(0))
    relays = [lambda j=j: relay(1, j, use_once(1)) for j in range(half)]
    second_sum(0, [relays[0], None, relays[1], lambda: gather_near(1, use_once(1))])
    scatter_start(2)
    gather_far(1, use_once(1))
    second_sum(1, [None, None, lambda: scatter_added(2), None])
    scatter_start(3)

    ggram[...] = jnp.zeros_like(ggram)

    def add_gram(p, ch):
        a = jnp.concatenate(split3(p * m_ref[:, columns(ch)]), axis=0)
        b = jnp.concatenate(split3(p), axis=0)
        ggram[...] += dot_nt(a, b)

    def collect_gram():
        g = ggram[...]
        rows3 = g[0:new] + (g[new : 2 * new] + g[2 * new :])
        gram = rows3[:, 0:new] + (rows3[:, new : 2 * new] + rows3[:, 2 * new :])
        return gram * scale

    def keep(h, k):
        return pltpu.make_async_copy(po.at[h, k], p_hbm.at[h, col * per_slice + k], psem.at[h, k])

    def both(k):
        return jnp.concatenate([po[0, k], po[1, k]], axis=0)

    def finish_second(h):
        def finish(k, value):
            ch = col * per_slice + k
            po[h, k] = vc[h, ch] - value
            keep(h, k).start()
            if h == 1:
                add_gram(both(k), ch)

        return finish

    nothing = lambda ch: None
    scatter_own(2, finish_second(0), nothing)
    scatter_added(3)

    def give_all(h):
        loop(half, lambda j: give_first(2 + h, j, po.at[h]))
        loop(half, lambda j: give_last(2 + h, j, po.at[h]))

    def hand_all(h):
        loop(half, lambda j: relay(2 + h, j, nothing))

    give_all(0)
    scatter_own(3, finish_second(1), nothing)
    gram = gram_sum(collect_gram(), grams[0], row, col, n_col, z_size, sent, None, lambda: give_all(1))
    upper_one, inverse_one = factorize(gram)

    ggram[...] = jnp.zeros_like(ggram)
    weights = terms_of(inverse_one)
    loop(per_slice, lambda k: add_gram(apply_terms(weights, both(k)), col * per_slice + k))
    gram = gram_sum(collect_gram(), grams[1], row, col, n_col, z_size, sent, lambda: hand_all(0), lambda: hand_all(1))
    upper_two, inverse_two = factorize(gram)
    f_ref[...] = jnp.dot(upper_two, upper_one, precision=HIGHEST, preferred_element_type=F32)
    t_ref[...] = terms_of(jnp.dot(inverse_two, inverse_one, precision=HIGHEST, preferred_element_type=F32))

    for copy in sent:
        copy.wait_send()

    def handed(g, k):
        hand_on(g, k, col, right).wait_send()

    def sent_step(k):
        for h in range(2):
            keep(h, k).wait()
        for c in range(4):
            far(c, k, right).wait_send()
            to_right(c, k).wait_send()
            to_left(c, k).wait_send()
        for g in range(4):
            at = targets(g).at[col * per_slice + k]
            give_right(g, at, k, col).wait_send()
            give_left(g, at, k, col).wait_send()
        for g in range(3):
            handed(g, k)

    loop(per_slice, sent_step)
    for h in range(2):
        gather_near(2 + h, nothing)
        gather_far(2 + h, nothing)
    loop(per_slice, lambda k: handed(3, k))


def apply_kernel(t_ref, p_ref, f_ref, o_ref, fo_ref):
    fo_ref[...] = f_ref[...]
    weights = t_ref[...]
    for i in range(p_ref.shape[1]):
        p = jnp.concatenate([p_ref[0, i], p_ref[1, i]], axis=0)
        o_ref[:, i * WIDTH : (i + 1) * WIDTH] = apply_terms(weights, p)


def local(n_col, n_row, locked, vectors, mass):
    mine, cols = locked.shape
    new = vectors.shape[0]
    part = new // 2
    chunks = cols // WIDTH
    per_slice = chunks // n_col
    z_size = n_row // GROUP
    dma = pltpu.SemaphoreType.DMA

    def exchange_scratch(rows):
        many = lambda n: pltpu.VMEM((n, rows, mine), F32)
        one = pltpu.VMEM((rows, mine), F32)
        x_size = GROUP // 2
        return [
            many(x_size), many(x_size), many(x_size - 1), dma((x_size - 1,)), dma((x_size - 1,)),
            one, many(2), dma((2,)), dma((2,)),
            one, many(z_size), dma((z_size,)), dma((z_size,)),
            dma((x_size,)), dma((x_size,)),
        ]

    def gram_scratch():
        packed = (new // 2, 2 * new)
        return [
            ref
            for size in (2, GROUP // 2, z_size, n_col)
            for ref in (pltpu.VMEM(packed, F32), pltpu.VMEM((size,) + packed, F32), dma((size,)), dma((size,)))
        ]

    chunk = lambda *n: pltpu.VMEM(n + (part, WIDTH), F32)
    scratch = [
        pltpu.VMEM((SLOTS, mine, 2 * WIDTH), F32), dma((SLOTS,)), chunk(2, chunks), dma((2, chunks)),
        pltpu.VMEM((chunks, mine, WIDTH), BF16), pltpu.VMEM((chunks, mine, WIDTH), BF16),
        pltpu.VMEM((3 * new, mine), F32), pltpu.VMEM((2, 3 * part, mine), F32),
        pltpu.VMEM((2, 3 * part, mine), BF16), pltpu.VMEM((3 * new, 3 * new), F32),
        chunk(2, chunks), chunk(2, per_slice), dma((2, per_slice)),
    ]
    scratch += exchange_scratch(2 * part // GROUP) * 4
    scratch += gram_scratch() * 2
    ring = [dma((3 * per_slice,)), dma((3 * per_slice,))]
    scratch += ([chunk(per_slice)] * 3 + [chunk(3 * per_slice)] + ring) * 4 + ring * 4
    vmem = pl.BlockSpec(memory_space=pltpu.VMEM)
    hbm = pl.BlockSpec(memory_space=pl.ANY)
    projected, transform, factor = pl.pallas_call(
        functools.partial(fused, n_col, n_row, 1.0 / (cols * n_row)),
        out_shape=(
            jax.ShapeDtypeStruct((2, chunks, part, WIDTH), F32),
            jax.ShapeDtypeStruct((2 * new, 4 * new), BF16),
            jax.ShapeDtypeStruct((new, new), F32),
        ),
        in_specs=[hbm, hbm, vmem],
        out_specs=(hbm, vmem, vmem),
        scratch_shapes=scratch,
        compiler_params=pltpu.CompilerParams(
            collective_id=0, has_side_effects=True, vmem_limit_bytes=60 << 20
        ),
        name="project_and_factor",
    )(locked, vectors, mass.reshape(1, cols))
    block = 8
    still = lambda n: pl.BlockSpec((n, n), lambda i: (0, 0))
    return tuple(
        pl.pallas_call(
            apply_kernel,
            grid=(chunks // block,),
            out_shape=(jax.ShapeDtypeStruct((new, cols), F32), jax.ShapeDtypeStruct((new, new), F32)),
            in_specs=[
                pl.BlockSpec((2 * new, 4 * new), lambda i: (0, 0)),
                pl.BlockSpec((2, block, part, WIDTH), lambda i: (0, i, 0, 0)),
                still(new),
            ],
            out_specs=(pl.BlockSpec((new, block * WIDTH), lambda i: (0, i)), still(new)),
            name="apply_factors",
        )(transform, projected, factor)
    )


def solution(mesh):
    return jax.shard_map(
        functools.partial(local, mesh.shape["col"], mesh.shape["row"]),
        mesh=mesh,
        in_specs=(P("col", "row"), P(None, "row"), P("row")),
        out_specs=(P(None, "row"), P()),
        check_vma=False,
    )
```

```python
import functools

import jax
import jax.numpy as jnp
from jax import lax
from jax.experimental import pallas as pl
from jax.experimental.pallas import tpu as pltpu
from jax.sharding import PartitionSpec as P

MESH = pl.DeviceIdType.MESH
F32 = jnp.float32
BF16 = jnp.bfloat16
HIGHEST = lax.Precision.HIGHEST
WIDTH = 1024
GROUP = 8
SLOTS = 4


def split2(x):
    high = x.astype(BF16)
    return high, (x - high.astype(F32)).astype(BF16)


def split3(x):
    high = x.astype(BF16)
    rest = x - high.astype(F32)
    middle = rest.astype(BF16)
    low = (rest - middle.astype(F32)).astype(BF16)
    return high, middle, low


def dot_nt(a, b):
    return lax.dot_general(a, b, (((1,), (1,)), ((), ())), preferred_element_type=F32)


def dot_nn(a, b):
    return lax.dot_general(a, b, (((1,), (0,)), ((), ())), preferred_element_type=F32)


def remote(src, dst, send_sem, recv_sem, device):
    return pltpu.make_async_remote_copy(
        src_ref=src, dst_ref=dst, send_sem=send_sem, recv_sem=recv_sem, device_id=device, device_id_type=MESH
    )


def exchange_steps(scratch, row, z_size, sent):
    (src, out, part, cred, cbuf, zred, zbuf, sems) = scratch
    place = lax.rem(row, GROUP)
    base = row - place
    z = lax.div(row, GROUP)
    x, core = lax.div(place, 2), lax.rem(place, 2)
    x_size = GROUP // 2
    here = {"row": row}
    others = [lax.rem(x + d, x_size) for d in range(1, x_size)]
    device = lambda p: {"row": base + 2 * p + core}

    for d, peer in enumerate(others):
        remote(src.at[peer], part.at[d], sems.at[0], sems.at[1], device(peer)).start()
    yield
    arrived = remote(part, part, sems.at[0], sems.at[1], here)
    arrived.wait_recv()
    total = src[x]
    for d in range(x_size - 1):
        total = total + part[d]
    cred[...] = total
    peer_start(cred, cbuf, sems.at[2], sems.at[3], core, [{"row": base + 2 * x + 1 - core}])
    yield
    zred[...] = peer_finish(cbuf, sems.at[2], sems.at[3], here, sent)
    peers = [{"row": lax.rem(z + d, z_size) * GROUP + place} for d in range(1, z_size)]
    peer_start(zred, zbuf, sems.at[4], sems.at[5], z, peers)
    yield
    out[x] = peer_finish(zbuf, sems.at[4], sems.at[5], here, sent)
    for peer in others:
        remote(out.at[x], out.at[x], sems.at[6], sems.at[7], device(peer)).start()
    yield
    rest = out.at[0 : x_size - 1]
    gathered = remote(rest, rest, sems.at[6], sems.at[7], here)
    gathered.wait_recv()
    sent += [arrived, gathered]


def peer_start(src, buf, send_sem, recv_sem, mine, devices):
    for device in devices:
        remote(src, buf.at[mine], send_sem, recv_sem, device).start()
    buf[mine] = src[...]


def peer_finish(buf, send_sem, recv_sem, here, sent):
    size = buf.shape[0]
    rest = buf.at[0 : size - 1]
    arrived = remote(rest, rest, send_sem, recv_sem, here)
    arrived.wait_recv()
    sent.append(arrived)
    total = buf[0]
    for i in range(1, size):
        total = total + buf[i]
    return total


def gram_sum(gram, scratch, row, col, n_col, z_size, sent, first, last):
    half = gram.shape[0] // 2
    place = lax.rem(row, GROUP)
    base = row - place
    z = lax.div(row, GROUP)
    x, core = lax.div(place, 2), lax.rem(place, 2)
    x_size = GROUP // 2
    stages = [
        (2, core, lambda p: {"row": base + 2 * x + p}, first),
        (x_size, x, lambda p: {"row": base + 2 * p + core}, None),
        (z_size, z, lambda p: {"row": p * GROUP + place}, None),
        (n_col, col, lambda p: {"col": p}, last),
    ]
    total = jnp.concatenate([gram[:half], gram[half:]], axis=1)
    sems = scratch[-1]
    for i, (size, mine, device, between) in enumerate(stages):
        src, buf = scratch[2 * i : 2 * i + 2]
        src[...] = total
        peer_start(src, buf, sems.at[2 * i], sems.at[2 * i + 1], mine, [device(lax.rem(mine + d, size)) for d in range(1, size)])
        if between is not None:
            between()
        total = peer_finish(buf, sems.at[2 * i], sems.at[2 * i + 1], {"row": row}, sent)
    new = gram.shape[0]
    return jnp.concatenate([total[:, :new], total[:, new:]], axis=0)


def factorize(gram):
    size = gram.shape[0]
    lane = lax.broadcasted_iota(jnp.int32, (size, 2 * size), 1)
    sub = lax.broadcasted_iota(jnp.int32, (size, 2 * size), 0)
    sub8 = lax.broadcasted_iota(jnp.int32, (8, 2 * size), 0)
    wide = jnp.concatenate([gram, jnp.zeros_like(gram)], axis=1)
    wide = jnp.where(lane < size, wide, jnp.where(lane - size == sub, 1.0, 0.0))
    blocks = [wide[8 * i : 8 * i + 8] for i in range(size // 8)]
    full = lambda x: jnp.broadcast_to(x, (8, 2 * size))
    for b in range(size // 8):
        j = 8 * b
        lines = [full(blocks[b][a : a + 1, :]) for a in range(8)]
        square = [[full(line[:, j + c : j + c + 1]) for c in range(8)] for line in lines]
        inverse = []
        for p in range(8):
            inverse.append(1.0 / square[p][p])
            for a in range(p + 1, 8):
                times = square[a][p] * inverse[p]
                lines[a] = lines[a] - times * lines[p]
                for c in range(p + 1, 8):
                    square[a][c] = square[a][c] - times * square[p][c]
        for i in range(b + 1, size // 8):
            column = [full(blocks[i][:, j + c : j + c + 1]) for c in range(8)]
            for p in range(8):
                times = column[p] * inverse[p]
                for q in range(p + 1, 8):
                    column[q] = column[q] - times * square[p][q]
                blocks[i] = blocks[i] - times * lines[p]
        for a in range(8):
            blocks[b] = jnp.where(sub8 == a, lines[a], blocks[b])
    body = jnp.concatenate(blocks, axis=0)
    pivots = jnp.sum(jnp.where(lane == sub, body, 0.0), axis=1, keepdims=True)
    body = body / jnp.sqrt(pivots)
    upper = jnp.where(lane >= sub, body, 0.0)[:, :size]
    return upper, body[:, size:]


def terms_of(matrix):
    a, b, c = split3(matrix)
    zero = jnp.zeros_like(a)
    return jnp.concatenate(
        [jnp.concatenate([a, a, a, b], axis=1), jnp.concatenate([c, b, zero, zero], axis=1)], axis=0
    )


def apply_terms(terms, x):
    new = x.shape[0]
    a, b, c = split3(x)
    r = dot_nn(terms, jnp.concatenate([a, b, c, a], axis=0))
    return r[:new] + r[new:]


def fused(
    n_col, n_row, scale,
    l_hbm, v_hbm, m_ref, p_hbm, t_ref, f_ref,
    lbuf, lsem, vc, vsem, l1, l2, acc, acc2, wsp, ggram, zf, po, psem,
    *rest,
):
    sums = [rest[8 * i : 8 * i + 8] for i in range(4)]
    grams = [rest[32 + 9 * i : 41 + 9 * i] for i in range(2)]
    scatters = [rest[50 + 6 * i : 56 + 6 * i] for i in range(4)]
    gathers = [rest[74 + 2 * i : 76 + 2 * i] for i in range(4)]
    col, row = lax.axis_index("col"), lax.axis_index("row")
    right, left = lax.rem(col + 1, n_col), lax.rem(col + n_col - 1, n_col)
    across = lax.rem(col + 2, n_col)
    z_size = n_row // GROUP
    place = lax.rem(row, GROUP)
    base = row - place
    z = lax.div(row, GROUP)
    chunks, part = vc.shape[1] // WIDTH, vc.shape[0] // 2
    per_slice = chunks // n_col
    half = per_slice // 2
    new = 2 * part

    def columns(ch):
        return pl.ds(pl.multiple_of(ch * WIDTH, WIDTH), WIDTH)

    def pair_columns(pair):
        return pl.ds(pl.multiple_of(pair * 2 * WIDTH, 2 * WIDTH), 2 * WIDTH)

    def load_l(pair, slot):
        return pltpu.make_async_copy(l_hbm.at[:, pair_columns(pair)], lbuf.at[slot], lsem.at[slot])

    def load_v(pair):
        at = pair_columns(pair)
        return pltpu.make_async_copy(v_hbm.at[:, at], vc.at[:, at], vsem.at[pair])

    def load(pair, slot):
        load_v(pair).start()
        load_l(pair, slot).start()

    def vectors_of(h, ch):
        return vc[h * part : (h + 1) * part, columns(ch)]

    for pair in range(SLOTS):
        load(pair, pair)

    barrier = pltpu.get_barrier_semaphore()
    for d in range(1, GROUP):
        pl.semaphore_signal(barrier, inc=1, device_id={"row": base + lax.rem(place + d, GROUP)}, device_id_type=MESH)
    for d in range(1, z_size):
        pl.semaphore_signal(
            barrier, inc=1, device_id={"row": lax.rem(z + d, z_size) * GROUP + place}, device_id_type=MESH
        )
    for d in range(1, n_col):
        pl.semaphore_signal(barrier, inc=1, device_id={"col": lax.rem(col + d, n_col)}, device_id_type=MESH)

    def collect(total):
        n = total.shape[0] // 3
        return (total[0:n] + (total[n : 2 * n] + total[2 * n :])) * scale

    acc[...] = jnp.zeros_like(acc)
    acc2[...] = jnp.zeros_like(acc2)

    def first_step(pair, carry):
        slot = lax.rem(pair, SLOTS)
        load_l(pair, slot).wait()
        high, low = split2(lbuf[slot])
        for i in range(2):
            l1[2 * pair + i] = high[:, i * WIDTH : (i + 1) * WIDTH]
            l2[2 * pair + i] = low[:, i * WIDTH : (i + 1) * WIDTH]
        load_v(pair).wait()
        x = vc[:, pair_columns(pair)] * m_ref[:, pair_columns(pair)]
        a = jnp.concatenate(split3(x), axis=0)
        acc[...] += dot_nt(a, high)
        acc[0 : 2 * new] += dot_nt(a[0 : 2 * new], low)

        @pl.when(pair + SLOTS < chunks // 2)
        def _():
            load(pair + SLOTS, slot)

        return carry

    lax.fori_loop(0, chunks // 2, first_step, 0)
    first = collect(acc[...])
    parts = sums[0][0].shape[0]
    for h in range(2):
        for i in range(parts):
            at = h * part + i * part // parts
            sums[h][0][i] = first[at : at + part // parts]
    pl.semaphore_wait(barrier, (GROUP - 1) + (z_size - 1) + (n_col - 1))
    sent = []
    firsts = [exchange_steps(sums[h], row, z_size, sent) for h in range(2)]
    for _ in range(4):
        for steps in firsts:
            next(steps)

    def summed(i):
        return jnp.concatenate([sums[i][1][k] for k in range(parts)], axis=0)

    def set_weights(h, b):
        for i, w in enumerate(split3(b)):
            wsp[h, i * part : (i + 1) * part] = w

    def term(h, ch):
        r = dot_nn(wsp[h], l1[ch])
        s = dot_nn(wsp[h, 0 : 2 * part], l2[ch])
        return r[0:part] + ((r[part : 2 * part] + s[0:part]) + (r[2 * part :] + s[part:]))

    def send(src, dst, sems, semr, index, where):
        return remote(src, dst, sems.at[0], semr.at[index], {"col": where})

    def far(c, k, where):
        d2, fl, fr, stage, ss, sr = scatters[c]
        return send(stage.at[k], d2.at[k], ss, sr, k, where)

    def to_right(c, k):
        d2, fl, fr, stage, ss, sr = scatters[c]
        return send(stage.at[per_slice + k], fl.at[k], ss, sr, per_slice + k, right)

    def to_left(c, k):
        d2, fl, fr, stage, ss, sr = scatters[c]
        return send(stage.at[2 * per_slice + k], fr.at[k], ss, sr, 2 * per_slice + k, left)

    def loop(count, body):
        def step(j, carry):
            body(j)
            return carry

        lax.fori_loop(0, count, step, 0)

    def scatter_start(c):
        h, stage = c % 2, scatters[c][3]

        def far_step(j):
            stage[j] = term(h, across * per_slice + j)
            far(c, j, right).start()
            stage[half + j] = term(h, across * per_slice + half + j)
            far(c, half + j, left).start()

        def pure_step(j):
            stage[per_slice + half + j] = term(h, right * per_slice + half + j)
            to_right(c, half + j).start()
            stage[2 * per_slice + j] = term(h, left * per_slice + j)
            to_left(c, j).start()

        loop(half, far_step)
        loop(half, pure_step)

    def scatter_added(c):
        h, d2, stage = c % 2, scatters[c][0], scatters[c][3]

        def added_step(j):
            own = term(h, right * per_slice + j)
            far(c, j, right).wait_recv()
            stage[per_slice + j] = own + d2[j]
            to_right(c, j).start()
            own = term(h, left * per_slice + half + j)
            far(c, half + j, left).wait_recv()
            stage[2 * per_slice + half + j] = own + d2[half + j]
            to_left(c, half + j).start()

        loop(half, added_step)

    def scatter_own(c, finish, done):
        h, fl, fr = c % 2, scatters[c][1], scatters[c][2]

        def own_step(j):
            for k in (j, half + j):
                own = term(h, col * per_slice + k)
                to_left(c, k).wait_recv()
                to_right(c, k).wait_recv()
                finish(k, own + (fl[k] + fr[k]))
            done(j)

        loop(half, own_step)

    def targets(g):
        return (zf if g < 2 else p_hbm).at[g % 2]

    def give_right(g, src, k, sl):
        return send(src, targets(g).at[sl * per_slice + k], *gathers[g], k, right)

    def give_left(g, src, k, sl):
        return send(src, targets(g).at[sl * per_slice + k], *gathers[g], per_slice + k, left)

    def hand_on(g, k, sl, where):
        at = targets(g).at[sl * per_slice + k]
        return send(at, at, *gathers[g], 2 * per_slice + k, where)

    def relay(g, j, use):
        give_right(g, targets(g).at[left * per_slice + j], j, left).wait_recv()
        hand_on(g, j, left, right).start()
        give_left(g, targets(g).at[right * per_slice + half + j], half + j, right).wait_recv()
        hand_on(g, half + j, right, left).start()
        use(left * per_slice + j)
        use(right * per_slice + half + j)

    def give_first(g, j, src):
        give_right(g, src.at[j], j, col).start()
        give_left(g, src.at[half + j], half + j, col).start()

    def give_last(g, j, src):
        give_left(g, src.at[j], j, col).start()
        give_right(g, src.at[half + j], half + j, col).start()

    def gather_near(g, use):
        def near_step(j):
            give_right(g, targets(g).at[left * per_slice + half + j], half + j, left).wait_recv()
            give_left(g, targets(g).at[right * per_slice + j], j, right).wait_recv()
            use(left * per_slice + half + j)
            use(right * per_slice + j)

        loop(half, near_step)

    def gather_far(g, use):
        def far_step(j):
            for k in (j, half + j):
                hand_on(g, k, across, right).wait_recv()
            for k in (j, half + j):
                use(across * per_slice + k)

        loop(half, far_step)

    def use_once(h):
        def use(ch):
            x = (vectors_of(h, ch) - zf[h, ch]) * m_ref[:, columns(ch)]
            a = jnp.concatenate(split3(x), axis=0)
            acc2[h] += dot_nt(a, l1[ch])
            acc2[h, 0 : 2 * part] += dot_nt(a[0 : 2 * part], l2[ch])

        return use

    def own_first(h):
        mine = zf.at[h, pl.ds(col * per_slice, per_slice)]

        def finish(k, value):
            zf[h, col * per_slice + k] = value

        scatter_own(h, finish, lambda j: give_first(h, j, mine))
        loop(half, lambda j: give_last(h, j, mine))
        loop(per_slice, lambda k: use_once(h)(col * per_slice + k))

    def second_sum(h, hooks):
        second = collect(acc2[h])
        for i in range(parts):
            sums[2 + h][0][i] = second[i * part // parts : (i + 1) * part // parts]
        for i, _ in enumerate(exchange_steps(sums[2 + h], row, z_size, sent)):
            if hooks[i] is not None:
                hooks[i]()
        set_weights(h, summed(h) + summed(2 + h))

    next(firsts[0], None)
    set_weights(0, summed(0))
    scatter_start(0)
    next(firsts[1], None)
    set_weights(1, summed(1))
    scatter_added(0)
    scatter_start(1)
    own_first(0)
    scatter_added(1)
    loop(half, lambda j: relay(0, j, use_once(0)))
    own_first(1)
    gather_near(0, use_once(0))
    gather_far(0, use_once(0))
    relays = [lambda j=j: relay(1, j, use_once(1)) for j in range(half)]
    second_sum(0, [relays[0], None, relays[1], lambda: gather_near(1, use_once(1))])
    scatter_start(2)
    gather_far(1, use_once(1))
    second_sum(1, [None, None, lambda: scatter_added(2), None])
    scatter_start(3)

    ggram[...] = jnp.zeros_like(ggram)

    def add_gram(p, ch):
        a = jnp.concatenate(split3(p * m_ref[:, columns(ch)]), axis=0)
        b = jnp.concatenate(split3(p), axis=0)
        ggram[...] += dot_nt(a, b)

    def collect_gram():
        g = ggram[...]
        rows3 = g[0:new] + (g[new : 2 * new] + g[2 * new :])
        gram = rows3[:, 0:new] + (rows3[:, new : 2 * new] + rows3[:, 2 * new :])
        return gram * scale

    def keep(h):
        return pltpu.make_async_copy(po.at[h], p_hbm.at[h, pl.ds(col * per_slice, per_slice)], psem.at[h])

    def both(k):
        return jnp.concatenate([po[0, k], po[1, k]], axis=0)

    def finish_second(h):
        def finish(k, value):
            ch = col * per_slice + k
            po[h, k] = vectors_of(h, ch) - value
            if h == 1:
                add_gram(both(k), ch)

        return finish

    nothing = lambda ch: None
    scatter_own(2, finish_second(0), nothing)
    keep(0).start()
    scatter_added(3)

    def give_all(h):
        loop(half, lambda j: give_first(2 + h, j, po.at[h]))
        loop(half, lambda j: give_last(2 + h, j, po.at[h]))

    def hand_all(h):
        loop(half, lambda j: relay(2 + h, j, nothing))

    give_all(0)
    scatter_own(3, finish_second(1), nothing)
    keep(1).start()
    gram = gram_sum(collect_gram(), grams[0], row, col, n_col, z_size, sent, None, lambda: give_all(1))
    upper_one, inverse_one = factorize(gram)

    ggram[...] = jnp.zeros_like(ggram)
    weights = terms_of(inverse_one)
    loop(per_slice, lambda k: add_gram(apply_terms(weights, both(k)), col * per_slice + k))
    gram = gram_sum(collect_gram(), grams[1], row, col, n_col, z_size, sent, lambda: hand_all(0), lambda: hand_all(1))
    upper_two, inverse_two = factorize(gram)
    f_ref[...] = jnp.dot(upper_two, upper_one, precision=HIGHEST, preferred_element_type=F32)
    t_ref[...] = terms_of(jnp.dot(inverse_two, inverse_one, precision=HIGHEST, preferred_element_type=F32))

    for copy in sent:
        copy.wait_send()

    def all_sent(c, sems, semr):
        stage = scatters[c][3]
        remote(stage, stage, sems.at[0], semr.at[0], {"col": right}).wait_send()

    for h in range(2):
        keep(h).wait()
    for c in range(4):
        all_sent(c, scatters[c][4], scatters[c][5])
    for g in range(2):
        all_sent(g, *gathers[g])
    for h in range(2):
        gather_near(2 + h, nothing)
        gather_far(2 + h, nothing)
    for g in range(2, 4):
        all_sent(g, *gathers[g])


def apply_kernel(t_ref, p_ref, f_ref, o_ref, fo_ref):
    fo_ref[...] = f_ref[...]
    weights = t_ref[...]
    for i in range(p_ref.shape[1]):
        p = jnp.concatenate([p_ref[0, i], p_ref[1, i]], axis=0)
        o_ref[:, i * WIDTH : (i + 1) * WIDTH] = apply_terms(weights, p)


def local(n_col, n_row, locked, vectors, mass):
    mine, cols = locked.shape
    new = vectors.shape[0]
    part = new // 2
    chunks = cols // WIDTH
    per_slice = chunks // n_col
    z_size = n_row // GROUP
    dma = pltpu.SemaphoreType.DMA

    def exchange_scratch(rows):
        many = lambda n: pltpu.VMEM((n, rows, mine), F32)
        one = pltpu.VMEM((rows, mine), F32)
        x_size = GROUP // 2
        return [many(x_size), many(x_size), many(x_size - 1), one, many(2), one, many(z_size), dma((8,))]

    def gram_scratch():
        packed = (new // 2, 2 * new)
        sizes = (2, GROUP // 2, z_size, n_col)
        return [ref for n in sizes for ref in (pltpu.VMEM(packed, F32), pltpu.VMEM((n,) + packed, F32))] + [dma((8,))]

    chunk = lambda *n: pltpu.VMEM(n + (part, WIDTH), F32)
    scratch = [
        pltpu.VMEM((SLOTS, mine, 2 * WIDTH), F32), dma((SLOTS,)), pltpu.VMEM((new, cols), F32), dma((chunks // 2,)),
        pltpu.VMEM((chunks, mine, WIDTH), BF16), pltpu.VMEM((chunks, mine, WIDTH), BF16),
        pltpu.VMEM((3 * new, mine), F32), pltpu.VMEM((2, 3 * part, mine), F32),
        pltpu.VMEM((2, 3 * part, mine), BF16), pltpu.VMEM((3 * new, 3 * new), F32),
        chunk(2, chunks), chunk(2, per_slice), dma((2,)),
    ]
    scratch += exchange_scratch(2 * part // GROUP) * 4
    scratch += gram_scratch() * 2
    ring = [dma((1,)), dma((3 * per_slice,))]
    scratch += ([chunk(per_slice)] * 3 + [chunk(3 * per_slice)] + ring) * 4 + ring * 4
    vmem = pl.BlockSpec(memory_space=pltpu.VMEM)
    hbm = pl.BlockSpec(memory_space=pl.ANY)
    projected, transform, factor = pl.pallas_call(
        functools.partial(fused, n_col, n_row, 1.0 / (cols * n_row)),
        out_shape=(
            jax.ShapeDtypeStruct((2, chunks, part, WIDTH), F32),
            jax.ShapeDtypeStruct((2 * new, 4 * new), BF16),
            jax.ShapeDtypeStruct((new, new), F32),
        ),
        in_specs=[hbm, hbm, vmem],
        out_specs=(hbm, vmem, vmem),
        scratch_shapes=scratch,
        compiler_params=pltpu.CompilerParams(
            collective_id=0, has_side_effects=True, vmem_limit_bytes=60 << 20
        ),
        name="project_and_factor",
    )(locked, vectors, mass.reshape(1, cols))
    block = 8
    still = lambda n: pl.BlockSpec((n, n), lambda i: (0, 0))
    return tuple(
        pl.pallas_call(
            apply_kernel,
            grid=(chunks // block,),
            out_shape=(jax.ShapeDtypeStruct((new, cols), F32), jax.ShapeDtypeStruct((new, new), F32)),
            in_specs=[
                pl.BlockSpec((2 * new, 4 * new), lambda i: (0, 0)),
                pl.BlockSpec((2, block, part, WIDTH), lambda i: (0, i, 0, 0)),
                still(new),
            ],
            out_specs=(pl.BlockSpec((new, block * WIDTH), lambda i: (0, i)), still(new)),
            name="apply_factors",
        )(transform, projected, factor)
    )


def solution(mesh):
    return jax.shard_map(
        functools.partial(local, mesh.shape["col"], mesh.shape["row"]),
        mesh=mesh,
        in_specs=(P("col", "row"), P(None, "row"), P("row")),
        out_specs=(P(None, "row"), P()),
        check_vma=False,
    )
```

```python
import functools

import jax
import jax.numpy as jnp
from jax import lax
from jax.experimental import pallas as pl
from jax.experimental.pallas import tpu as pltpu
from jax.sharding import PartitionSpec as P

MESH = pl.DeviceIdType.MESH
F32 = jnp.float32
BF16 = jnp.bfloat16
HIGHEST = lax.Precision.HIGHEST
WIDTH = 1024
GROUP = 8
SLOTS = 4


def split2(x):
    high = x.astype(BF16)
    return high, (x - high.astype(F32)).astype(BF16)


def split3(x):
    high = x.astype(BF16)
    rest = x - high.astype(F32)
    middle = rest.astype(BF16)
    low = (rest - middle.astype(F32)).astype(BF16)
    return high, middle, low


def dot_nt(a, b):
    return lax.dot_general(a, b, (((1,), (1,)), ((), ())), preferred_element_type=F32)


def dot_nn(a, b):
    return lax.dot_general(a, b, (((1,), (0,)), ((), ())), preferred_element_type=F32)


def remote(src, dst, send_sem, recv_sem, device):
    return pltpu.make_async_remote_copy(
        src_ref=src, dst_ref=dst, send_sem=send_sem, recv_sem=recv_sem, device_id=device, device_id_type=MESH
    )


def exchange_steps(scratch, row, z_size, sent):
    (src, out, part, cred, cbuf, zred, zbuf, sems) = scratch
    place = lax.rem(row, GROUP)
    base = row - place
    z = lax.div(row, GROUP)
    x, core = lax.div(place, 2), lax.rem(place, 2)
    x_size = GROUP // 2
    here = {"row": row}
    others = [lax.rem(x + d, x_size) for d in range(1, x_size)]
    device = lambda p: {"row": base + 2 * p + core}

    for d, peer in enumerate(others):
        remote(src.at[peer], part.at[d], sems.at[0], sems.at[1], device(peer)).start()
    yield
    arrived = remote(part, part, sems.at[0], sems.at[1], here)
    arrived.wait_recv()
    total = src[x]
    for d in range(x_size - 1):
        total = total + part[d]
    cred[...] = total
    peer_start(cred, cbuf, sems.at[2], sems.at[3], core, [{"row": base + 2 * x + 1 - core}])
    yield
    zred[...] = peer_finish(cbuf, sems.at[2], sems.at[3], here, sent)
    peers = [{"row": lax.rem(z + d, z_size) * GROUP + place} for d in range(1, z_size)]
    peer_start(zred, zbuf, sems.at[4], sems.at[5], z, peers)
    yield
    out[x] = peer_finish(zbuf, sems.at[4], sems.at[5], here, sent)
    for peer in others:
        remote(out.at[x], out.at[x], sems.at[6], sems.at[7], device(peer)).start()
    yield
    rest = out.at[0 : x_size - 1]
    gathered = remote(rest, rest, sems.at[6], sems.at[7], here)
    gathered.wait_recv()
    sent += [arrived, gathered]


def peer_start(src, buf, send_sem, recv_sem, mine, devices):
    for device in devices:
        remote(src, buf.at[mine], send_sem, recv_sem, device).start()
    buf[mine] = src[...]


def peer_finish(buf, send_sem, recv_sem, here, sent):
    size = buf.shape[0]
    rest = buf.at[0 : size - 1]
    arrived = remote(rest, rest, send_sem, recv_sem, here)
    arrived.wait_recv()
    sent.append(arrived)
    total = buf[0]
    for i in range(1, size):
        total = total + buf[i]
    return total


def gram_sum(gram, scratch, row, col, n_col, z_size, sent, first, last):
    half = gram.shape[0] // 2
    place = lax.rem(row, GROUP)
    base = row - place
    z = lax.div(row, GROUP)
    x, core = lax.div(place, 2), lax.rem(place, 2)
    x_size = GROUP // 2
    stages = [
        (2, core, lambda p: {"row": base + 2 * x + p}, first),
        (x_size, x, lambda p: {"row": base + 2 * p + core}, None),
        (z_size, z, lambda p: {"row": p * GROUP + place}, None),
        (n_col, col, lambda p: {"col": p}, last),
    ]
    total = jnp.concatenate([gram[:half], gram[half:]], axis=1)
    sems = scratch[-1]
    for i, (size, mine, device, between) in enumerate(stages):
        src, buf = scratch[2 * i : 2 * i + 2]
        src[...] = total
        peer_start(src, buf, sems.at[2 * i], sems.at[2 * i + 1], mine, [device(lax.rem(mine + d, size)) for d in range(1, size)])
        if between is not None:
            between()
        total = peer_finish(buf, sems.at[2 * i], sems.at[2 * i + 1], {"row": row}, sent)
    new = gram.shape[0]
    return jnp.concatenate([total[:, :new], total[:, new:]], axis=0)


def factorize(gram):
    size = gram.shape[0]
    lane = lax.broadcasted_iota(jnp.int32, (size, 2 * size), 1)
    sub = lax.broadcasted_iota(jnp.int32, (size, 2 * size), 0)
    sub8 = lax.broadcasted_iota(jnp.int32, (8, 2 * size), 0)
    wide = jnp.concatenate([gram, jnp.zeros_like(gram)], axis=1)
    wide = jnp.where(lane < size, wide, jnp.where(lane - size == sub, 1.0, 0.0))
    blocks = [wide[8 * i : 8 * i + 8] for i in range(size // 8)]
    full = lambda x: jnp.broadcast_to(x, (8, 2 * size))
    for b in range(size // 8):
        j = 8 * b
        lines = [full(blocks[b][a : a + 1, :]) for a in range(8)]
        square = [[full(line[:, j + c : j + c + 1]) for c in range(8)] for line in lines]
        inverse = []
        for p in range(8):
            inverse.append(1.0 / square[p][p])
            for a in range(p + 1, 8):
                times = square[a][p] * inverse[p]
                lines[a] = lines[a] - times * lines[p]
                for c in range(p + 1, 8):
                    square[a][c] = square[a][c] - times * square[p][c]
        for i in range(b + 1, size // 8):
            column = [full(blocks[i][:, j + c : j + c + 1]) for c in range(8)]
            for p in range(8):
                times = column[p] * inverse[p]
                for q in range(p + 1, 8):
                    column[q] = column[q] - times * square[p][q]
                blocks[i] = blocks[i] - times * lines[p]
        for a in range(8):
            blocks[b] = jnp.where(sub8 == a, lines[a], blocks[b])
    body = jnp.concatenate(blocks, axis=0)
    pivots = jnp.sum(jnp.where(lane == sub, body, 0.0), axis=1, keepdims=True)
    body = body / jnp.sqrt(pivots)
    upper = jnp.where(lane >= sub, body, 0.0)[:, :size]
    return upper, body[:, size:]


def terms_of(matrix):
    a, b, c = split3(matrix)
    zero = jnp.zeros_like(a)
    return jnp.concatenate(
        [jnp.concatenate([a, a, a, b], axis=1), jnp.concatenate([c, b, zero, zero], axis=1)], axis=0
    )


def apply_terms(terms, x):
    new = x.shape[0]
    a, b, c = split3(x)
    r = dot_nn(terms, jnp.concatenate([a, b, c, a], axis=0))
    return r[:new] + r[new:]


def fused(
    n_col, n_row, scale,
    l_hbm, v_hbm, m_hbm, p_hbm, t_hbm, f_hbm,
    m_ref, t_ref, f_ref, small,
    lbuf, lsem, vc, vsem, l1, l2, acc, acc2, wsp, ggram, zf, po, psem,
    *rest,
):
    sums = [rest[8 * i : 8 * i + 8] for i in range(4)]
    grams = [rest[32 + 9 * i : 41 + 9 * i] for i in range(2)]
    scatters = [rest[50 + 6 * i : 56 + 6 * i] for i in range(4)]
    gathers = [rest[74 + 2 * i : 76 + 2 * i] for i in range(4)]
    col, row = lax.axis_index("col"), lax.axis_index("row")
    right, left = lax.rem(col + 1, n_col), lax.rem(col + n_col - 1, n_col)
    across = lax.rem(col + 2, n_col)
    z_size = n_row // GROUP
    place = lax.rem(row, GROUP)
    base = row - place
    z = lax.div(row, GROUP)
    chunks, part = vc.shape[1] // WIDTH, vc.shape[0] // 2
    per_slice = chunks // n_col
    half = per_slice // 2
    new = 2 * part

    def columns(ch):
        return pl.ds(pl.multiple_of(ch * WIDTH, WIDTH), WIDTH)

    def pair_columns(pair):
        return pl.ds(pl.multiple_of(pair * 2 * WIDTH, 2 * WIDTH), 2 * WIDTH)

    def load_l(pair, slot):
        return pltpu.make_async_copy(l_hbm.at[:, pair_columns(pair)], lbuf.at[slot], lsem.at[slot])

    def load_v(pair):
        at = pair_columns(pair)
        return pltpu.make_async_copy(v_hbm.at[:, at], vc.at[:, at], vsem.at[pair])

    def load(pair, slot):
        load_v(pair).start()
        load_l(pair, slot).start()

    def vectors_of(h, ch):
        return vc[h * part : (h + 1) * part, columns(ch)]

    mass = pltpu.make_async_copy(m_hbm, m_ref, small.at[0])
    mass.start()
    for pair in range(SLOTS):
        load(pair, pair)

    barrier = pltpu.get_barrier_semaphore()
    for d in range(1, GROUP):
        pl.semaphore_signal(barrier, inc=1, device_id={"row": base + lax.rem(place + d, GROUP)}, device_id_type=MESH)
    for d in range(1, z_size):
        pl.semaphore_signal(
            barrier, inc=1, device_id={"row": lax.rem(z + d, z_size) * GROUP + place}, device_id_type=MESH
        )
    for d in range(1, n_col):
        pl.semaphore_signal(barrier, inc=1, device_id={"col": lax.rem(col + d, n_col)}, device_id_type=MESH)

    def collect(total):
        n = total.shape[0] // 3
        return (total[0:n] + (total[n : 2 * n] + total[2 * n :])) * scale

    acc[...] = jnp.zeros_like(acc)
    acc2[...] = jnp.zeros_like(acc2)

    mass.wait()

    def first_step(pair, carry):
        slot = lax.rem(pair, SLOTS)
        load_l(pair, slot).wait()
        high, low = split2(lbuf[slot])
        for i in range(2):
            l1[2 * pair + i] = high[:, i * WIDTH : (i + 1) * WIDTH]
            l2[2 * pair + i] = low[:, i * WIDTH : (i + 1) * WIDTH]
        load_v(pair).wait()
        x = vc[:, pair_columns(pair)] * m_ref[:, pair_columns(pair)]
        a = jnp.concatenate(split3(x), axis=0)
        acc[...] += dot_nt(a, high)
        acc[0 : 2 * new] += dot_nt(a[0 : 2 * new], low)

        @pl.when(pair + SLOTS < chunks // 2)
        def _():
            load(pair + SLOTS, slot)

        return carry

    lax.fori_loop(0, chunks // 2, first_step, 0)
    first = collect(acc[...])
    parts = sums[0][0].shape[0]
    for h in range(2):
        for i in range(parts):
            at = h * part + i * part // parts
            sums[h][0][i] = first[at : at + part // parts]
    pl.semaphore_wait(barrier, (GROUP - 1) + (z_size - 1) + (n_col - 1))
    sent = []
    firsts = [exchange_steps(sums[h], row, z_size, sent) for h in range(2)]
    for _ in range(4):
        for steps in firsts:
            next(steps)

    def summed(i):
        return jnp.concatenate([sums[i][1][k] for k in range(parts)], axis=0)

    def set_weights(h, b):
        for i, w in enumerate(split3(b)):
            wsp[h, i * part : (i + 1) * part] = w

    def term(h, ch):
        r = dot_nn(wsp[h], l1[ch])
        s = dot_nn(wsp[h, 0 : 2 * part], l2[ch])
        return r[0:part] + ((r[part : 2 * part] + s[0:part]) + (r[2 * part :] + s[part:]))

    def send(src, dst, sems, semr, index, where):
        return remote(src, dst, sems.at[0], semr.at[index], {"col": where})

    def wait_blocks(stage, sems, semr, index, count):
        blocks = stage.at[0:count]
        remote(blocks, blocks, sems.at[0], semr.at[index], {"col": right}).wait_recv()

    def far(c, k, j, where):
        d2, fl, fr, stage, ss, sr = scatters[c]
        return send(stage.at[k], d2.at[k], ss, sr, j, where)

    def to_right(c, k, j):
        d2, fl, fr, stage, ss, sr = scatters[c]
        return send(stage.at[per_slice + k], fl.at[k], ss, sr, half + j, right)

    def to_left(c, k, j):
        d2, fl, fr, stage, ss, sr = scatters[c]
        return send(stage.at[2 * per_slice + k], fr.at[k], ss, sr, half + j, left)

    def loop(count, body):
        def step(j, carry):
            body(j)
            return carry

        lax.fori_loop(0, count, step, 0)

    def scatter_start(c):
        h, stage = c % 2, scatters[c][3]

        def far_step(j):
            stage[j] = term(h, across * per_slice + j)
            far(c, j, j, right).start()
            stage[half + j] = term(h, across * per_slice + half + j)
            far(c, half + j, j, left).start()

        def pure_step(j):
            stage[per_slice + half + j] = term(h, right * per_slice + half + j)
            to_right(c, half + j, j).start()
            stage[2 * per_slice + j] = term(h, left * per_slice + j)
            to_left(c, j, j).start()

        loop(half, far_step)
        loop(half, pure_step)

    def scatter_added(c):
        h, d2, stage = c % 2, scatters[c][0], scatters[c][3]

        def added_step(j):
            to_the_right = term(h, right * per_slice + j)
            to_the_left = term(h, left * per_slice + half + j)
            wait_blocks(stage, *scatters[c][4:], j, 2)
            stage[per_slice + j] = to_the_right + d2[j]
            to_right(c, j, j).start()
            stage[2 * per_slice + half + j] = to_the_left + d2[half + j]
            to_left(c, half + j, j).start()

        loop(half, added_step)

    def scatter_own(c, finish, done):
        h, fl, fr = c % 2, scatters[c][1], scatters[c][2]

        def own_step(j):
            own = [term(h, col * per_slice + k) for k in (j, half + j)]
            wait_blocks(scatters[c][3], *scatters[c][4:], half + j, 4)
            for k, value in zip((j, half + j), own):
                finish(k, value + (fl[k] + fr[k]))
            done(j)

        loop(half, own_step)

    def targets(g):
        return (zf if g < 2 else p_hbm).at[g % 2]

    def give_right(g, src, k, index):
        send(src, targets(g).at[col * per_slice + k], *gathers[g], index, right).start()

    def give_left(g, src, k, index):
        send(src, targets(g).at[col * per_slice + k], *gathers[g], index, left).start()

    def hand_on(g, j, k, sl, where):
        at = targets(g).at[sl * per_slice + k]
        send(at, at, *gathers[g], 2 * half + j, where).start()

    def relay(g, j, use):
        wait_blocks(scatters[g][3], *gathers[g], j, 2)
        hand_on(g, j, j, left, right)
        hand_on(g, j, half + j, right, left)
        use(left * per_slice + j)
        use(right * per_slice + half + j)

    def give_first(g, j, src):
        give_right(g, src.at[j], j, j)
        give_left(g, src.at[half + j], half + j, j)

    def give_last(g, j, src):
        give_left(g, src.at[j], j, half + j)
        give_right(g, src.at[half + j], half + j, half + j)

    def gather_near(g, use):
        def near_step(j):
            wait_blocks(scatters[g][3], *gathers[g], half + j, 2)
            use(left * per_slice + half + j)
            use(right * per_slice + j)

        loop(half, near_step)

    def gather_far(g, use):
        def far_step(j):
            wait_blocks(scatters[g][3], *gathers[g], 2 * half + j, 2)
            for k in (j, half + j):
                use(across * per_slice + k)

        loop(half, far_step)

    def use_once(h):
        def use(ch):
            x = (vectors_of(h, ch) - zf[h, ch]) * m_ref[:, columns(ch)]
            a = jnp.concatenate(split3(x), axis=0)
            acc2[h] += dot_nt(a, l1[ch])
            acc2[h, 0 : 2 * part] += dot_nt(a[0 : 2 * part], l2[ch])

        return use

    def own_first(h):
        mine = zf.at[h, pl.ds(col * per_slice, per_slice)]

        def finish(k, value):
            zf[h, col * per_slice + k] = value

        scatter_own(h, finish, lambda j: give_first(h, j, mine))
        loop(half, lambda j: give_last(h, j, mine))
        loop(per_slice, lambda k: use_once(h)(col * per_slice + k))

    def second_sum(h, hooks):
        second = collect(acc2[h])
        for i in range(parts):
            sums[2 + h][0][i] = second[i * part // parts : (i + 1) * part // parts]
        for i, _ in enumerate(exchange_steps(sums[2 + h], row, z_size, sent)):
            if hooks[i] is not None:
                hooks[i]()
        set_weights(h, summed(h) + summed(2 + h))

    next(firsts[0], None)
    set_weights(0, summed(0))
    scatter_start(0)
    next(firsts[1], None)
    set_weights(1, summed(1))
    scatter_added(0)
    scatter_start(1)
    own_first(0)
    scatter_added(1)
    loop(half, lambda j: relay(0, j, use_once(0)))
    own_first(1)
    gather_near(0, use_once(0))
    gather_far(0, use_once(0))
    relays = [lambda j=j: relay(1, j, use_once(1)) for j in range(half)]
    second_sum(0, [relays[0], None, relays[1], lambda: gather_near(1, use_once(1))])
    scatter_start(2)
    gather_far(1, use_once(1))
    second_sum(1, [None, None, lambda: scatter_added(2), None])
    scatter_start(3)

    ggram[...] = jnp.zeros_like(ggram)

    def add_gram(p, ch):
        a = jnp.concatenate(split3(p * m_ref[:, columns(ch)]), axis=0)
        b = jnp.concatenate(split3(p), axis=0)
        ggram[...] += dot_nt(a, b)

    def collect_gram():
        g = ggram[...]
        rows3 = g[0:new] + (g[new : 2 * new] + g[2 * new :])
        gram = rows3[:, 0:new] + (rows3[:, new : 2 * new] + rows3[:, 2 * new :])
        return gram * scale

    def keep(h):
        return pltpu.make_async_copy(po.at[h], p_hbm.at[h, pl.ds(col * per_slice, per_slice)], psem.at[h])

    def both(k):
        return jnp.concatenate([po[0, k], po[1, k]], axis=0)

    def finish_second(h):
        def finish(k, value):
            ch = col * per_slice + k
            po[h, k] = vectors_of(h, ch) - value
            if h == 1:
                add_gram(both(k), ch)

        return finish

    nothing = lambda ch: None
    scatter_own(2, finish_second(0), nothing)
    keep(0).start()
    scatter_added(3)

    def give_all(h):
        loop(half, lambda j: give_first(2 + h, j, po.at[h]))
        loop(half, lambda j: give_last(2 + h, j, po.at[h]))

    def hand_all(h):
        loop(half, lambda j: relay(2 + h, j, nothing))

    give_all(0)
    scatter_own(3, finish_second(1), nothing)
    keep(1).start()
    gram = gram_sum(collect_gram(), grams[0], row, col, n_col, z_size, sent, None, lambda: give_all(1))
    upper_one, inverse_one = factorize(gram)

    ggram[...] = jnp.zeros_like(ggram)
    weights = terms_of(inverse_one)
    loop(per_slice, lambda k: add_gram(apply_terms(weights, both(k)), col * per_slice + k))
    gram = gram_sum(collect_gram(), grams[1], row, col, n_col, z_size, sent, lambda: hand_all(0), lambda: hand_all(1))
    upper_two, inverse_two = factorize(gram)
    f_ref[...] = jnp.dot(upper_two, upper_one, precision=HIGHEST, preferred_element_type=F32)
    t_ref[...] = terms_of(jnp.dot(inverse_two, inverse_one, precision=HIGHEST, preferred_element_type=F32))

    results = [
        pltpu.make_async_copy(t_ref, t_hbm, small.at[1]),
        pltpu.make_async_copy(f_ref, f_hbm, small.at[2]),
    ]
    for copy in results:
        copy.start()
    for copy in sent:
        copy.wait_send()

    def all_sent(c, sems, semr):
        stage = scatters[c][3]
        remote(stage, stage, sems.at[0], semr.at[0], {"col": right}).wait_send()

    for copy in results:
        copy.wait()
    for h in range(2):
        keep(h).wait()
    for c in range(4):
        all_sent(c, scatters[c][4], scatters[c][5])
    for g in range(2):
        all_sent(g, *gathers[g])
    for h in range(2):
        gather_near(2 + h, nothing)
        gather_far(2 + h, nothing)
    for g in range(2, 4):
        all_sent(g, *gathers[g])


def apply_kernel(t_ref, p_ref, f_ref, o_ref, fo_ref):
    fo_ref[...] = f_ref[...]
    weights = t_ref[...]
    for i in range(p_ref.shape[1]):
        p = jnp.concatenate([p_ref[0, i], p_ref[1, i]], axis=0)
        o_ref[:, i * WIDTH : (i + 1) * WIDTH] = apply_terms(weights, p)


def local(n_col, n_row, locked, vectors, mass):
    mine, cols = locked.shape
    new = vectors.shape[0]
    part = new // 2
    chunks = cols // WIDTH
    per_slice = chunks // n_col
    z_size = n_row // GROUP
    dma = pltpu.SemaphoreType.DMA

    def exchange_scratch(rows):
        many = lambda n: pltpu.VMEM((n, rows, mine), F32)
        one = pltpu.VMEM((rows, mine), F32)
        x_size = GROUP // 2
        return [many(x_size), many(x_size), many(x_size - 1), one, many(2), one, many(z_size), dma((8,))]

    def gram_scratch():
        packed = (new // 2, 2 * new)
        sizes = (2, GROUP // 2, z_size, n_col)
        return [ref for n in sizes for ref in (pltpu.VMEM(packed, F32), pltpu.VMEM((n,) + packed, F32))] + [dma((8,))]

    chunk = lambda *n: pltpu.VMEM(n + (part, WIDTH), F32)
    scratch = [
        pltpu.VMEM((1, cols), F32), pltpu.VMEM((2 * new, 4 * new), BF16), pltpu.VMEM((new, new), F32), dma((3,)),
        pltpu.VMEM((SLOTS, mine, 2 * WIDTH), F32), dma((SLOTS,)), pltpu.VMEM((new, cols), F32), dma((chunks // 2,)),
        pltpu.VMEM((chunks, mine, WIDTH), BF16), pltpu.VMEM((chunks, mine, WIDTH), BF16),
        pltpu.VMEM((3 * new, mine), F32), pltpu.VMEM((2, 3 * part, mine), F32),
        pltpu.VMEM((2, 3 * part, mine), BF16), pltpu.VMEM((3 * new, 3 * new), F32),
        chunk(2, chunks), chunk(2, per_slice), dma((2,)),
    ]
    scratch += exchange_scratch(2 * part // GROUP) * 4
    scratch += gram_scratch() * 2
    ring = lambda n: [dma((1,)), dma((n * per_slice // 2,))]
    scratch += ([chunk(per_slice)] * 3 + [chunk(3 * per_slice)] + ring(2)) * 4 + ring(3) * 4
    hbm = pl.BlockSpec(memory_space=pl.ANY)
    projected, transform, factor = pl.pallas_call(
        functools.partial(fused, n_col, n_row, 1.0 / (cols * n_row)),
        out_shape=(
            jax.ShapeDtypeStruct((2, chunks, part, WIDTH), F32),
            jax.ShapeDtypeStruct((2 * new, 4 * new), BF16),
            jax.ShapeDtypeStruct((new, new), F32),
        ),
        in_specs=[hbm] * 3,
        out_specs=(hbm,) * 3,
        scratch_shapes=scratch,
        compiler_params=pltpu.CompilerParams(
            collective_id=0, has_side_effects=True, vmem_limit_bytes=60 << 20
        ),
        name="project_and_factor",
    )(locked, vectors, mass.reshape(1, cols))
    block = 8
    still = lambda n: pl.BlockSpec((n, n), lambda i: (0, 0))
    return tuple(
        pl.pallas_call(
            apply_kernel,
            grid=(chunks // block,),
            out_shape=(jax.ShapeDtypeStruct((new, cols), F32), jax.ShapeDtypeStruct((new, new), F32)),
            in_specs=[
                pl.BlockSpec((2 * new, 4 * new), lambda i: (0, 0)),
                pl.BlockSpec((2, block, part, WIDTH), lambda i: (0, i, 0, 0)),
                still(new),
            ],
            out_specs=(pl.BlockSpec((new, block * WIDTH), lambda i: (0, i)), still(new)),
            name="apply_factors",
        )(transform, projected, factor)
    )


def solution(mesh):
    return jax.shard_map(
        functools.partial(local, mesh.shape["col"], mesh.shape["row"]),
        mesh=mesh,
        in_specs=(P("col", "row"), P(None, "row"), P("row")),
        out_specs=(P(None, "row"), P()),
        check_vma=False,
    )
```

```python
import functools

import jax
import jax.numpy as jnp
from jax import lax
from jax.experimental import pallas as pl
from jax.experimental.pallas import tpu as pltpu
from jax.sharding import PartitionSpec as P

MESH = pl.DeviceIdType.MESH
F32 = jnp.float32
BF16 = jnp.bfloat16
HIGHEST = lax.Precision.HIGHEST
WIDTH = 1024
GROUP = 8
SLOTS = 4


def split2(x):
    high = x.astype(BF16)
    return high, (x - high.astype(F32)).astype(BF16)


def split3(x):
    high = x.astype(BF16)
    rest = x - high.astype(F32)
    middle = rest.astype(BF16)
    low = (rest - middle.astype(F32)).astype(BF16)
    return high, middle, low


def dot_nt(a, b):
    return lax.dot_general(a, b, (((1,), (1,)), ((), ())), preferred_element_type=F32)


def dot_nn(a, b):
    return lax.dot_general(a, b, (((1,), (0,)), ((), ())), preferred_element_type=F32)


def remote(src, dst, send_sem, recv_sem, device):
    return pltpu.make_async_remote_copy(
        src_ref=src, dst_ref=dst, send_sem=send_sem, recv_sem=recv_sem, device_id=device, device_id_type=MESH
    )


def exchange_steps(scratch, row, z_size, sent):
    (src, out, part, cred, cbuf, zred, zbuf, sems) = scratch
    place = lax.rem(row, GROUP)
    base = row - place
    z = lax.div(row, GROUP)
    x, core = lax.div(place, 2), lax.rem(place, 2)
    x_size = GROUP // 2
    here = {"row": row}
    others = [lax.rem(x + d, x_size) for d in range(1, x_size)]
    device = lambda p: {"row": base + 2 * p + core}

    for d, peer in enumerate(others):
        remote(src.at[peer], part.at[d], sems.at[0], sems.at[1], device(peer)).start()
    yield
    arrived = remote(part, part, sems.at[0], sems.at[1], here)
    arrived.wait_recv()
    total = src[x]
    for d in range(x_size - 1):
        total = total + part[d]
    cred[...] = total
    peer_start(cred, cbuf, sems.at[2], sems.at[3], core, [{"row": base + 2 * x + 1 - core}])
    yield
    zred[...] = peer_finish(cbuf, sems.at[2], sems.at[3], here, sent)
    peers = [{"row": lax.rem(z + d, z_size) * GROUP + place} for d in range(1, z_size)]
    peer_start(zred, zbuf, sems.at[4], sems.at[5], z, peers)
    yield
    out[x] = peer_finish(zbuf, sems.at[4], sems.at[5], here, sent)
    for peer in others:
        remote(out.at[x], out.at[x], sems.at[6], sems.at[7], device(peer)).start()
    yield
    rest = out.at[0 : x_size - 1]
    gathered = remote(rest, rest, sems.at[6], sems.at[7], here)
    gathered.wait_recv()
    sent += [arrived, gathered]


def peer_start(src, buf, send_sem, recv_sem, mine, devices):
    for device in devices:
        remote(src, buf.at[mine], send_sem, recv_sem, device).start()
    buf[mine] = src[...]


def peer_finish(buf, send_sem, recv_sem, here, sent):
    size = buf.shape[0]
    rest = buf.at[0 : size - 1]
    arrived = remote(rest, rest, send_sem, recv_sem, here)
    arrived.wait_recv()
    sent.append(arrived)
    total = buf[0]
    for i in range(1, size):
        total = total + buf[i]
    return total


def gram_sum(gram, scratch, row, col, n_col, z_size, sent, first, last):
    half = gram.shape[0] // 2
    place = lax.rem(row, GROUP)
    base = row - place
    z = lax.div(row, GROUP)
    x, core = lax.div(place, 2), lax.rem(place, 2)
    x_size = GROUP // 2
    stages = [
        (2, core, lambda p: {"row": base + 2 * x + p}, first),
        (x_size, x, lambda p: {"row": base + 2 * p + core}, None),
        (z_size, z, lambda p: {"row": p * GROUP + place}, None),
        (n_col, col, lambda p: {"col": p}, last),
    ]
    total = jnp.concatenate([gram[:half], gram[half:]], axis=1)
    sems = scratch[-1]
    for i, (size, mine, device, between) in enumerate(stages):
        src, buf = scratch[2 * i : 2 * i + 2]
        src[...] = total
        peer_start(src, buf, sems.at[2 * i], sems.at[2 * i + 1], mine, [device(lax.rem(mine + d, size)) for d in range(1, size)])
        if between is not None:
            between()
        total = peer_finish(buf, sems.at[2 * i], sems.at[2 * i + 1], {"row": row}, sent)
    new = gram.shape[0]
    return jnp.concatenate([total[:, :new], total[:, new:]], axis=0)


def factorize(gram):
    size = gram.shape[0]
    lane = lax.broadcasted_iota(jnp.int32, (size, 2 * size), 1)
    sub = lax.broadcasted_iota(jnp.int32, (size, 2 * size), 0)
    sub8 = lax.broadcasted_iota(jnp.int32, (8, 2 * size), 0)
    wide = jnp.concatenate([gram, jnp.zeros_like(gram)], axis=1)
    wide = jnp.where(lane < size, wide, jnp.where(lane - size == sub, 1.0, 0.0))
    blocks = [wide[8 * i : 8 * i + 8] for i in range(size // 8)]
    full = lambda x: jnp.broadcast_to(x, (8, 2 * size))
    for b in range(size // 8):
        j = 8 * b
        lines = [full(blocks[b][a : a + 1, :]) for a in range(8)]
        square = [[full(line[:, j + c : j + c + 1]) for c in range(8)] for line in lines]
        inverse = []
        for p in range(8):
            inverse.append(1.0 / square[p][p])
            for a in range(p + 1, 8):
                times = square[a][p] * inverse[p]
                lines[a] = lines[a] - times * lines[p]
                for c in range(p + 1, 8):
                    square[a][c] = square[a][c] - times * square[p][c]
        for i in range(b + 1, size // 8):
            column = [full(blocks[i][:, j + c : j + c + 1]) for c in range(8)]
            for p in range(8):
                times = column[p] * inverse[p]
                for q in range(p + 1, 8):
                    column[q] = column[q] - times * square[p][q]
                blocks[i] = blocks[i] - times * lines[p]
        for a in range(8):
            blocks[b] = jnp.where(sub8 == a, lines[a], blocks[b])
    body = jnp.concatenate(blocks, axis=0)
    pivots = jnp.sum(jnp.where(lane == sub, body, 0.0), axis=1, keepdims=True)
    body = body / jnp.sqrt(pivots)
    upper = jnp.where(lane >= sub, body, 0.0)[:, :size]
    return upper, body[:, size:]


def terms_of(matrix):
    a, b, c = split3(matrix)
    zero = jnp.zeros_like(a)
    return jnp.concatenate(
        [jnp.concatenate([a, a, a, b], axis=1), jnp.concatenate([c, b, zero, zero], axis=1)], axis=0
    )


def apply_terms(terms, x):
    new = x.shape[0]
    a, b, c = split3(x)
    r = dot_nn(terms, jnp.concatenate([a, b, c, a], axis=0))
    return r[:new] + r[new:]


def fused(
    n_col, n_row, scale,
    l_hbm, v_hbm, m_hbm, p_hbm, t_hbm, f_hbm,
    m_ref, t_ref, f_ref, small,
    lbuf, lsem, vc, vsem, l1, l2, acc, acc2, wsp, ggram, zf, po, psem,
    *rest,
):
    sums = [rest[8 * i : 8 * i + 8] for i in range(4)]
    grams = [rest[32 + 9 * i : 41 + 9 * i] for i in range(2)]
    scatters = [rest[50 + 6 * i : 56 + 6 * i] for i in range(4)]
    gathers = [rest[74 + 2 * i : 76 + 2 * i] for i in range(4)]
    col, row = lax.axis_index("col"), lax.axis_index("row")
    right, left = lax.rem(col + 1, n_col), lax.rem(col + n_col - 1, n_col)
    across = lax.rem(col + 2, n_col)
    z_size = n_row // GROUP
    place = lax.rem(row, GROUP)
    base = row - place
    z = lax.div(row, GROUP)
    chunks, part = vc.shape[1] // WIDTH, vc.shape[0] // 2
    per_slice = chunks // n_col
    half = per_slice // 2
    new = 2 * part

    def columns(ch):
        return pl.ds(pl.multiple_of(ch * WIDTH, WIDTH), WIDTH)

    def pair_columns(pair):
        return pl.ds(pl.multiple_of(pair * 2 * WIDTH, 2 * WIDTH), 2 * WIDTH)

    def load_l(pair, slot):
        return pltpu.make_async_copy(l_hbm.at[:, pair_columns(pair)], lbuf.at[slot], lsem.at[slot])

    def load_v(pair):
        at = pair_columns(pair)
        return pltpu.make_async_copy(v_hbm.at[:, at], vc.at[:, at], vsem.at[pair])

    def load(pair, slot):
        load_v(pair).start()
        load_l(pair, slot).start()

    def vectors_of(h, ch):
        return vc[h * part : (h + 1) * part, columns(ch)]

    mass = pltpu.make_async_copy(m_hbm, m_ref, small.at[0])
    mass.start()
    for pair in range(SLOTS):
        load(pair, pair)

    barrier = pltpu.get_barrier_semaphore()
    for d in range(1, GROUP):
        pl.semaphore_signal(barrier, inc=1, device_id={"row": base + lax.rem(place + d, GROUP)}, device_id_type=MESH)
    for d in range(1, z_size):
        pl.semaphore_signal(
            barrier, inc=1, device_id={"row": lax.rem(z + d, z_size) * GROUP + place}, device_id_type=MESH
        )
    for d in range(1, n_col):
        pl.semaphore_signal(barrier, inc=1, device_id={"col": lax.rem(col + d, n_col)}, device_id_type=MESH)

    def collect(total):
        n = total.shape[0] // 3
        return (total[0:n] + (total[n : 2 * n] + total[2 * n :])) * scale

    acc[...] = jnp.zeros_like(acc)
    acc2[...] = jnp.zeros_like(acc2)

    mass.wait()

    def first_step(pair, carry):
        slot = lax.rem(pair, SLOTS)
        load_l(pair, slot).wait()
        load_v(pair).wait()
        x = vc[:, pair_columns(pair)] * m_ref[:, pair_columns(pair)]
        a = jnp.concatenate(split3(x), axis=0)
        high, low = split2(lbuf[slot])
        for i in range(2):
            l1[2 * pair + i] = high[:, i * WIDTH : (i + 1) * WIDTH]
            l2[2 * pair + i] = low[:, i * WIDTH : (i + 1) * WIDTH]
        acc[...] += dot_nt(high, a) + dot_nt(low, a)

        @pl.when(pair + SLOTS < chunks // 2)
        def _():
            load(pair + SLOTS, slot)

        return carry

    lax.fori_loop(0, chunks // 2, first_step, 0)
    first = (acc[:, :new] + (acc[:, new : 2 * new] + acc[:, 2 * new :])).T * scale
    parts = sums[0][0].shape[0]
    for h in range(2):
        for i in range(parts):
            at = h * part + i * part // parts
            sums[h][0][i] = first[at : at + part // parts]
    pl.semaphore_wait(barrier, (GROUP - 1) + (z_size - 1) + (n_col - 1))
    sent = []
    firsts = [exchange_steps(sums[h], row, z_size, sent) for h in range(2)]
    for _ in range(4):
        for steps in firsts:
            next(steps)

    def summed(i):
        return jnp.concatenate([sums[i][1][k] for k in range(parts)], axis=0)

    def set_weights(h, b):
        for i, w in enumerate(split3(b)):
            wsp[h, i * part : (i + 1) * part] = w

    def term(h, ch):
        r = dot_nn(wsp[h], l1[ch])
        s = dot_nn(wsp[h, 0 : 2 * part], l2[ch])
        return r[0:part] + ((r[part : 2 * part] + s[0:part]) + (r[2 * part :] + s[part:]))

    def send(src, dst, sems, semr, index, where):
        return remote(src, dst, sems.at[0], semr.at[index], {"col": where})

    def wait_blocks(stage, sems, semr, index, count):
        blocks = stage.at[0:count]
        remote(blocks, blocks, sems.at[0], semr.at[index], {"col": right}).wait_recv()

    def far(c, k, j, where):
        d2, fl, fr, stage, ss, sr = scatters[c]
        return send(stage.at[k], d2.at[k], ss, sr, j, where)

    def to_right(c, k, j):
        d2, fl, fr, stage, ss, sr = scatters[c]
        return send(stage.at[per_slice + k], fl.at[k], ss, sr, half + j, right)

    def to_left(c, k, j):
        d2, fl, fr, stage, ss, sr = scatters[c]
        return send(stage.at[2 * per_slice + k], fr.at[k], ss, sr, half + j, left)

    def loop(count, body):
        def step(j, carry):
            body(j)
            return carry

        lax.fori_loop(0, count, step, 0)

    def scatter_start(c):
        h, stage = c % 2, scatters[c][3]

        def far_step(j):
            stage[j] = term(h, across * per_slice + j)
            far(c, j, j, right).start()
            stage[half + j] = term(h, across * per_slice + half + j)
            far(c, half + j, j, left).start()

        def pure_step(j):
            stage[per_slice + half + j] = term(h, right * per_slice + half + j)
            to_right(c, half + j, j).start()
            stage[2 * per_slice + j] = term(h, left * per_slice + j)
            to_left(c, j, j).start()

        loop(half, far_step)
        loop(half, pure_step)

    def scatter_added(c):
        h, d2, stage = c % 2, scatters[c][0], scatters[c][3]

        def added_step(j):
            to_the_right = term(h, right * per_slice + j)
            to_the_left = term(h, left * per_slice + half + j)
            wait_blocks(stage, *scatters[c][4:], j, 2)
            stage[per_slice + j] = to_the_right + d2[j]
            to_right(c, j, j).start()
            stage[2 * per_slice + half + j] = to_the_left + d2[half + j]
            to_left(c, half + j, j).start()

        loop(half, added_step)

    def scatter_own(c, finish, done):
        h, fl, fr = c % 2, scatters[c][1], scatters[c][2]

        def own_step(j):
            own = [term(h, col * per_slice + k) for k in (j, half + j)]
            wait_blocks(scatters[c][3], *scatters[c][4:], half + j, 4)
            for k, value in zip((j, half + j), own):
                finish(k, value + (fl[k] + fr[k]))
            done(j)

        loop(half, own_step)

    def targets(g):
        return (zf if g < 2 else p_hbm).at[g % 2]

    def give_right(g, src, k, index):
        send(src, targets(g).at[col * per_slice + k], *gathers[g], index, right).start()

    def give_left(g, src, k, index):
        send(src, targets(g).at[col * per_slice + k], *gathers[g], index, left).start()

    def hand_on(g, j, k, sl, where):
        at = targets(g).at[sl * per_slice + k]
        send(at, at, *gathers[g], 2 * half + j, where).start()

    def relay(g, j, use):
        wait_blocks(scatters[g][3], *gathers[g], j, 2)
        hand_on(g, j, j, left, right)
        hand_on(g, j, half + j, right, left)
        use(left * per_slice + j)
        use(right * per_slice + half + j)

    def give_first(g, j, src):
        give_right(g, src.at[j], j, j)
        give_left(g, src.at[half + j], half + j, j)

    def give_last(g, j, src):
        give_left(g, src.at[j], j, half + j)
        give_right(g, src.at[half + j], half + j, half + j)

    def gather_near(g, use):
        def near_step(j):
            wait_blocks(scatters[g][3], *gathers[g], half + j, 2)
            use(left * per_slice + half + j)
            use(right * per_slice + j)

        loop(half, near_step)

    def gather_far(g, use):
        def far_step(j):
            wait_blocks(scatters[g][3], *gathers[g], 2 * half + j, 2)
            for k in (j, half + j):
                use(across * per_slice + k)

        loop(half, far_step)

    def use_once(h):
        def use(ch):
            x = (vectors_of(h, ch) - zf[h, ch]) * m_ref[:, columns(ch)]
            a = jnp.concatenate(split3(x), axis=0)
            acc2[h] += dot_nt(a, l1[ch])
            acc2[h, 0 : 2 * part] += dot_nt(a[0 : 2 * part], l2[ch])

        return use

    def own_first(h):
        mine = zf.at[h, pl.ds(col * per_slice, per_slice)]

        def finish(k, value):
            zf[h, col * per_slice + k] = value

        scatter_own(h, finish, lambda j: give_first(h, j, mine))
        loop(half, lambda j: give_last(h, j, mine))
        loop(per_slice, lambda k: use_once(h)(col * per_slice + k))

    def second_sum(h, hooks):
        second = collect(acc2[h])
        for i in range(parts):
            sums[2 + h][0][i] = second[i * part // parts : (i + 1) * part // parts]
        for i, _ in enumerate(exchange_steps(sums[2 + h], row, z_size, sent)):
            if hooks[i] is not None:
                hooks[i]()
        set_weights(h, summed(h) + summed(2 + h))

    next(firsts[0], None)
    set_weights(0, summed(0))
    scatter_start(0)
    next(firsts[1], None)
    set_weights(1, summed(1))
    scatter_added(0)
    scatter_start(1)
    own_first(0)
    scatter_added(1)
    loop(half, lambda j: relay(0, j, use_once(0)))
    own_first(1)
    gather_near(0, use_once(0))
    gather_far(0, use_once(0))
    relays = [lambda j=j: relay(1, j, use_once(1)) for j in range(half)]
    second_sum(0, [relays[0], None, relays[1], lambda: gather_near(1, use_once(1))])
    scatter_start(2)
    gather_far(1, use_once(1))
    second_sum(1, [None, None, lambda: scatter_added(2), None])
    scatter_start(3)

    ggram[...] = jnp.zeros_like(ggram)

    def add_gram(p, ch):
        a = jnp.concatenate(split3(p * m_ref[:, columns(ch)]), axis=0)
        b = jnp.concatenate(split3(p), axis=0)
        ggram[...] += dot_nt(a, b)

    def collect_gram():
        g = ggram[...]
        rows3 = g[0:new] + (g[new : 2 * new] + g[2 * new :])
        gram = rows3[:, 0:new] + (rows3[:, new : 2 * new] + rows3[:, 2 * new :])
        return gram * scale

    def keep(h):
        return pltpu.make_async_copy(po.at[h], p_hbm.at[h, pl.ds(col * per_slice, per_slice)], psem.at[h])

    def both(k):
        return jnp.concatenate([po[0, k], po[1, k]], axis=0)

    def finish_second(h):
        def finish(k, value):
            ch = col * per_slice + k
            po[h, k] = vectors_of(h, ch) - value
            if h == 1:
                add_gram(both(k), ch)

        return finish

    nothing = lambda ch: None
    scatter_own(2, finish_second(0), nothing)
    keep(0).start()
    scatter_added(3)

    def give_all(h):
        loop(half, lambda j: give_first(2 + h, j, po.at[h]))
        loop(half, lambda j: give_last(2 + h, j, po.at[h]))

    def hand_all(h):
        loop(half, lambda j: relay(2 + h, j, nothing))

    give_all(0)
    scatter_own(3, finish_second(1), nothing)
    keep(1).start()
    gram = gram_sum(collect_gram(), grams[0], row, col, n_col, z_size, sent, None, lambda: give_all(1))
    upper_one, inverse_one = factorize(gram)

    ggram[...] = jnp.zeros_like(ggram)
    weights = terms_of(inverse_one)
    loop(per_slice, lambda k: add_gram(apply_terms(weights, both(k)), col * per_slice + k))
    gram = gram_sum(collect_gram(), grams[1], row, col, n_col, z_size, sent, lambda: hand_all(0), lambda: hand_all(1))
    upper_two, inverse_two = factorize(gram)
    f_ref[...] = jnp.dot(upper_two, upper_one, precision=HIGHEST, preferred_element_type=F32)
    t_ref[...] = terms_of(jnp.dot(inverse_two, inverse_one, precision=HIGHEST, preferred_element_type=F32))

    results = [
        pltpu.make_async_copy(t_ref, t_hbm, small.at[1]),
        pltpu.make_async_copy(f_ref, f_hbm, small.at[2]),
    ]
    for copy in results:
        copy.start()
    for copy in sent:
        copy.wait_send()

    def all_sent(c, sems, semr):
        stage = scatters[c][3]
        remote(stage, stage, sems.at[0], semr.at[0], {"col": right}).wait_send()

    for copy in results:
        copy.wait()
    for h in range(2):
        keep(h).wait()
    for c in range(4):
        all_sent(c, scatters[c][4], scatters[c][5])
    for g in range(2):
        all_sent(g, *gathers[g])
    for h in range(2):
        gather_near(2 + h, nothing)
        gather_far(2 + h, nothing)
    for g in range(2, 4):
        all_sent(g, *gathers[g])


def apply_kernel(t_ref, p_ref, f_ref, o_ref, fo_ref):
    fo_ref[...] = f_ref[...]
    weights = t_ref[...]
    for i in range(p_ref.shape[1]):
        p = jnp.concatenate([p_ref[0, i], p_ref[1, i]], axis=0)
        o_ref[:, i * WIDTH : (i + 1) * WIDTH] = apply_terms(weights, p)


def local(n_col, n_row, locked, vectors, mass):
    mine, cols = locked.shape
    new = vectors.shape[0]
    part = new // 2
    chunks = cols // WIDTH
    per_slice = chunks // n_col
    z_size = n_row // GROUP
    dma = pltpu.SemaphoreType.DMA

    def exchange_scratch(rows):
        many = lambda n: pltpu.VMEM((n, rows, mine), F32)
        one = pltpu.VMEM((rows, mine), F32)
        x_size = GROUP // 2
        return [many(x_size), many(x_size), many(x_size - 1), one, many(2), one, many(z_size), dma((8,))]

    def gram_scratch():
        packed = (new // 2, 2 * new)
        sizes = (2, GROUP // 2, z_size, n_col)
        return [ref for n in sizes for ref in (pltpu.VMEM(packed, F32), pltpu.VMEM((n,) + packed, F32))] + [dma((8,))]

    chunk = lambda *n: pltpu.VMEM(n + (part, WIDTH), F32)
    scratch = [
        pltpu.VMEM((1, cols), F32), pltpu.VMEM((2 * new, 4 * new), BF16), pltpu.VMEM((new, new), F32), dma((3,)),
        pltpu.VMEM((SLOTS, mine, 2 * WIDTH), F32), dma((SLOTS,)), pltpu.VMEM((new, cols), F32), dma((chunks // 2,)),
        pltpu.VMEM((chunks, mine, WIDTH), BF16), pltpu.VMEM((chunks, mine, WIDTH), BF16),
        pltpu.VMEM((mine, 3 * new), F32), pltpu.VMEM((2, 3 * part, mine), F32),
        pltpu.VMEM((2, 3 * part, mine), BF16), pltpu.VMEM((3 * new, 3 * new), F32),
        chunk(2, chunks), chunk(2, per_slice), dma((2,)),
    ]
    scratch += exchange_scratch(2 * part // GROUP) * 4
    scratch += gram_scratch() * 2
    ring = lambda n: [dma((1,)), dma((n * per_slice // 2,))]
    scratch += ([chunk(per_slice)] * 3 + [chunk(3 * per_slice)] + ring(2)) * 4 + ring(3) * 4
    hbm = pl.BlockSpec(memory_space=pl.ANY)
    projected, transform, factor = pl.pallas_call(
        functools.partial(fused, n_col, n_row, 1.0 / (cols * n_row)),
        out_shape=(
            jax.ShapeDtypeStruct((2, chunks, part, WIDTH), F32),
            jax.ShapeDtypeStruct((2 * new, 4 * new), BF16),
            jax.ShapeDtypeStruct((new, new), F32),
        ),
        in_specs=[hbm] * 3,
        out_specs=(hbm,) * 3,
        scratch_shapes=scratch,
        compiler_params=pltpu.CompilerParams(
            collective_id=0, has_side_effects=True, vmem_limit_bytes=60 << 20
        ),
        name="project_and_factor",
    )(locked, vectors, mass.reshape(1, cols))
    block = 8
    still = lambda n: pl.BlockSpec((n, n), lambda i: (0, 0))
    return tuple(
        pl.pallas_call(
            apply_kernel,
            grid=(chunks // block,),
            out_shape=(jax.ShapeDtypeStruct((new, cols), F32), jax.ShapeDtypeStruct((new, new), F32)),
            in_specs=[
                pl.BlockSpec((2 * new, 4 * new), lambda i: (0, 0)),
                pl.BlockSpec((2, block, part, WIDTH), lambda i: (0, i, 0, 0)),
                still(new),
            ],
            out_specs=(pl.BlockSpec((new, block * WIDTH), lambda i: (0, i)), still(new)),
            name="apply_factors",
        )(transform, projected, factor)
    )


def solution(mesh):
    return jax.shard_map(
        functools.partial(local, mesh.shape["col"], mesh.shape["row"]),
        mesh=mesh,
        in_specs=(P("col", "row"), P(None, "row"), P("row")),
        out_specs=(P(None, "row"), P()),
        check_vma=False,
    )
```

```python
import functools

import jax
import jax.numpy as jnp
from jax import lax
from jax.experimental import pallas as pl
from jax.experimental.pallas import tpu as pltpu
from jax.sharding import PartitionSpec as P

MESH = pl.DeviceIdType.MESH
F32 = jnp.float32
BF16 = jnp.bfloat16
HIGHEST = lax.Precision.HIGHEST
WIDTH = 1024
GROUP = 8
SLOTS = 6


def split2(x):
    high = x.astype(BF16)
    return high, (x - high.astype(F32)).astype(BF16)


def split3(x):
    high = x.astype(BF16)
    rest = x - high.astype(F32)
    middle = rest.astype(BF16)
    low = (rest - middle.astype(F32)).astype(BF16)
    return high, middle, low


def dot_nt(a, b):
    return lax.dot_general(a, b, (((1,), (1,)), ((), ())), preferred_element_type=F32)


def dot_nn(a, b):
    return lax.dot_general(a, b, (((1,), (0,)), ((), ())), preferred_element_type=F32)


def remote(src, dst, send_sem, recv_sem, device):
    return pltpu.make_async_remote_copy(
        src_ref=src, dst_ref=dst, send_sem=send_sem, recv_sem=recv_sem, device_id=device, device_id_type=MESH
    )


def exchange_steps(scratch, row, z_size, sent):
    (src, out, part, cred, cbuf, zred, zbuf, sems) = scratch
    place = lax.rem(row, GROUP)
    base = row - place
    z = lax.div(row, GROUP)
    x, core = lax.div(place, 2), lax.rem(place, 2)
    x_size = GROUP // 2
    here = {"row": row}
    others = [lax.rem(x + d, x_size) for d in range(1, x_size)]
    device = lambda p: {"row": base + 2 * p + core}

    for d, peer in enumerate(others):
        remote(src.at[peer], part.at[d], sems.at[0], sems.at[1], device(peer)).start()
    yield
    arrived = remote(part, part, sems.at[0], sems.at[1], here)
    arrived.wait_recv()
    total = src[x]
    for d in range(x_size - 1):
        total = total + part[d]
    cred[...] = total
    peer_start(cred, cbuf, sems.at[2], sems.at[3], core, [{"row": base + 2 * x + 1 - core}])
    yield
    zred[...] = peer_finish(cbuf, sems.at[2], sems.at[3], here, sent)
    peers = [{"row": lax.rem(z + d, z_size) * GROUP + place} for d in range(1, z_size)]
    peer_start(zred, zbuf, sems.at[4], sems.at[5], z, peers)
    yield
    out[x] = peer_finish(zbuf, sems.at[4], sems.at[5], here, sent)
    for peer in others:
        remote(out.at[x], out.at[x], sems.at[6], sems.at[7], device(peer)).start()
    yield
    rest = out.at[0 : x_size - 1]
    gathered = remote(rest, rest, sems.at[6], sems.at[7], here)
    gathered.wait_recv()
    sent += [arrived, gathered]


def peer_start(src, buf, send_sem, recv_sem, mine, devices):
    for device in devices:
        remote(src, buf.at[mine], send_sem, recv_sem, device).start()
    buf[mine] = src[...]


def peer_finish(buf, send_sem, recv_sem, here, sent):
    size = buf.shape[0]
    rest = buf.at[0 : size - 1]
    arrived = remote(rest, rest, send_sem, recv_sem, here)
    arrived.wait_recv()
    sent.append(arrived)
    total = buf[0]
    for i in range(1, size):
        total = total + buf[i]
    return total


def gram_sum(gram, scratch, row, col, n_col, z_size, sent, first, last):
    half = gram.shape[0] // 2
    place = lax.rem(row, GROUP)
    base = row - place
    z = lax.div(row, GROUP)
    x, core = lax.div(place, 2), lax.rem(place, 2)
    x_size = GROUP // 2
    stages = [
        (2, core, lambda p: {"row": base + 2 * x + p}, first),
        (x_size, x, lambda p: {"row": base + 2 * p + core}, None),
        (z_size, z, lambda p: {"row": p * GROUP + place}, None),
        (n_col, col, lambda p: {"col": p}, last),
    ]
    total = jnp.concatenate([gram[:half], gram[half:]], axis=1)
    sems = scratch[-1]
    for i, (size, mine, device, between) in enumerate(stages):
        src, buf = scratch[2 * i : 2 * i + 2]
        src[...] = total
        peer_start(src, buf, sems.at[2 * i], sems.at[2 * i + 1], mine, [device(lax.rem(mine + d, size)) for d in range(1, size)])
        if between is not None:
            between()
        total = peer_finish(buf, sems.at[2 * i], sems.at[2 * i + 1], {"row": row}, sent)
    new = gram.shape[0]
    return jnp.concatenate([total[:, :new], total[:, new:]], axis=0)


def factorize(gram):
    size = gram.shape[0]
    lane = lax.broadcasted_iota(jnp.int32, (size, 2 * size), 1)
    sub = lax.broadcasted_iota(jnp.int32, (size, 2 * size), 0)
    sub8 = lax.broadcasted_iota(jnp.int32, (8, 2 * size), 0)
    wide = jnp.concatenate([gram, jnp.zeros_like(gram)], axis=1)
    wide = jnp.where(lane < size, wide, jnp.where(lane - size == sub, 1.0, 0.0))
    blocks = [wide[8 * i : 8 * i + 8] for i in range(size // 8)]
    full = lambda x: jnp.broadcast_to(x, (8, 2 * size))
    for b in range(size // 8):
        j = 8 * b
        lines = [full(blocks[b][a : a + 1, :]) for a in range(8)]
        square = [[full(line[:, j + c : j + c + 1]) for c in range(8)] for line in lines]
        inverse = []
        for p in range(8):
            inverse.append(1.0 / square[p][p])
            for a in range(p + 1, 8):
                times = square[a][p] * inverse[p]
                lines[a] = lines[a] - times * lines[p]
                for c in range(p + 1, 8):
                    square[a][c] = square[a][c] - times * square[p][c]
        for i in range(b + 1, size // 8):
            column = [full(blocks[i][:, j + c : j + c + 1]) for c in range(8)]
            for p in range(8):
                times = column[p] * inverse[p]
                for q in range(p + 1, 8):
                    column[q] = column[q] - times * square[p][q]
                blocks[i] = blocks[i] - times * lines[p]
        for a in range(8):
            blocks[b] = jnp.where(sub8 == a, lines[a], blocks[b])
    body = jnp.concatenate(blocks, axis=0)
    pivots = jnp.sum(jnp.where(lane == sub, body, 0.0), axis=1, keepdims=True)
    body = body / jnp.sqrt(pivots)
    upper = jnp.where(lane >= sub, body, 0.0)[:, :size]
    return upper, body[:, size:]


def terms_of(matrix):
    a, b, c = split3(matrix)
    zero = jnp.zeros_like(a)
    return jnp.concatenate(
        [jnp.concatenate([a, a, a, b], axis=1), jnp.concatenate([c, b, zero, zero], axis=1)], axis=0
    )


def apply_terms(terms, x):
    new = x.shape[0]
    a, b, c = split3(x)
    r = dot_nn(terms, jnp.concatenate([a, b, c, a], axis=0))
    return r[:new] + r[new:]


def fused(
    n_col, n_row, scale,
    l_hbm, v_hbm, m_hbm, p_hbm, t_hbm, f_hbm,
    m_ref, t_ref, f_ref, small,
    lbuf, lsem, vc, vsem, l1, l2, acc, acc2, wsp, ggram, zf, po, psem,
    *rest,
):
    sums = [rest[8 * i : 8 * i + 8] for i in range(4)]
    grams = [rest[32 + 9 * i : 41 + 9 * i] for i in range(2)]
    scatters = [rest[50 + 6 * i : 56 + 6 * i] for i in range(4)]
    gathers = [rest[74 + 2 * i : 76 + 2 * i] for i in range(4)]
    col, row = lax.axis_index("col"), lax.axis_index("row")
    right, left = lax.rem(col + 1, n_col), lax.rem(col + n_col - 1, n_col)
    across = lax.rem(col + 2, n_col)
    z_size = n_row // GROUP
    place = lax.rem(row, GROUP)
    base = row - place
    z = lax.div(row, GROUP)
    chunks, part = vc.shape[1] // WIDTH, vc.shape[0] // 2
    per_slice = chunks // n_col
    half = per_slice // 2
    new = 2 * part

    def columns(ch):
        return pl.ds(pl.multiple_of(ch * WIDTH, WIDTH), WIDTH)

    def pair_columns(pair):
        return pl.ds(pl.multiple_of(pair * 2 * WIDTH, 2 * WIDTH), 2 * WIDTH)

    def load_l(pair, slot):
        return pltpu.make_async_copy(l_hbm.at[:, pair_columns(pair)], lbuf.at[slot], lsem.at[slot])

    def load_v(pair):
        at = pair_columns(pair)
        return pltpu.make_async_copy(v_hbm.at[:, at], vc.at[:, at], vsem.at[pair])

    def load(pair, slot):
        load_v(pair).start()
        load_l(pair, slot).start()

    def vectors_of(h, ch):
        return vc[h * part : (h + 1) * part, columns(ch)]

    mass = pltpu.make_async_copy(m_hbm, m_ref, small.at[0])
    mass.start()
    for pair in range(SLOTS):
        load(pair, pair)

    barrier = pltpu.get_barrier_semaphore()
    for d in range(1, GROUP):
        pl.semaphore_signal(barrier, inc=1, device_id={"row": base + lax.rem(place + d, GROUP)}, device_id_type=MESH)
    for d in range(1, z_size):
        pl.semaphore_signal(
            barrier, inc=1, device_id={"row": lax.rem(z + d, z_size) * GROUP + place}, device_id_type=MESH
        )
    for d in range(1, n_col):
        pl.semaphore_signal(barrier, inc=1, device_id={"col": lax.rem(col + d, n_col)}, device_id_type=MESH)

    def collect(total):
        n = total.shape[0] // 3
        return (total[0:n] + (total[n : 2 * n] + total[2 * n :])) * scale

    acc[...] = jnp.zeros_like(acc)
    acc2[...] = jnp.zeros_like(acc2)

    mass.wait()

    def first_step(pair, carry):
        slot = lax.rem(pair, SLOTS)
        load_l(pair, slot).wait()
        load_v(pair).wait()
        x = vc[:, pair_columns(pair)] * m_ref[:, pair_columns(pair)]
        a = jnp.concatenate(split3(x), axis=0)
        high, low = split2(lbuf[slot])
        for i in range(2):
            l1[2 * pair + i] = high[:, i * WIDTH : (i + 1) * WIDTH]
            l2[2 * pair + i] = low[:, i * WIDTH : (i + 1) * WIDTH]
        acc[...] += dot_nt(high, a) + dot_nt(low, a)

        @pl.when(pair + SLOTS < chunks // 2)
        def _():
            load(pair + SLOTS, slot)

        return carry

    lax.fori_loop(0, chunks // 2, first_step, 0)
    first = (acc[:, :new] + (acc[:, new : 2 * new] + acc[:, 2 * new :])).T * scale
    parts = sums[0][0].shape[0]
    for h in range(2):
        for i in range(parts):
            at = h * part + i * part // parts
            sums[h][0][i] = first[at : at + part // parts]
    pl.semaphore_wait(barrier, (GROUP - 1) + (z_size - 1) + (n_col - 1))
    sent = []
    firsts = [exchange_steps(sums[h], row, z_size, sent) for h in range(2)]
    for _ in range(4):
        for steps in firsts:
            next(steps)

    def summed(i):
        return jnp.concatenate([sums[i][1][k] for k in range(parts)], axis=0)

    def set_weights(h, b):
        for i, w in enumerate(split3(b)):
            wsp[h, i * part : (i + 1) * part] = w

    def term(h, ch):
        r = dot_nn(wsp[h], l1[ch])
        s = dot_nn(wsp[h, 0 : 2 * part], l2[ch])
        return r[0:part] + ((r[part : 2 * part] + s[0:part]) + (r[2 * part :] + s[part:]))

    def send(src, dst, sems, semr, index, where):
        return remote(src, dst, sems.at[0], semr.at[index], {"col": where})

    def wait_blocks(stage, sems, semr, index, count):
        blocks = stage.at[0:count]
        remote(blocks, blocks, sems.at[0], semr.at[index], {"col": right}).wait_recv()

    def far(c, k, j, where):
        d2, fl, fr, stage, ss, sr = scatters[c]
        return send(stage.at[k], d2.at[k], ss, sr, j, where)

    def to_right(c, k, j):
        d2, fl, fr, stage, ss, sr = scatters[c]
        return send(stage.at[per_slice + k], fl.at[k], ss, sr, half + j, right)

    def to_left(c, k, j):
        d2, fl, fr, stage, ss, sr = scatters[c]
        return send(stage.at[2 * per_slice + k], fr.at[k], ss, sr, half + j, left)

    def loop(count, body):
        def step(j, carry):
            body(j)
            return carry

        lax.fori_loop(0, count, step, 0)

    def scatter_start(c):
        h, stage = c % 2, scatters[c][3]

        def far_step(j):
            stage[j] = term(h, across * per_slice + j)
            far(c, j, j, right).start()
            stage[half + j] = term(h, across * per_slice + half + j)
            far(c, half + j, j, left).start()

        def pure_step(j):
            stage[per_slice + half + j] = term(h, right * per_slice + half + j)
            to_right(c, half + j, j).start()
            stage[2 * per_slice + j] = term(h, left * per_slice + j)
            to_left(c, j, j).start()

        loop(half, far_step)
        loop(half, pure_step)

    def scatter_added(c):
        h, d2, stage = c % 2, scatters[c][0], scatters[c][3]

        def added_step(j):
            to_the_right = term(h, right * per_slice + j)
            to_the_left = term(h, left * per_slice + half + j)
            wait_blocks(stage, *scatters[c][4:], j, 2)
            stage[per_slice + j] = to_the_right + d2[j]
            to_right(c, j, j).start()
            stage[2 * per_slice + half + j] = to_the_left + d2[half + j]
            to_left(c, half + j, j).start()

        loop(half, added_step)

    def scatter_own(c, finish, done):
        h, fl, fr = c % 2, scatters[c][1], scatters[c][2]

        def own_step(j):
            own = [term(h, col * per_slice + k) for k in (j, half + j)]
            wait_blocks(scatters[c][3], *scatters[c][4:], half + j, 4)
            for k, value in zip((j, half + j), own):
                finish(k, value + (fl[k] + fr[k]))
            done(j)

        loop(half, own_step)

    def targets(g):
        return (zf if g < 2 else p_hbm).at[g % 2]

    def give_right(g, src, k, index):
        send(src, targets(g).at[col * per_slice + k], *gathers[g], index, right).start()

    def give_left(g, src, k, index):
        send(src, targets(g).at[col * per_slice + k], *gathers[g], index, left).start()

    def hand_on(g, j, k, sl, where):
        at = targets(g).at[sl * per_slice + k]
        send(at, at, *gathers[g], 2 * half + j, where).start()

    def relay(g, j, use):
        wait_blocks(scatters[g][3], *gathers[g], j, 2)
        hand_on(g, j, j, left, right)
        hand_on(g, j, half + j, right, left)
        use(left * per_slice + j)
        use(right * per_slice + half + j)

    def give_first(g, j, src):
        give_right(g, src.at[j], j, j)
        give_left(g, src.at[half + j], half + j, j)

    def give_last(g, j, src):
        give_left(g, src.at[j], j, half + j)
        give_right(g, src.at[half + j], half + j, half + j)

    def gather_near(g, use):
        def near_step(j):
            wait_blocks(scatters[g][3], *gathers[g], half + j, 2)
            use(left * per_slice + half + j)
            use(right * per_slice + j)

        loop(half, near_step)

    def gather_far(g, use):
        def far_step(j):
            wait_blocks(scatters[g][3], *gathers[g], 2 * half + j, 2)
            for k in (j, half + j):
                use(across * per_slice + k)

        loop(half, far_step)

    def use_once(h):
        def use(ch):
            x = (vectors_of(h, ch) - zf[h, ch]) * m_ref[:, columns(ch)]
            a = jnp.concatenate(split3(x), axis=0)
            acc2[h] += dot_nt(a, l1[ch])
            acc2[h, 0 : 2 * part] += dot_nt(a[0 : 2 * part], l2[ch])

        return use

    def own_first(h):
        mine = zf.at[h, pl.ds(col * per_slice, per_slice)]

        def finish(k, value):
            zf[h, col * per_slice + k] = value

        scatter_own(h, finish, lambda j: give_first(h, j, mine))
        loop(half, lambda j: give_last(h, j, mine))
        loop(per_slice, lambda k: use_once(h)(col * per_slice + k))

    def second_sum(h, hooks):
        second = collect(acc2[h])
        for i in range(parts):
            sums[2 + h][0][i] = second[i * part // parts : (i + 1) * part // parts]
        for i, _ in enumerate(exchange_steps(sums[2 + h], row, z_size, sent)):
            if hooks[i] is not None:
                hooks[i]()
        set_weights(h, summed(h) + summed(2 + h))

    next(firsts[0], None)
    set_weights(0, summed(0))
    scatter_start(0)
    next(firsts[1], None)
    set_weights(1, summed(1))
    scatter_added(0)
    scatter_start(1)
    own_first(0)
    scatter_added(1)
    loop(half, lambda j: relay(0, j, use_once(0)))
    own_first(1)
    gather_near(0, use_once(0))
    gather_far(0, use_once(0))
    relays = [lambda j=j: relay(1, j, use_once(1)) for j in range(half)]
    second_sum(0, [relays[0], None, relays[1], lambda: gather_near(1, use_once(1))])
    scatter_start(2)
    gather_far(1, use_once(1))
    second_sum(1, [None, None, lambda: scatter_added(2), None])
    scatter_start(3)

    ggram[...] = jnp.zeros_like(ggram)

    def add_gram(p, ch):
        a = jnp.concatenate(split3(p * m_ref[:, columns(ch)]), axis=0)
        b = jnp.concatenate(split3(p), axis=0)
        ggram[...] += dot_nt(a, b)

    def collect_gram():
        g = ggram[...]
        rows3 = g[0:new] + (g[new : 2 * new] + g[2 * new :])
        gram = rows3[:, 0:new] + (rows3[:, new : 2 * new] + rows3[:, 2 * new :])
        return gram * scale

    def keep(h):
        return pltpu.make_async_copy(po.at[h], p_hbm.at[h, pl.ds(col * per_slice, per_slice)], psem.at[h])

    def both(k):
        return jnp.concatenate([po[0, k], po[1, k]], axis=0)

    def finish_second(h):
        def finish(k, value):
            ch = col * per_slice + k
            po[h, k] = vectors_of(h, ch) - value
            if h == 1:
                add_gram(both(k), ch)

        return finish

    nothing = lambda ch: None
    scatter_own(2, finish_second(0), nothing)
    keep(0).start()
    scatter_added(3)

    def give_all(h):
        loop(half, lambda j: give_first(2 + h, j, po.at[h]))
        loop(half, lambda j: give_last(2 + h, j, po.at[h]))

    def hand_all(h):
        loop(half, lambda j: relay(2 + h, j, nothing))

    give_all(0)
    scatter_own(3, finish_second(1), nothing)
    keep(1).start()
    gram = gram_sum(collect_gram(), grams[0], row, col, n_col, z_size, sent, None, lambda: give_all(1))
    upper_one, inverse_one = factorize(gram)

    ggram[...] = jnp.zeros_like(ggram)
    weights = terms_of(inverse_one)
    loop(per_slice, lambda k: add_gram(apply_terms(weights, both(k)), col * per_slice + k))
    gram = gram_sum(collect_gram(), grams[1], row, col, n_col, z_size, sent, lambda: hand_all(0), lambda: hand_all(1))
    upper_two, inverse_two = factorize(gram)
    f_ref[...] = jnp.dot(upper_two, upper_one, precision=HIGHEST, preferred_element_type=F32)
    t_ref[...] = terms_of(jnp.dot(inverse_two, inverse_one, precision=HIGHEST, preferred_element_type=F32))

    results = [
        pltpu.make_async_copy(t_ref, t_hbm, small.at[1]),
        pltpu.make_async_copy(f_ref, f_hbm, small.at[2]),
    ]
    for copy in results:
        copy.start()
    for copy in sent:
        copy.wait_send()

    def all_sent(c, sems, semr):
        stage = scatters[c][3]
        remote(stage, stage, sems.at[0], semr.at[0], {"col": right}).wait_send()

    for copy in results:
        copy.wait()
    for h in range(2):
        keep(h).wait()
    for c in range(4):
        all_sent(c, scatters[c][4], scatters[c][5])
    for g in range(2):
        all_sent(g, *gathers[g])
    for h in range(2):
        gather_near(2 + h, nothing)
        gather_far(2 + h, nothing)
    for g in range(2, 4):
        all_sent(g, *gathers[g])


def apply_kernel(t_ref, p_ref, f_ref, o_ref, fo_ref):
    fo_ref[...] = f_ref[...]
    weights = t_ref[...]
    for i in range(p_ref.shape[1]):
        p = jnp.concatenate([p_ref[0, i], p_ref[1, i]], axis=0)
        o_ref[:, i * WIDTH : (i + 1) * WIDTH] = apply_terms(weights, p)


def local(n_col, n_row, locked, vectors, mass):
    mine, cols = locked.shape
    new = vectors.shape[0]
    part = new // 2
    chunks = cols // WIDTH
    per_slice = chunks // n_col
    z_size = n_row // GROUP
    dma = pltpu.SemaphoreType.DMA

    def exchange_scratch(rows):
        many = lambda n: pltpu.VMEM((n, rows, mine), F32)
        one = pltpu.VMEM((rows, mine), F32)
        x_size = GROUP // 2
        return [many(x_size), many(x_size), many(x_size - 1), one, many(2), one, many(z_size), dma((8,))]

    def gram_scratch():
        packed = (new // 2, 2 * new)
        sizes = (2, GROUP // 2, z_size, n_col)
        return [ref for n in sizes for ref in (pltpu.VMEM(packed, F32), pltpu.VMEM((n,) + packed, F32))] + [dma((8,))]

    chunk = lambda *n: pltpu.VMEM(n + (part, WIDTH), F32)
    scratch = [
        pltpu.VMEM((1, cols), F32), pltpu.VMEM((2 * new, 4 * new), BF16), pltpu.VMEM((new, new), F32), dma((3,)),
        pltpu.VMEM((SLOTS, mine, 2 * WIDTH), F32), dma((SLOTS,)), pltpu.VMEM((new, cols), F32), dma((chunks // 2,)),
        pltpu.VMEM((chunks, mine, WIDTH), BF16), pltpu.VMEM((chunks, mine, WIDTH), BF16),
        pltpu.VMEM((mine, 3 * new), F32), pltpu.VMEM((2, 3 * part, mine), F32),
        pltpu.VMEM((2, 3 * part, mine), BF16), pltpu.VMEM((3 * new, 3 * new), F32),
        chunk(2, chunks), chunk(2, per_slice), dma((2,)),
    ]
    scratch += exchange_scratch(2 * part // GROUP) * 4
    scratch += gram_scratch() * 2
    ring = lambda n: [dma((1,)), dma((n * per_slice // 2,))]
    scratch += ([chunk(per_slice)] * 3 + [chunk(3 * per_slice)] + ring(2)) * 4 + ring(3) * 4
    hbm = pl.BlockSpec(memory_space=pl.ANY)
    projected, transform, factor = pl.pallas_call(
        functools.partial(fused, n_col, n_row, 1.0 / (cols * n_row)),
        out_shape=(
            jax.ShapeDtypeStruct((2, chunks, part, WIDTH), F32),
            jax.ShapeDtypeStruct((2 * new, 4 * new), BF16),
            jax.ShapeDtypeStruct((new, new), F32),
        ),
        in_specs=[hbm] * 3,
        out_specs=(hbm,) * 3,
        scratch_shapes=scratch,
        compiler_params=pltpu.CompilerParams(
            collective_id=0, has_side_effects=True, vmem_limit_bytes=60 << 20
        ),
        name="project_and_factor",
    )(locked, vectors, mass.reshape(1, cols))
    block = 8
    still = lambda n: pl.BlockSpec((n, n), lambda i: (0, 0))
    return tuple(
        pl.pallas_call(
            apply_kernel,
            grid=(chunks // block,),
            out_shape=(jax.ShapeDtypeStruct((new, cols), F32), jax.ShapeDtypeStruct((new, new), F32)),
            in_specs=[
                pl.BlockSpec((2 * new, 4 * new), lambda i: (0, 0)),
                pl.BlockSpec((2, block, part, WIDTH), lambda i: (0, i, 0, 0)),
                still(new),
            ],
            out_specs=(pl.BlockSpec((new, block * WIDTH), lambda i: (0, i)), still(new)),
            name="apply_factors",
        )(transform, projected, factor)
    )


def solution(mesh):
    return jax.shard_map(
        functools.partial(local, mesh.shape["col"], mesh.shape["row"]),
        mesh=mesh,
        in_specs=(P("col", "row"), P(None, "row"), P("row")),
        out_specs=(P(None, "row"), P()),
        check_vma=False,
    )
```
